256 devices in a mesh: depth: 8 (over x_lo, y), row: 32 (over x_hi, z, core).
Axes of the slice: x: 4 (x_hi: 2, x_lo: 2; x = x_hi * 2 + x_lo), y: 4, z: 8, core: 2. Of those that a mesh axis runs over, the one named last changes fastest.
Arguments:
- field: float32 [2, 8, 4096, 4096], P(None, 'depth', 'row'), may hold values from -6 to 6
- hologram: float32 [4096, 4096], P('row'), may hold values from -16 to 16
- defocus: float32 [8], P('depth'), may hold values from 512 to 2048
Outputs:
- estimate: float32 [2, 8, 4096, 4096], P(None, 'depth', 'row')
The draws below stay inside these ranges and needn't reach their ends.
All inputs are finite; a program needn't handle non-finite values.
Results may differ from the reference program's by a relative error of at most 0.00045.
Values sent between devices are 32-bit elements; how exact they have to be, the bound alone decides.
A program may use at most 320 MiB of HBM per device.

```python
import math
import jax
import jax.numpy as jnp
from jax import lax

N = 4096
ITERS = 1
PLANES = 8


def block_levels(key, dims, split, least, high):
    def one(position, parts):
        draws = jax.random.uniform(jax.random.fold_in(jax.random.fold_in(key, 6), position), (parts,), jnp.float32, least / len(split), high / len(split))
        return jnp.repeat(jnp.exp(draws), dims[position] // parts).reshape((-1,) + (1,) * (len(dims) - position - 1))

    factor_of = one(*split[0])
    for cut in split[1:]:
        factor_of = factor_of * one(*cut)
    return factor_of


def normal_values(rng, dims, deviation, bound, shards=(), kind=jnp.bfloat16):
    drawn = deviation * jax.random.normal(rng, dims, jnp.float32)
    if shards:
        drawn = drawn * block_levels(rng, dims, shards, -0.22, 0.18)
    return jnp.clip(drawn, -bound, bound).astype(kind)


def setup_inputs(seed: int = 0) -> dict:
    seeds = jax.random.split(jax.random.key(seed), 4)
    return {
        "field": normal_values(seeds[0], (2, PLANES, N, N), 1.0, 6.0, ((1, 8), (2, 32)), jnp.float32),
        "hologram": normal_values(seeds[1], (N, N), (PLANES ** 0.5), 16.0, ((0, 32),), jnp.float32),
        "defocus": jnp.clip(jnp.exp(math.log(2048.0) - 1.3862944 * jax.random.uniform(seeds[2], (PLANES,), jnp.float32) ** block_levels(seeds[2], (PLANES,), ((0, 8),), -0.2, 0.2)), 512.0, 2048.0),
    }


tv_step_size = 1.0 / 12.0
tv_sharpness = 0.25

def signed_squares(length_total):
    indices = jnp.arange(length_total, dtype=jnp.int32)
    centred = jnp.where(indices < length_total // 2, indices, indices - length_total)
    return (centred * centred).astype(jnp.float32)

def defocus_phase(depth_value, length_total):
    squares = signed_squares(length_total)
    grid_sum = (squares[:, None] + squares[None, :]) * (math.pi / (length_total * length_total))
    return depth_value * grid_sum

def forward_diff(values, axis_pos):
    extent = values.shape[axis_pos]
    shifted = jnp.concatenate([lax.slice_in_dim(values, 1, extent, axis=axis_pos), lax.slice_in_dim(values, extent - 1, extent, axis=axis_pos)], axis=axis_pos)
    return shifted - values

def backward_diff(values, axis_pos):
    extent = values.shape[axis_pos]
    shifted = jnp.concatenate([jnp.zeros_like(lax.slice_in_dim(values, 0, 1, axis=axis_pos)), lax.slice_in_dim(values, 0, extent - 1, axis=axis_pos)], axis=axis_pos)
    return values - shifted

def plane_flux(here_plane, ahead_plane):
    depth_diff = ahead_plane - here_plane
    row_diff = forward_diff(here_plane, 1)
    col_diff = forward_diff(here_plane, 2)
    magnitude = jnp.sqrt(lax.optimization_barrier(jnp.sum(depth_diff * depth_diff + row_diff * row_diff + col_diff * col_diff, axis=0)))
    factor = 1.0 / (1.0 + tv_sharpness * magnitude)
    return (depth_diff * factor, row_diff * factor, col_diff * factor)

def tv_shrink(moved_field):
    plane_total = moved_field.shape[1]

    def one_plane(index_z):
        here_plane = lax.dynamic_index_in_dim(moved_field, index_z, 1, keepdims=False)
        ahead_plane = lax.dynamic_index_in_dim(moved_field, jnp.minimum(index_z + 1, plane_total - 1), 1, keepdims=False)
        behind = lax.dynamic_index_in_dim(moved_field, jnp.maximum(index_z - 1, 0), 1, keepdims=False)
        flux_z, flux_y, flux_x = plane_flux(here_plane, ahead_plane)
        prior_z, prior_y, prior_x = plane_flux(behind, here_plane)
        prior_z = prior_z * (index_z > 0).astype(moved_field.dtype)
        divergence = flux_z - prior_z + backward_diff(flux_y, 1) + backward_diff(flux_x, 2)
        return here_plane + tv_step_size * divergence
    planes_out = lax.map(one_plane, jnp.arange(plane_total, dtype=jnp.int32))
    return jnp.moveaxis(planes_out, 0, 1)

def reference(field, hologram, defocus):
    length_total = field.shape[-1]
    plane_total = field.shape[1]
    zero_plane = jnp.zeros((length_total, length_total), jnp.float32)
    estimate = field
    for step_index in range(ITERS):

        def add_plane(summed, scan_item):
            real_part, imag_part, depth_value = scan_item
            spectrum = jnp.fft.fft2(lax.complex(real_part, imag_part))
            phase_table = defocus_phase(depth_value, length_total)
            return (summed + spectrum * lax.complex(jnp.cos(phase_table), -jnp.sin(phase_table)), None)
        summed, unused = lax.scan(add_plane, lax.complex(zero_plane, zero_plane), (estimate[0], estimate[1], defocus))
        image_real = jnp.real(jnp.fft.ifft2(summed))
        misfit = image_real - hologram
        misfit_spec = jnp.fft.fft2(lax.complex(misfit, jnp.zeros_like(misfit)))

        def adjoint_plane(depth_value):
            phase_table = defocus_phase(depth_value, length_total)
            plane_field = jnp.fft.ifft2(misfit_spec * lax.complex(jnp.cos(phase_table), jnp.sin(phase_table)))
            return (jnp.real(plane_field), jnp.imag(plane_field))
        grad_real, grad_imag = lax.map(adjoint_plane, defocus)
        gradient = jnp.stack([grad_real, grad_imag])
        moved_field = estimate - 1.0 / plane_total * gradient
        estimate = tv_shrink(moved_field)
    return estimate
```

```python
import functools
import math

import jax
import jax.numpy as jnp
import ml_dtypes
import numpy as np
from jax import lax
from jax.experimental import pallas as pl
from jax.experimental.pallas import tpu as pltpu
from jax.sharding import Mesh
from jax.sharding import PartitionSpec as P

tv_step_size = 1.0 / 12.0
tv_sharpness = 0.25

N = 4096
RADIX = 16
INNER = 256
CLASSES = 9
PLANES = 8
LANES = 128
F32 = jnp.float32
BF16 = jnp.bfloat16

DEPTH = ("x_lo", "y")
ROW = ("x_hi", "z", "core")
LAYER = ("x_lo", "y", "x_hi", "core")


def split_table(table):
    high = table.astype(ml_dtypes.bfloat16)
    low = (table - high.astype(np.float64)).astype(ml_dtypes.bfloat16)
    return high, low


def inner_tables():
    index = np.arange(INNER)
    angle = 2.0 * np.pi * (np.outer(index, index) % INNER) / INNER
    cosine, sine = np.cos(angle), np.sin(angle)
    tables = []
    for sign in (1.0, -1.0):
        whole = np.block([[cosine, -sign * sine], [sign * sine, cosine]])
        high, low = split_table(whole)
        tables.append(np.concatenate([high, high, low], axis=0))
    return tables


def twiddles():
    angle = 2.0 * np.pi * np.outer(np.arange(RADIX), np.arange(INNER)) / N
    return np.stack([np.cos(angle), np.sin(angle)]).astype(np.float32)


def class_frequencies():
    return (RADIX * np.arange(INNER)[None, :] + np.arange(CLASSES)[:, None]) % N


def class_tables():
    freq = class_frequencies()
    angle = 2.0 * np.pi * ((freq[:, :, None] * np.arange(INNER)[None, None, :]) % N) / N
    table = np.concatenate([np.cos(angle), np.sin(angle)], axis=1)
    high, low = split_table(table)
    forward = np.concatenate([high, high, low], axis=2)
    high, low = split_table(np.swapaxes(table, 1, 2))
    backward = np.concatenate([high, high, low], axis=2)
    return forward, backward


def squares_of(index):
    centred = np.where(index < N // 2, index, index - N)
    return (centred * centred).astype(np.float32)


def dft4(values, inverse):
    (ar, ai), (br, bi), (cr, ci), (dr, di) = values
    s0r, s0i, s1r, s1i = ar + cr, ai + ci, ar - cr, ai - ci
    s2r, s2i, s3r, s3i = br + dr, bi + di, br - dr, bi - di
    plus = (s1r - s3i, s1i + s3r)
    minus = (s1r + s3i, s1i - s3r)
    first, third = (plus, minus) if inverse else (minus, plus)
    return [(s0r + s2r, s0i + s2i), first, (s0r - s2r, s0i - s2i), third]


def times_constant(value, cosine, sine):
    real, imag = value
    if abs(sine) < 1e-9 and abs(cosine - 1.0) < 1e-9:
        return value
    if abs(cosine) < 1e-9 and abs(sine - 1.0) < 1e-9:
        return (-imag, real)
    if abs(cosine) < 1e-9 and abs(sine + 1.0) < 1e-9:
        return (imag, -real)
    if abs(abs(cosine) - abs(sine)) < 1e-9:
        root = math.sqrt(0.5)
        sc, ss = math.copysign(1.0, cosine), math.copysign(1.0, sine)
        first = (real if sc > 0 else -real) - (imag if ss > 0 else -imag)
        second = (imag if sc > 0 else -imag) + (real if ss > 0 else -real)
        return (first * root, second * root)
    return (real * cosine - imag * sine, imag * cosine + real * sine)


def dft16(values, inverse):
    direction = 1.0 if inverse else -1.0
    stage = [dft4([values[4 * n1 + n2] for n1 in range(4)], inverse) for n2 in range(4)]
    result = [None] * 16
    for k1 in range(4):
        column = []
        for n2 in range(4):
            angle = direction * 2.0 * math.pi * n2 * k1 / 16
            column.append(times_constant(stage[n2][k1], math.cos(angle), math.sin(angle)))
        for k2, value in enumerate(dft4(column, inverse)):
            result[k1 + 4 * k2] = value
    return result


def weighted_sum(terms):
    total = None
    for coefficient, value in terms:
        if abs(coefficient) < 1e-9:
            continue
        if abs(coefficient - 1.0) < 1e-9:
            total = value if total is None else total + value
        elif abs(coefficient + 1.0) < 1e-9:
            total = -value if total is None else total - value
        else:
            piece = value * float(np.float32(coefficient))
            total = piece if total is None else total + piece
    return total


def real_dft16(blocks):
    sums = [blocks[0]] + [blocks[b] + blocks[16 - b] for b in range(1, 8)] + [blocks[8]]
    diffs = [None] + [blocks[b] - blocks[16 - b] for b in range(1, 8)]
    result = []
    for k in range(CLASSES):
        real = weighted_sum([(math.cos(2 * math.pi * k * b / 16), sums[b]) for b in range(9)])
        if k in (0, 8):
            imag = jnp.zeros_like(real)
        else:
            imag = weighted_sum(
                [(-math.sin(2 * math.pi * k * b / 16), diffs[b]) for b in range(1, 8)]
            )
        result.append((real, imag))
    return result


def real_inverse16(values):
    result = [None] * 16
    for b in range(9):
        even = weighted_sum([(math.cos(2 * math.pi * k * b / 16), values[k][0]) for k in range(9)])
        if b in (0, 8):
            result[b] = even
        else:
            odd = weighted_sum(
                [(math.sin(2 * math.pi * k * b / 16), values[k][1]) for k in range(1, 8)]
            )
            result[b] = even - odd
            result[16 - b] = even + odd
    return result


def halves(value):
    high = value.astype(BF16)
    low = (value - high.astype(F32)).astype(BF16)
    return high, low


STEP_ROWS = 32
CHUNK_CLASSES = 8


def filter_rows(load, store, tw_ref, d_ref, wf_ref, wi_ref, x_ref):
    groups = [(r, h) for r in range(STEP_ROWS // 8) for h in range(INNER // LANES)]
    for r, h in groups:
        values = [load(r, b * (INNER // LANES) + h) for b in range(RADIX)]
        lanes = slice(h * LANES, (h + 1) * LANES)
        for k, (real, imag) in enumerate(dft16(values, False)):
            if k:
                cosine, sine = tw_ref[0, k : k + 1, lanes], tw_ref[1, k : k + 1, lanes]
                real, imag = real * cosine + imag * sine, imag * cosine - real * sine
            rows = slice(k * STEP_ROWS + 8 * r, k * STEP_ROWS + 8 * r + 8)
            x_ref[rows, lanes] = real
            x_ref[rows, INNER + h * LANES : INNER + (h + 1) * LANES] = imag
    for chunk in range(RADIX // CHUNK_CLASSES):
        base = chunk * CHUNK_CLASSES * STEP_ROWS
        rows = slice(base, base + CHUNK_CLASSES * STEP_ROWS)
        high, low = halves(x_ref[rows, :])
        spectrum = jnp.dot(
            jnp.concatenate([high, low, high], axis=1), wf_ref[...], preferred_element_type=F32
        )
        pieces = []
        for kk in range(CHUNK_CLASSES):
            k = chunk * CHUNK_CLASSES + kk
            cosine, sine = d_ref[0, k : k + 1, :], d_ref[1, k : k + 1, :]
            real = spectrum[kk * STEP_ROWS : (kk + 1) * STEP_ROWS, :INNER]
            imag = spectrum[kk * STEP_ROWS : (kk + 1) * STEP_ROWS, INNER:]
            pieces.append(
                jnp.concatenate(
                    [real * cosine - imag * sine, imag * cosine + real * sine], axis=1
                )
            )
        high, low = halves(jnp.concatenate(pieces, axis=0))
        x_ref[rows, :] = jnp.dot(
            jnp.concatenate([high, low, high], axis=1), wi_ref[...], preferred_element_type=F32
        )
    for r, h in groups:
        lanes = slice(h * LANES, (h + 1) * LANES)
        values = []
        for k in range(RADIX):
            rows = slice(k * STEP_ROWS + 8 * r, k * STEP_ROWS + 8 * r + 8)
            real = x_ref[rows, lanes]
            imag = x_ref[rows, INNER + h * LANES : INNER + (h + 1) * LANES]
            if k:
                cosine, sine = tw_ref[0, k : k + 1, lanes], tw_ref[1, k : k + 1, lanes]
                real, imag = real * cosine - imag * sine, imag * cosine + real * sine
            values.append((real, imag))
        for b, value in enumerate(dft16(values, True)):
            store(r, b * (INNER // LANES) + h, value)


def forward_x_kernel(f_ref, hol_ref, tw_ref, d_ref, wf_ref, wi_ref, o_ref, x_ref):
    step = pl.program_id(0)

    @pl.when(step == 0)
    def _():
        for j in range(32):
            o_ref[j, 256:272, :] = hol_ref[:, j * LANES : (j + 1) * LANES]

    def load(r, j):
        rows, lanes = slice(8 * r, 8 * r + 8), slice(j * LANES, (j + 1) * LANES)
        return f_ref[0, rows, lanes], f_ref[1, rows, lanes]

    def store(r, j, value):
        for c in range(2):
            start = pl.multiple_of(step * STEP_ROWS + 128 * c + 8 * r, 8)
            o_ref[j, pl.ds(start, 8), :] = value[c]

    filter_rows(load, store, tw_ref, d_ref, wf_ref, wi_ref, x_ref)


def backward_x_kernel(g_ref, f_ref, tw_ref, d_ref, wf_ref, wi_ref, o_ref, x_ref):
    def load(r, j):
        rows = slice(8 * r, 8 * r + 8)
        return g_ref[j, 0, rows, :], g_ref[j, 1, rows, :]

    def store(r, j, value):
        rows, lanes = slice(8 * r, 8 * r + 8), slice(j * LANES, (j + 1) * LANES)
        for c in range(2):
            o_ref[c, rows, lanes] = f_ref[c, rows, lanes] + value[c]

    filter_rows(load, store, tw_ref, d_ref, wf_ref, wi_ref, x_ref)


def whole(shape):
    return pl.BlockSpec(shape, lambda *_: (0,) * len(shape))


def params():
    return pltpu.CompilerParams(vmem_limit_bytes=56 << 20)


def x_tables():
    forward, inverse = inner_tables()
    return jnp.asarray(twiddles()), jnp.asarray(forward), jnp.asarray(inverse)


def forward_x(field, hologram_rows, transfer):
    tw, wf, wi = x_tables()
    return pl.pallas_call(
        forward_x_kernel,
        grid=(128 // STEP_ROWS,),
        in_specs=[
            pl.BlockSpec((2, STEP_ROWS, N), lambda i: (0, i, 0)),
            whole((16, N)),
            whole((2, RADIX, INNER)),
            whole((2, RADIX, INNER)),
            whole((1536, 512)),
            whole((1536, 512)),
        ],
        out_specs=whole((32, 272, LANES)),
        out_shape=jax.ShapeDtypeStruct((32, 272, LANES), F32),
        scratch_shapes=[pltpu.VMEM((RADIX * STEP_ROWS, 2 * INNER), F32)],
        compiler_params=params(),
        name="filter_x_forward",
    )(field, hologram_rows, tw, transfer, wf, wi)


def backward_x(gradient, field, transfer):
    tw, wf, wi = x_tables()
    return pl.pallas_call(
        backward_x_kernel,
        grid=(128 // STEP_ROWS,),
        in_specs=[
            pl.BlockSpec((32, 2, STEP_ROWS, LANES), lambda i: (0, 0, i, 0)),
            pl.BlockSpec((2, STEP_ROWS, N), lambda i: (0, i, 0)),
            whole((2, RADIX, INNER)),
            whole((2, RADIX, INNER)),
            whole((1536, 512)),
            whole((1536, 512)),
        ],
        out_specs=pl.BlockSpec((2, STEP_ROWS, N), lambda i: (0, i, 0)),
        out_shape=jax.ShapeDtypeStruct((2, 128, N), F32),
        scratch_shapes=[pltpu.VMEM((RADIX * STEP_ROWS, 2 * INNER), F32)],
        compiler_params=params(),
        name="filter_x_backward",
    )(gradient, field, tw, transfer, wf, wi)


def forward_y_kernel(z_ref, g_ref, t_ref, tt_ref, cs_ref, o_ref, u_ref, s_ref):
    step = pl.program_id(0)

    @pl.when(step == 0)
    def _():
        @pl.loop(0, PLANES)
        def _(p):
            for core in range(2):
                for c in range(2):
                    rows = slice(c * 128, (c + 1) * 128)
                    upper = g_ref[p * 4 + core, rows, :]
                    lower = g_ref[p * 4 + 2 + core, rows, :]
                    for parity, value in ((0, upper + lower), (1, upper - lower)):
                        high, low = halves(value)
                        for part, piece in ((0, high), (1, low), (2, high)):
                            start = part * INNER + core * 128
                            u_ref[parity, p, start : start + 128, c * LANES : (c + 1) * LANES] = (
                                piece
                            )

    parity = lax.rem(step, 2)
    chunks = []
    for half in range(2):
        rows = slice(half * INNER, (half + 1) * INNER)
        total = None
        for p in range(PLANES):
            result = jnp.dot(t_ref[0, rows, :], u_ref[parity, p], preferred_element_type=F32)
            piece = (
                cs_ref[0, :, 2 * p : 2 * p + 1] * result[:, :LANES]
                + cs_ref[0, :, 2 * p + 1 : 2 * p + 2] * result[:, LANES:]
            )
            total = piece if total is None else total + piece
        chunks.append(total)
    cosine, sine = chunks
    pair = jnp.concatenate(
        [jnp.concatenate([cosine, sine], axis=0), jnp.concatenate([-sine, cosine], axis=0)], axis=1
    )
    high, low = halves(pair)
    s_ref[step] = jnp.dot(
        tt_ref[0], jnp.concatenate([high, low, high], axis=0), preferred_element_type=F32
    )

    @pl.when(step == CLASSES - 1)
    def _():
        shift = z_ref[0]

        @pl.loop(0, INNER // 8)
        def _(i):
            rows = pl.ds(pl.multiple_of(i * 8, 8), 8)
            values = [(s_ref[k, rows, :LANES], s_ref[k, rows, LANES:]) for k in range(CLASSES)]
            for b, value in enumerate(real_inverse16(values)):
                block = lax.rem(shift + b, 16)
                o_ref[lax.rem(block, 8), lax.div(block, 8), rows, :] = value


def forward_y(z_index, received, factors):
    forward, backward = class_tables()
    return pl.pallas_call(
        forward_y_kernel,
        grid=(CLASSES,),
        in_specs=[
            pl.BlockSpec(memory_space=pltpu.SMEM),
            whole((32, 272, LANES)),
            pl.BlockSpec((1, 512, 768), lambda k: (k, 0, 0)),
            pl.BlockSpec((1, 256, 1536), lambda k: (k, 0, 0)),
            pl.BlockSpec((1, 256, 16), lambda k: (k, 0, 0)),
        ],
        out_specs=whole((8, 2, INNER, LANES)),
        out_shape=jax.ShapeDtypeStruct((8, 2, INNER, LANES), F32),
        scratch_shapes=[
            pltpu.VMEM((2, PLANES, 768, 2 * LANES), BF16),
            pltpu.VMEM((CLASSES, INNER, 2 * LANES), F32),
        ],
        compiler_params=params(),
        name="filter_y_forward",
    )(z_index, received, jnp.asarray(forward), jnp.asarray(backward), factors)


def backward_y_kernel(z_ref, m_ref, t_ref, tt_ref, cs_ref, o_ref, x_ref, a_ref):
    step = pl.program_id(0)

    @pl.when(step == 0)
    def _():
        shift = z_ref[0]

        @pl.loop(0, INNER // 8)
        def _(i):
            rows = pl.ds(pl.multiple_of(i * 8, 8), 8)
            blocks = []
            for b in range(16):
                block = lax.rem(shift + b, 16)
                blocks.append(m_ref[lax.rem(block, 8), lax.div(block, 8), rows, :])
            for k, (real, imag) in enumerate(real_dft16(blocks)):
                x_ref[k, rows, :LANES] = real
                x_ref[k, rows, LANES:] = imag

        @pl.loop(0, PLANES)
        def _(p):
            for parity in range(2):
                a_ref[parity, p] = jnp.zeros((INNER, 2 * LANES), F32)

    parity = lax.rem(step, 2)
    high, low = halves(x_ref[step])
    mixed = jnp.dot(
        t_ref[0], jnp.concatenate([high, low, high], axis=0), preferred_element_type=F32
    )
    cosine = mixed[:INNER, :LANES] + mixed[INNER:, LANES:]
    sine = mixed[INNER:, :LANES] - mixed[:INNER, LANES:]
    for p in range(PLANES):
        first = cs_ref[0, :, 2 * p : 2 * p + 1]
        second = cs_ref[0, :, 2 * p + 1 : 2 * p + 2]
        product = jnp.concatenate(
            [
                jnp.concatenate([first * cosine, second * cosine], axis=1),
                jnp.concatenate([first * sine, second * sine], axis=1),
            ],
            axis=0,
        )
        high, low = halves(product)
        a_ref[parity, p] += jnp.dot(
            tt_ref[0], jnp.concatenate([high, low, high], axis=0), preferred_element_type=F32
        )

    @pl.when(step == CLASSES - 1)
    def _():
        @pl.loop(0, PLANES)
        def _(p):
            for core in range(2):
                rows = slice(core * 128, (core + 1) * 128)
                for c in range(2):
                    lanes = slice(c * LANES, (c + 1) * LANES)
                    even, odd = a_ref[0, p, rows, lanes], a_ref[1, p, rows, lanes]
                    o_ref[p * 4 + core, c] = even + odd
                    o_ref[p * 4 + 2 + core, c] = even - odd


def backward_y(z_index, misfit, factors):
    forward, backward = class_tables()
    return pl.pallas_call(
        backward_y_kernel,
        grid=(CLASSES,),
        in_specs=[
            pl.BlockSpec(memory_space=pltpu.SMEM),
            whole((8, 2, INNER, LANES)),
            pl.BlockSpec((1, 512, 768), lambda k: (k, 0, 0)),
            pl.BlockSpec((1, 256, 1536), lambda k: (k, 0, 0)),
            pl.BlockSpec((1, 256, 16), lambda k: (k, 0, 0)),
        ],
        out_specs=whole((32, 2, 128, LANES)),
        out_shape=jax.ShapeDtypeStruct((32, 2, 128, LANES), F32),
        scratch_shapes=[
            pltpu.VMEM((CLASSES, INNER, 2 * LANES), F32),
            pltpu.VMEM((2, PLANES, INNER, 2 * LANES), F32),
        ],
        compiler_params=params(),
        name="filter_y_backward",
    )(z_index, misfit, jnp.asarray(forward), jnp.asarray(backward), factors)


def moved_along(block, axes, distance, size):
    route = [(i - distance, i) for i in range(size) if 0 <= i - distance < size]
    return lax.ppermute(block, axes, route)


def diagonal(block, depth_distance, row_distance):
    route = []
    for depth in range(8):
        for row in range(32):
            from_depth, from_row = depth - depth_distance, row - row_distance
            if 0 <= from_depth < 8 and 0 <= from_row < 32:
                route.append((from_depth * 32 + from_row, depth * 32 + row))
    return lax.ppermute(block, DEPTH + ROW, route)


def flux_of(here, ahead, below, has_ahead, has_below):
    depth_diff = jnp.where(has_ahead, ahead - here, 0.0)
    row_diff = jnp.where(has_below, below - here, 0.0)
    col_diff = jnp.concatenate([here[..., 1:], here[..., -1:]], axis=-1) - here
    magnitude = jnp.sqrt(
        jnp.sum(depth_diff * depth_diff + row_diff * row_diff + col_diff * col_diff, axis=0)
    )
    factor = 1.0 / (1.0 + tv_sharpness * magnitude)
    return depth_diff * factor, row_diff * factor, col_diff * factor


def shrink(moved, depth_index, row_index):
    ahead = moved_along(moved, DEPTH, -1, 8)
    behind = moved_along(moved, DEPTH, 1, 8)
    first, last = moved[:, :1], moved[:, -1:]
    above = moved_along(last, ROW, 1, 32)
    below = moved_along(first, ROW, -1, 32)
    ahead_above = diagonal(last, -1, 1)
    behind_below = diagonal(first, 1, -1)
    has_ahead = depth_index < 7
    has_behind = depth_index > 0
    row_ids = row_index * 128 + jnp.arange(128, dtype=jnp.int32)[None, :, None]
    has_below = row_ids < N - 1
    shifted = jnp.concatenate([moved[:, 1:], below], axis=1)
    flux_z, flux_y, flux_x = flux_of(moved, ahead, shifted, has_ahead, has_below)
    _, above_y, _ = flux_of(above, ahead_above, first, has_ahead, True)
    above_y = jnp.where(row_index > 0, above_y, 0.0)
    behind_shifted = jnp.concatenate([behind[:, 1:], behind_below], axis=1)
    behind_z, _, _ = flux_of(behind, moved, behind_shifted, True, has_below)
    behind_z = jnp.where(has_behind, behind_z, 0.0)
    divergence = (
        flux_z
        - behind_z
        + flux_y
        - jnp.concatenate([above_y, flux_y[:, :-1]], axis=1)
        + flux_x
        - jnp.concatenate([jnp.zeros_like(flux_x[..., :1]), flux_x[..., :-1]], axis=-1)
    )
    return moved + tv_step_size * divergence


def phase_of(depth_values, squares):
    return depth_values * (squares * (math.pi / (N * N)))


def per_device(field, hologram, defocus):
    x_lo, y = lax.axis_index("x_lo"), lax.axis_index("y")
    x_hi, z, core = lax.axis_index("x_hi"), lax.axis_index("z"), lax.axis_index("core")
    depth_index = x_lo * 4 + y
    row_index = x_hi * 16 + z * 2 + core
    z_index = z[None].astype(jnp.int32)
    field = field[:, 0]

    x_freq = RADIX * np.arange(INNER)[None, :] + np.arange(RADIX)[:, None]
    x_phase = phase_of(defocus[0], jnp.asarray(squares_of(x_freq)))
    x_cos, x_sin = jnp.cos(x_phase) / N, jnp.sin(x_phase) / N
    x_forward = jnp.stack([x_cos, -x_sin])
    x_backward = jnp.stack([x_cos, x_sin]) * (-1.0 / PLANES)

    depths = lax.all_gather(defocus, DEPTH, tiled=True)
    y_phase = phase_of(
        depths[None, None, :], jnp.asarray(squares_of(class_frequencies()))[:, :, None]
    )
    weights = np.full((CLASSES, 1, 1), 2.0 / N, np.float32)
    weights[0] = weights[8] = 1.0 / N
    factors = jnp.stack([jnp.cos(y_phase), jnp.sin(y_phase)], axis=-1)
    factors = factors.reshape(CLASSES, INNER, 2 * PLANES) * weights

    hologram_rows = lax.dynamic_slice_in_dim(hologram, depth_index * 16, 16, 0)
    sent = forward_x(field, hologram_rows, x_forward)
    received = lax.all_to_all(sent, LAYER, 0, 0, tiled=True)
    partial = forward_y(z_index, received, factors)
    image = lax.psum_scatter(partial, "z", scatter_dimension=0, tiled=True)
    tile = received[:, 256:, :].reshape(PLANES, 2, 2, 16, LANES)
    tile = jnp.transpose(tile, (1, 2, 0, 3, 4)).reshape(1, 2, INNER, LANES)
    misfit = lax.all_gather(image - tile, "z", axis=0, tiled=True)
    sent = backward_y(z_index, misfit, factors)
    received = lax.all_to_all(sent, LAYER, 0, 0, tiled=True)
    moved = backward_x(received, field, x_backward)
    return shrink(moved, depth_index, row_index)[:, None]


def solution(mesh):
    fine = Mesh(mesh.devices.reshape(2, 4, 2, 8, 2), DEPTH + ROW)
    return jax.shard_map(
        per_device,
        mesh=fine,
        in_specs=(P(None, DEPTH, ROW, None), P(ROW, None), P(DEPTH)),
        out_specs=P(None, DEPTH, ROW, None),
        check_vma=False,
    )
```

```python
import functools
import math

import jax
import jax.numpy as jnp
import ml_dtypes
import numpy as np
from jax import lax
from jax.experimental import pallas as pl
from jax.experimental.pallas import tpu as pltpu
from jax.sharding import Mesh
from jax.sharding import PartitionSpec as P

tv_step_size = 1.0 / 12.0
tv_sharpness = 0.25

N = 4096
RADIX = 16
INNER = 256
CLASSES = 9
PLANES = 8
LANES = 128
HALF = 64
F32 = jnp.float32
BF16 = jnp.bfloat16

DEPTH = ("x_lo", "y")
ROW = ("x_hi", "z", "core")
LAYER = ("x_lo", "y", "x_hi", "core")


def split_table(table):
    high = table.astype(ml_dtypes.bfloat16)
    low = (table - high.astype(np.float64)).astype(ml_dtypes.bfloat16)
    return high, low


def inner_tables():
    index = np.arange(INNER)
    angle = 2.0 * np.pi * (np.outer(index, index) % INNER) / INNER
    cosine, sine = np.cos(angle), np.sin(angle)
    tables = []
    for sign in (1.0, -1.0):
        whole = np.block([[cosine, -sign * sine], [sign * sine, cosine]])
        high, low = split_table(whole)
        tables.append(np.concatenate([high, high, low], axis=0))
    return tables


def twiddles():
    angle = 2.0 * np.pi * np.outer(np.arange(RADIX), np.arange(INNER)) / N
    return np.stack([np.cos(angle), np.sin(angle)]).astype(np.float32)


def class_frequencies():
    return (RADIX * np.arange(INNER)[None, :] + np.arange(CLASSES)[:, None]) % N


def class_tables():
    freq = class_frequencies()
    angle = 2.0 * np.pi * ((freq[:, None, :] * np.arange(INNER)[None, :, None]) % N) / N
    table = np.concatenate([np.cos(angle), np.sin(angle)], axis=2)
    tables = []
    for each in (table, np.swapaxes(table, 1, 2)):
        high, low = split_table(each)
        tables.append(np.concatenate([high, high, low], axis=1))
    return tables


def squares_of(index):
    centred = np.where(index < N // 2, index, index - N)
    return (centred * centred).astype(np.float32)


def dft4(values, inverse):
    (ar, ai), (br, bi), (cr, ci), (dr, di) = values
    s0r, s0i, s1r, s1i = ar + cr, ai + ci, ar - cr, ai - ci
    s2r, s2i, s3r, s3i = br + dr, bi + di, br - dr, bi - di
    plus = (s1r - s3i, s1i + s3r)
    minus = (s1r + s3i, s1i - s3r)
    first, third = (plus, minus) if inverse else (minus, plus)
    return [(s0r + s2r, s0i + s2i), first, (s0r - s2r, s0i - s2i), third]


def times_constant(value, cosine, sine):
    real, imag = value
    if abs(sine) < 1e-9 and abs(cosine - 1.0) < 1e-9:
        return value
    if abs(cosine) < 1e-9 and abs(sine - 1.0) < 1e-9:
        return (-imag, real)
    if abs(cosine) < 1e-9 and abs(sine + 1.0) < 1e-9:
        return (imag, -real)
    if abs(abs(cosine) - abs(sine)) < 1e-9:
        root = math.sqrt(0.5)
        sc, ss = math.copysign(1.0, cosine), math.copysign(1.0, sine)
        first = (real if sc > 0 else -real) - (imag if ss > 0 else -imag)
        second = (imag if sc > 0 else -imag) + (real if ss > 0 else -real)
        return (first * root, second * root)
    return (real * cosine - imag * sine, imag * cosine + real * sine)


def dft16(values, inverse):
    direction = 1.0 if inverse else -1.0
    stage = [dft4([values[4 * n1 + n2] for n1 in range(4)], inverse) for n2 in range(4)]
    result = [None] * 16
    for k1 in range(4):
        column = []
        for n2 in range(4):
            angle = direction * 2.0 * math.pi * n2 * k1 / 16
            column.append(times_constant(stage[n2][k1], math.cos(angle), math.sin(angle)))
        for k2, value in enumerate(dft4(column, inverse)):
            result[k1 + 4 * k2] = value
    return result


def weighted_sum(terms):
    total = None
    for coefficient, value in terms:
        if abs(coefficient) < 1e-9:
            continue
        if abs(coefficient - 1.0) < 1e-9:
            total = value if total is None else total + value
        elif abs(coefficient + 1.0) < 1e-9:
            total = -value if total is None else total - value
        else:
            piece = value * float(np.float32(coefficient))
            total = piece if total is None else total + piece
    return total


def real_dft16(blocks):
    sums = [blocks[0]] + [blocks[b] + blocks[16 - b] for b in range(1, 8)] + [blocks[8]]
    diffs = [None] + [blocks[b] - blocks[16 - b] for b in range(1, 8)]
    result = []
    for k in range(CLASSES):
        real = weighted_sum([(math.cos(2 * math.pi * k * b / 16), sums[b]) for b in range(9)])
        if k in (0, 8):
            imag = jnp.zeros_like(real)
        else:
            imag = weighted_sum(
                [(-math.sin(2 * math.pi * k * b / 16), diffs[b]) for b in range(1, 8)]
            )
        result.append((real, imag))
    return result


def real_inverse16(values):
    result = [None] * 16
    for b in range(9):
        even = weighted_sum([(math.cos(2 * math.pi * k * b / 16), values[k][0]) for k in range(9)])
        if b in (0, 8):
            result[b] = even
        else:
            odd = weighted_sum(
                [(math.sin(2 * math.pi * k * b / 16), values[k][1]) for k in range(1, 8)]
            )
            result[b] = even - odd
            result[16 - b] = even + odd
    return result


def halves(value):
    high = value.astype(BF16)
    low = (value - high.astype(F32)).astype(BF16)
    return high, low


STEP_ROWS = 32
CHUNK_CLASSES = 16


def filter_rows(load, store, tw_ref, d_ref, wf_ref, wi_ref, x_ref):
    groups = [(r, h) for r in range(STEP_ROWS // 8) for h in range(INNER // LANES)]
    for r, h in groups:
        values = [load(r, b * (INNER // LANES) + h) for b in range(RADIX)]
        lanes = slice(h * LANES, (h + 1) * LANES)
        for k, (real, imag) in enumerate(dft16(values, False)):
            if k:
                cosine, sine = tw_ref[0, k : k + 1, lanes], tw_ref[1, k : k + 1, lanes]
                real, imag = real * cosine + imag * sine, imag * cosine - real * sine
            rows = slice(k * STEP_ROWS + 8 * r, k * STEP_ROWS + 8 * r + 8)
            x_ref[rows, lanes] = real
            x_ref[rows, INNER + h * LANES : INNER + (h + 1) * LANES] = imag
    for chunk in range(RADIX // CHUNK_CLASSES):
        base = chunk * CHUNK_CLASSES * STEP_ROWS
        rows = slice(base, base + CHUNK_CLASSES * STEP_ROWS)
        high, low = halves(x_ref[rows, :])
        spectrum = jnp.dot(
            jnp.concatenate([high, low, high], axis=1), wf_ref[...], preferred_element_type=F32
        )
        pieces = []
        for kk in range(CHUNK_CLASSES):
            k = chunk * CHUNK_CLASSES + kk
            cosine, sine = per_row(d_ref[0, k]), per_row(d_ref[1, k])
            real = spectrum[kk * STEP_ROWS : (kk + 1) * STEP_ROWS, :INNER]
            imag = spectrum[kk * STEP_ROWS : (kk + 1) * STEP_ROWS, INNER:]
            pieces.append(
                jnp.concatenate(
                    [real * cosine - imag * sine, imag * cosine + real * sine], axis=1
                )
            )
        high, low = halves(jnp.concatenate(pieces, axis=0))
        x_ref[rows, :] = jnp.dot(
            jnp.concatenate([high, low, high], axis=1), wi_ref[...], preferred_element_type=F32
        )
    for r, h in groups:
        lanes = slice(h * LANES, (h + 1) * LANES)
        values = []
        for k in range(RADIX):
            rows = slice(k * STEP_ROWS + 8 * r, k * STEP_ROWS + 8 * r + 8)
            real = x_ref[rows, lanes]
            imag = x_ref[rows, INNER + h * LANES : INNER + (h + 1) * LANES]
            if k:
                cosine, sine = tw_ref[0, k : k + 1, lanes], tw_ref[1, k : k + 1, lanes]
                real, imag = real * cosine - imag * sine, imag * cosine + real * sine
            values.append((real, imag))
        for b, value in enumerate(dft16(values, True)):
            store(r, b * (INNER // LANES) + h, value)


def per_row(factor):
    if factor.shape[0] == 1:
        return factor
    return jnp.concatenate([factor] * (STEP_ROWS // factor.shape[0]), axis=0)


def low_lanes(shape):
    return lax.broadcasted_iota(jnp.int32, shape, len(shape) - 1) < HALF


def exchange_halves(first, second):
    low = low_lanes(first.shape)
    axis = first.ndim - 1
    return (
        jnp.where(low, first, pltpu.roll(second, HALF, axis)),
        jnp.where(low, pltpu.roll(first, HALF, axis), second),
    )


def forward_x_kernel(f_ref, hol_ref, tw_ref, d_ref, wf_ref, wi_ref, a_ref, b_ref, x_ref):
    step = pl.program_id(0)

    @pl.when(step == 0)
    def _():
        for j in range(32):
            lanes = slice(j * LANES, (j + 1) * LANES)
            first, second = exchange_halves(hol_ref[0, :, lanes], hol_ref[1, :, lanes])
            a_ref[j, 128:136, :] = first
            b_ref[j, 128:136, :] = second

    def load(r, j):
        rows, lanes = slice(8 * r, 8 * r + 8), slice(j * LANES, (j + 1) * LANES)
        return f_ref[0, rows, lanes], f_ref[1, rows, lanes]

    def store(r, j, value):
        rows = pl.ds(pl.multiple_of(step * STEP_ROWS + 8 * r, 8), 8)
        first, second = exchange_halves(*value)
        a_ref[j, rows, :] = first
        b_ref[j, rows, :] = second

    filter_rows(load, store, tw_ref, d_ref, wf_ref, wi_ref, x_ref)


def backward_x_kernel(ga_ref, gb_ref, fr_ref, fi_ref, tw_ref, d_ref, wf_ref, wi_ref, o_ref, x_ref, f_ref):
    step = pl.program_id(0)

    @pl.when(step == 0)
    def _():
        for c, source in ((0, fr_ref), (1, fi_ref)):
            for p in range(PLANES):
                for j in range(N // LANES):
                    f_ref[c, j, pl.ds(p, 16, stride=PLANES), :] = source[
                        p, :, j * LANES : (j + 1) * LANES
                    ]

    def load(r, j):
        rows = slice(8 * r, 8 * r + 8)
        return exchange_halves(ga_ref[j, rows, :], gb_ref[j, rows, :])

    def store(r, j, value):
        rows, lanes = slice(8 * r, 8 * r + 8), slice(j * LANES, (j + 1) * LANES)
        held = pl.ds(pl.multiple_of(step * STEP_ROWS + 8 * r, 8), 8)
        for c in range(2):
            o_ref[c, rows, lanes] = f_ref[c, j, held, :] + value[c]

    filter_rows(load, store, tw_ref, d_ref, wf_ref, wi_ref, x_ref)


def whole(shape):
    return pl.BlockSpec(shape, lambda *_: (0,) * len(shape))


def params():
    return pltpu.CompilerParams(vmem_limit_bytes=56 << 20)


def x_tables():
    forward, inverse = inner_tables()
    return jnp.asarray(twiddles()), jnp.asarray(forward), jnp.asarray(inverse)


def forward_x(field, hologram_rows, transfer):
    tw, wf, wi = x_tables()
    return pl.pallas_call(
        forward_x_kernel,
        grid=(128 // STEP_ROWS,),
        in_specs=[
            pl.BlockSpec((2, STEP_ROWS, N), lambda i: (0, i, 0)),
            whole((2, 8, N)),
            whole((2, RADIX, INNER)),
            whole((2, RADIX, 1, INNER)),
            whole((1536, 512)),
            whole((1536, 512)),
        ],
        out_specs=[whole((32, 136, LANES))] * 2,
        out_shape=[jax.ShapeDtypeStruct((32, 136, LANES), F32)] * 2,
        scratch_shapes=[pltpu.VMEM((RADIX * STEP_ROWS, 2 * INNER), F32)],
        compiler_params=params(),
        name="filter_x_forward",
    )(field, hologram_rows, tw, transfer, wf, wi)


def backward_x(first, second, field_real, field_imag, transfer):
    tw, wf, wi = x_tables()
    return pl.pallas_call(
        backward_x_kernel,
        grid=(128 // STEP_ROWS,),
        in_specs=[
            pl.BlockSpec((32, STEP_ROWS, LANES), lambda i: (0, i, 0)),
            pl.BlockSpec((32, STEP_ROWS, LANES), lambda i: (0, i, 0)),
            whole((PLANES, 16, N)),
            whole((PLANES, 16, N)),
            whole((2, RADIX, INNER)),
            whole((2, RADIX, PLANES, INNER)),
            whole((1536, 512)),
            whole((1536, 512)),
        ],
        out_specs=pl.BlockSpec((2, STEP_ROWS, N), lambda i: (0, i, 0)),
        out_shape=jax.ShapeDtypeStruct((2, 128, N), F32),
        scratch_shapes=[
            pltpu.VMEM((RADIX * STEP_ROWS, 2 * INNER), F32),
            pltpu.VMEM((2, N // LANES, 128, LANES), F32),
        ],
        compiler_params=params(),
        name="filter_x_backward",
    )(first, second, field_real, field_imag, tw, transfer, wf, wi)


DOT_PLANES = 4


def forward_y_kernel(z_ref, g_ref, t_ref, tt_ref, cs_ref, o_ref, h_ref, u_ref, s_ref):
    step = pl.program_id(0)

    @pl.when(step == 0)
    def _():
        @pl.loop(0, PLANES)
        def _(p):
            held = pl.ds(pl.multiple_of(p * LANES, LANES), LANES)
            for core in range(2):
                upper = g_ref[p * 4 + core, :128, :].T
                lower = g_ref[p * 4 + 2 + core, :128, :].T
                for parity, value in ((0, upper + lower), (1, upper - lower)):
                    high, low = halves(value)
                    for part, piece in ((0, high), (1, low), (2, high)):
                        start = part * INNER + core * 128
                        u_ref[parity, held, start : start + 128] = piece

        for upper in range(2):
            for core in range(2):
                rows = [g_ref[p * 4 + upper * 2 + core, 128:, :] for p in range(PLANES)]
                block = jnp.concatenate(rows, axis=0).T
                block = jnp.concatenate([block[:HALF], block[HALF:]], axis=1)
                h_ref[0, upper, :, core * 128 : (core + 1) * 128] = block

    parity = lax.rem(step, 2)
    total = None
    for chunk in range(PLANES // DOT_PLANES):
        rows = slice(chunk * DOT_PLANES * LANES, (chunk + 1) * DOT_PLANES * LANES)
        result = jnp.dot(u_ref[parity, rows, :], t_ref[0], preferred_element_type=F32)
        for i in range(DOT_PLANES):
            p = chunk * DOT_PLANES + i
            piece = (
                cs_ref[0, 2 * p : 2 * p + 1, :] * result[i * LANES : i * LANES + HALF]
                + cs_ref[0, 2 * p + 1 : 2 * p + 2, :] * result[i * LANES + HALF : (i + 1) * LANES]
            )
            total = piece if total is None else total + piece
    turned = jnp.concatenate([-total[:, INNER:], total[:, :INNER]], axis=1)
    high, low = halves(jnp.concatenate([total, turned], axis=0))
    s_ref[step] = jnp.dot(
        jnp.concatenate([high, low, high], axis=1), tt_ref[0], preferred_element_type=F32
    )

    @pl.when(step == CLASSES - 1)
    def _():
        shift = z_ref[0]

        @pl.loop(0, HALF // 8)
        def _(i):
            rows = pl.ds(pl.multiple_of(i * 8, 8), 8)
            other = pl.ds(pl.multiple_of(HALF + i * 8, 8), 8)
            for half in range(2):
                lanes = slice(half * LANES, (half + 1) * LANES)
                values = [(s_ref[k, rows, lanes], s_ref[k, other, lanes]) for k in range(CLASSES)]
                for b, value in enumerate(real_inverse16(values)):
                    block = lax.rem(shift + b, 16)
                    o_ref[lax.rem(block, 8), lax.div(block, 8), rows, lanes] = value


def forward_y(z_index, received, factors):
    forward, backward = class_tables()
    return pl.pallas_call(
        forward_y_kernel,
        grid=(CLASSES,),
        in_specs=[
            pl.BlockSpec(memory_space=pltpu.SMEM),
            whole((32, 136, LANES)),
            pl.BlockSpec((1, 768, 512), lambda k: (k, 0, 0)),
            pl.BlockSpec((1, 1536, 256), lambda k: (k, 0, 0)),
            pl.BlockSpec((1, 16, 512), lambda k: (k, 0, 0)),
        ],
        out_specs=[whole((8, 2, HALF, INNER)), whole((1, 2, HALF, INNER))],
        out_shape=[
            jax.ShapeDtypeStruct((8, 2, HALF, INNER), F32),
            jax.ShapeDtypeStruct((1, 2, HALF, INNER), F32),
        ],
        scratch_shapes=[
            pltpu.VMEM((2, PLANES * LANES, 768), BF16),
            pltpu.VMEM((CLASSES, LANES, INNER), F32),
        ],
        compiler_params=params(),
        name="filter_y_forward",
    )(z_index, received, jnp.asarray(forward), jnp.asarray(backward), factors)


def backward_y_kernel(z_ref, m_ref, t_ref, tt_ref, cs_ref, o_ref, x_ref, a_ref):
    step = pl.program_id(0)

    @pl.when(step == 0)
    def _():
        shift = z_ref[0]

        @pl.loop(0, HALF // 8)
        def _(i):
            rows = pl.ds(pl.multiple_of(i * 8, 8), 8)
            other = pl.ds(pl.multiple_of(HALF + i * 8, 8), 8)
            for half in range(2):
                lanes = slice(half * LANES, (half + 1) * LANES)
                blocks = []
                for b in range(16):
                    block = lax.rem(shift + b, 16)
                    blocks.append(m_ref[lax.rem(block, 8), lax.div(block, 8), rows, lanes])
                for k, (real, imag) in enumerate(real_dft16(blocks)):
                    x_ref[k, rows, lanes] = real
                    x_ref[k, other, lanes] = imag

        @pl.loop(0, PLANES)
        def _(p):
            held = pl.ds(pl.multiple_of(p * LANES, LANES), LANES)
            for parity in range(2):
                a_ref[parity, held, :] = jnp.zeros((LANES, INNER), F32)

    parity = lax.rem(step, 2)
    high, low = halves(x_ref[step])
    mixed = jnp.dot(
        jnp.concatenate([high, low, high], axis=1), t_ref[0], preferred_element_type=F32
    )
    cosine = mixed[:HALF, :INNER] + mixed[HALF:, INNER:]
    sine = mixed[:HALF, INNER:] - mixed[HALF:, :INNER]
    spectrum = jnp.concatenate([cosine, sine], axis=1)
    for chunk in range(PLANES // DOT_PLANES):
        rows = slice(chunk * DOT_PLANES * LANES, (chunk + 1) * DOT_PLANES * LANES)
        pieces = []
        for row in range(2 * DOT_PLANES * chunk, 2 * DOT_PLANES * (chunk + 1)):
            pieces.append(cs_ref[0, row : row + 1, :] * spectrum)
        high, low = halves(jnp.concatenate(pieces, axis=0))
        a_ref[parity, rows, :] += jnp.dot(
            jnp.concatenate([high, low, high], axis=1), tt_ref[0], preferred_element_type=F32
        )

    @pl.when(step == CLASSES - 1)
    def _():
        @pl.loop(0, PLANES)
        def _(p):
            rows = pl.ds(pl.multiple_of(p * LANES, LANES), LANES)
            for core in range(2):
                lanes = slice(core * 128, (core + 1) * 128)
                even, odd = a_ref[0, rows, lanes], a_ref[1, rows, lanes]
                upper, lower = (even + odd).T, (even - odd).T
                for owner in range(PLANES):
                    part = slice(owner * 16, owner * 16 + 16)
                    held = pl.ds(p, 16, stride=PLANES)
                    o_ref[owner * 4 + core, held, :] = upper[part]
                    o_ref[owner * 4 + 2 + core, held, :] = lower[part]


def backward_y(z_index, misfit, factors):
    forward, backward = class_tables()
    return pl.pallas_call(
        backward_y_kernel,
        grid=(CLASSES,),
        in_specs=[
            pl.BlockSpec(memory_space=pltpu.SMEM),
            whole((8, 2, HALF, INNER)),
            pl.BlockSpec((1, 768, 512), lambda k: (k, 0, 0)),
            pl.BlockSpec((1, 1536, 256), lambda k: (k, 0, 0)),
            pl.BlockSpec((1, 16, 512), lambda k: (k, 0, 0)),
        ],
        out_specs=whole((32, 128, LANES)),
        out_shape=jax.ShapeDtypeStruct((32, 128, LANES), F32),
        scratch_shapes=[
            pltpu.VMEM((CLASSES, LANES, INNER), F32),
            pltpu.VMEM((2, PLANES * LANES, INNER), F32),
        ],
        compiler_params=params(),
        name="filter_y_backward",
    )(z_index, misfit, jnp.asarray(forward), jnp.asarray(backward), factors)


TV_ROWS = 8


def shrink_kernel(edge_ref, m_ref, next_ref, above_ref, below_ref, o_ref, e_ref, prior_ref):
    step = pl.program_id(0)
    plane = lax.broadcasted_iota(jnp.int32, (PLANES, N), 0)
    column = lax.broadcasted_iota(jnp.int32, (PLANES, N), 1)
    last_plane, first_plane = plane == PLANES - 1, plane == 0
    last_column, first_column = column == N - 1, column == 0

    def flux(here, below):
        squares = None
        diffs = []
        for c in range(2):
            depth = jnp.where(last_plane, 0.0, pltpu.roll(here[c], PLANES - 1, 0) - here[c])
            row = below[c] - here[c]
            col = jnp.where(last_column, 0.0, pltpu.roll(here[c], N - 1, 1) - here[c])
            diffs.append((depth, row, col))
            term = depth * depth + row * row + col * col
            squares = term if squares is None else squares + term
        factor = 1.0 / (1.0 + tv_sharpness * jnp.sqrt(squares))
        return [tuple(d * factor for d in triple) for triple in diffs]

    @pl.when(step == 0)
    def _():
        above = [above_ref[c] for c in range(2)]
        first = [m_ref[c, :PLANES, :] for c in range(2)]
        terms = flux(above, first)
        for c in range(2):
            prior_ref[c] = jnp.where(edge_ref[0] > 0, terms[c][1], 0.0)

    def row_at(t):
        rows = pl.ds(pl.multiple_of(t * PLANES, PLANES), PLANES)
        return [m_ref[c, rows, :] for c in range(2)]

    def emit(t, here, below):
        terms = flux(here, below)
        rows = pl.ds(pl.multiple_of(t * PLANES, PLANES), PLANES)
        for c in range(2):
            depth, row, col = terms[c]
            divergence = (
                (depth - jnp.where(first_plane, 0.0, pltpu.roll(depth, 1, 0)))
                + (row - prior_ref[c])
                + (col - jnp.where(first_column, 0.0, pltpu.roll(col, 1, 1)))
            )
            prior_ref[c] = row
            estimate = here[c] + tv_step_size * divergence
            for j in range(N // LANES):
                e_ref[c, j, rows, :] = estimate[:, j * LANES : (j + 1) * LANES]

    @pl.loop(0, TV_ROWS - 1)
    def _(t):
        emit(t, row_at(t), row_at(t + 1))

    here = row_at(TV_ROWS - 1)
    final = step == 16 // TV_ROWS - 1
    below = []
    for c in range(2):
        beyond = jnp.where(edge_ref[1] > 0, below_ref[c], here[c])
        below.append(jnp.where(final, beyond, next_ref[c]))
    emit(TV_ROWS - 1, here, below)
    for p in range(PLANES):
        for c in range(2):
            for j in range(N // LANES):
                held = pl.ds(p, TV_ROWS, stride=PLANES)
                o_ref[p, c, :, j * LANES : (j + 1) * LANES] = e_ref[c, j, held, :]


def shrink(edges, moved, above, below):
    steps = 16 // TV_ROWS
    return pl.pallas_call(
        shrink_kernel,
        grid=(steps,),
        in_specs=[
            pl.BlockSpec(memory_space=pltpu.SMEM),
            pl.BlockSpec((2, TV_ROWS * PLANES, N), lambda i: (0, i, 0)),
            pl.BlockSpec((2, PLANES, N), lambda i: (0, jnp.minimum((i + 1) * TV_ROWS, 15), 0)),
            whole((2, PLANES, N)),
            whole((2, PLANES, N)),
        ],
        out_specs=pl.BlockSpec((PLANES, 2, TV_ROWS, N), lambda i: (0, 0, i, 0)),
        out_shape=jax.ShapeDtypeStruct((PLANES, 2, 16, N), F32),
        scratch_shapes=[
            pltpu.VMEM((2, N // LANES, TV_ROWS * PLANES, LANES), F32),
            pltpu.VMEM((2, PLANES, N), F32),
        ],
        compiler_params=params(),
        name="tv_shrink",
    )(edges, moved, moved, above, below)


def along_rows(block, distance):
    place = lambda line: (line % 8) * 32 + line // 8
    route = [
        (place(line - distance), place(line)) for line in range(256) if 0 <= line - distance < 256
    ]
    return lax.ppermute(block, DEPTH + ROW, route)


def phase_of(depth_values, squares):
    return depth_values * (squares * (math.pi / (N * N)))


def per_device(field, hologram, defocus):
    x_lo, y = lax.axis_index("x_lo"), lax.axis_index("y")
    x_hi, z, core = lax.axis_index("x_hi"), lax.axis_index("z"), lax.axis_index("core")
    depth_index = x_lo * 4 + y
    row_index = x_hi * 16 + z * 2 + core
    z_index = z[None].astype(jnp.int32)
    field = field[:, 0]

    x_freq = RADIX * np.arange(INNER)[None, :] + np.arange(RADIX)[:, None]
    x_squares = jnp.asarray(squares_of(x_freq))[:, None, :]
    x_phase = phase_of(defocus[0], x_squares)
    x_forward = jnp.stack([jnp.cos(x_phase) / N, -jnp.sin(x_phase) / N])

    depths = lax.all_gather(defocus, DEPTH, tiled=True)
    x_phase = phase_of(depths[None, :, None], x_squares)
    x_backward = jnp.stack([jnp.cos(x_phase), jnp.sin(x_phase)]) * (-1.0 / (PLANES * N))
    y_squares = jnp.asarray(squares_of(class_frequencies()))[:, None, None, :]
    y_phase = phase_of(depths[None, :, None, None], y_squares)
    weights = np.full((CLASSES, 1, 1, 1), 2.0 / N, np.float32)
    weights[0] = weights[8] = 1.0 / N
    factors = jnp.concatenate([jnp.cos(y_phase), jnp.sin(y_phase)], axis=2) * weights
    factors = factors.reshape(CLASSES, 2 * PLANES, INNER)
    factors = jnp.concatenate([factors, factors], axis=2)

    hologram_rows = lax.dynamic_slice_in_dim(
        hologram.reshape(2, HALF, N), depth_index * 8, 8, axis=1
    )
    sent = forward_x(field, hologram_rows, x_forward)
    first = lax.all_to_all(sent[0], LAYER, 0, 0, tiled=True)
    first, later = lax.optimization_barrier((first, sent[1]))
    second = lax.all_to_all(later, LAYER, 0, 0, tiled=True)
    second, field = lax.optimization_barrier((second, field))
    held = [
        lax.all_to_all(field[c].reshape(PLANES, 16, N), DEPTH, 0, 0, tiled=True) for c in range(2)
    ]
    returned = []
    for received in (first, second):
        partial, tile = forward_y(z_index, received, factors)
        image = lax.psum_scatter(partial, "z", scatter_dimension=0, tiled=True)
        misfit = lax.all_gather(image - tile, "z", axis=0, tiled=True)
        sent = backward_y(z_index, misfit, factors)
        returned.append(lax.all_to_all(sent, LAYER, 0, 0, tiled=True))
    moved = backward_x(returned[0], returned[1], held[0], held[1], x_backward)
    above = along_rows(moved[:, 120:], 1)
    below = along_rows(moved[:, :8], -1)
    line = row_index * 8 + depth_index
    edges = jnp.stack([line > 0, line < 255]).astype(jnp.int32)
    estimate = shrink(edges, moved, above, below)
    estimate = lax.all_to_all(estimate, DEPTH, 0, 0, tiled=True)
    return jnp.transpose(estimate, (1, 0, 2, 3)).reshape(2, 1, 128, N)


def solution(mesh):
    fine = Mesh(mesh.devices.reshape(2, 4, 2, 8, 2), DEPTH + ROW)
    return jax.shard_map(
        per_device,
        mesh=fine,
        in_specs=(P(None, DEPTH, ROW, None), P(ROW, None), P(DEPTH)),
        out_specs=P(None, DEPTH, ROW, None),
        check_vma=False,
    )
```

```python
import functools
import math

import jax
import jax.numpy as jnp
import ml_dtypes
import numpy as np
from jax import lax
from jax.experimental import pallas as pl
from jax.experimental.pallas import tpu as pltpu
from jax.sharding import Mesh
from jax.sharding import PartitionSpec as P

tv_step_size = 1.0 / 12.0
tv_sharpness = 0.25

N = 4096
RADIX = 16
INNER = 256
CLASSES = 9
PLANES = 8
LANES = 128
F32 = jnp.float32
BF16 = jnp.bfloat16

DEPTH = ("x_lo", "y")
ROW = ("x_hi", "z", "core")
LAYER = ("x_lo", "y", "x_hi", "core")


def split_table(table):
    high = table.astype(ml_dtypes.bfloat16)
    low = (table - high.astype(np.float64)).astype(ml_dtypes.bfloat16)
    return high, low


def inner_tables():
    index = np.arange(INNER)
    angle = 2.0 * np.pi * (np.outer(index, index) % INNER) / INNER
    cosine, sine = np.cos(angle), np.sin(angle)
    tables = []
    for sign in (1.0, -1.0):
        whole = np.block([[cosine, -sign * sine], [sign * sine, cosine]])
        high, low = split_table(whole)
        tables.append(np.concatenate([high, high, low], axis=0))
    return tables


def twiddles():
    angle = 2.0 * np.pi * np.outer(np.arange(RADIX), np.arange(INNER)) / N
    return np.stack([np.cos(angle), np.sin(angle)]).astype(np.float32)


def class_frequencies():
    return (RADIX * np.arange(INNER)[None, :] + np.arange(CLASSES)[:, None]) % N


def class_tables():
    freq = class_frequencies()
    angle = 2.0 * np.pi * ((freq[:, None, :] * np.arange(INNER)[None, :, None]) % N) / N
    table = np.concatenate([np.cos(angle), np.sin(angle)], axis=2)
    tables = []
    for each in (table, np.swapaxes(table, 1, 2)):
        high, low = split_table(each)
        tables.append(np.concatenate([high, high, low], axis=1))
    return tables


def squares_of(index):
    centred = np.where(index < N // 2, index, index - N)
    return (centred * centred).astype(np.float32)


def dft4(values, inverse):
    (ar, ai), (br, bi), (cr, ci), (dr, di) = values
    s0r, s0i, s1r, s1i = ar + cr, ai + ci, ar - cr, ai - ci
    s2r, s2i, s3r, s3i = br + dr, bi + di, br - dr, bi - di
    plus = (s1r - s3i, s1i + s3r)
    minus = (s1r + s3i, s1i - s3r)
    first, third = (plus, minus) if inverse else (minus, plus)
    return [(s0r + s2r, s0i + s2i), first, (s0r - s2r, s0i - s2i), third]


def times_constant(value, cosine, sine):
    real, imag = value
    if abs(sine) < 1e-9 and abs(cosine - 1.0) < 1e-9:
        return value
    if abs(cosine) < 1e-9 and abs(sine - 1.0) < 1e-9:
        return (-imag, real)
    if abs(cosine) < 1e-9 and abs(sine + 1.0) < 1e-9:
        return (imag, -real)
    if abs(abs(cosine) - abs(sine)) < 1e-9:
        root = math.sqrt(0.5)
        sc, ss = math.copysign(1.0, cosine), math.copysign(1.0, sine)
        first = (real if sc > 0 else -real) - (imag if ss > 0 else -imag)
        second = (imag if sc > 0 else -imag) + (real if ss > 0 else -real)
        return (first * root, second * root)
    return (real * cosine - imag * sine, imag * cosine + real * sine)


def dft16(values, inverse):
    direction = 1.0 if inverse else -1.0
    stage = [dft4([values[4 * n1 + n2] for n1 in range(4)], inverse) for n2 in range(4)]
    result = [None] * 16
    for k1 in range(4):
        column = []
        for n2 in range(4):
            angle = direction * 2.0 * math.pi * n2 * k1 / 16
            column.append(times_constant(stage[n2][k1], math.cos(angle), math.sin(angle)))
        for k2, value in enumerate(dft4(column, inverse)):
            result[k1 + 4 * k2] = value
    return result


def weighted_sum(terms):
    total = None
    for coefficient, value in terms:
        if abs(coefficient) < 1e-9:
            continue
        if abs(coefficient - 1.0) < 1e-9:
            total = value if total is None else total + value
        elif abs(coefficient + 1.0) < 1e-9:
            total = -value if total is None else total - value
        else:
            piece = value * float(np.float32(coefficient))
            total = piece if total is None else total + piece
    return total


def real_dft16(blocks):
    sums = [blocks[0]] + [blocks[b] + blocks[16 - b] for b in range(1, 8)] + [blocks[8]]
    diffs = [None] + [blocks[b] - blocks[16 - b] for b in range(1, 8)]
    result = []
    for k in range(CLASSES):
        real = weighted_sum([(math.cos(2 * math.pi * k * b / 16), sums[b]) for b in range(9)])
        if k in (0, 8):
            imag = jnp.zeros_like(real)
        else:
            imag = weighted_sum(
                [(-math.sin(2 * math.pi * k * b / 16), diffs[b]) for b in range(1, 8)]
            )
        result.append((real, imag))
    return result


def real_inverse16(values):
    result = [None] * 16
    for b in range(9):
        even = weighted_sum([(math.cos(2 * math.pi * k * b / 16), values[k][0]) for k in range(9)])
        if b in (0, 8):
            result[b] = even
        else:
            odd = weighted_sum(
                [(math.sin(2 * math.pi * k * b / 16), values[k][1]) for k in range(1, 8)]
            )
            result[b] = even - odd
            result[16 - b] = even + odd
    return result


def halves(value):
    high = value.astype(BF16)
    low = (value - high.astype(F32)).astype(BF16)
    return high, low


STEP_ROWS = 32
CHUNK_CLASSES = 16


def filter_rows(load, store, tw_ref, d_ref, wf_ref, wi_ref, x_ref):
    groups = [(r, h) for r in range(STEP_ROWS // 8) for h in range(INNER // LANES)]
    for r, h in groups:
        values = [load(r, b * (INNER // LANES) + h) for b in range(RADIX)]
        lanes = slice(h * LANES, (h + 1) * LANES)
        for k, (real, imag) in enumerate(dft16(values, False)):
            if k:
                cosine, sine = tw_ref[0, k : k + 1, lanes], tw_ref[1, k : k + 1, lanes]
                real, imag = real * cosine + imag * sine, imag * cosine - real * sine
            rows = slice(k * STEP_ROWS + 8 * r, k * STEP_ROWS + 8 * r + 8)
            x_ref[rows, lanes] = real
            x_ref[rows, INNER + h * LANES : INNER + (h + 1) * LANES] = imag
    for chunk in range(RADIX // CHUNK_CLASSES):
        base = chunk * CHUNK_CLASSES * STEP_ROWS
        rows = slice(base, base + CHUNK_CLASSES * STEP_ROWS)
        high, low = halves(x_ref[rows, :])
        spectrum = jnp.dot(
            jnp.concatenate([high, low, high], axis=1), wf_ref[...], preferred_element_type=F32
        )
        pieces = []
        for kk in range(CHUNK_CLASSES):
            k = chunk * CHUNK_CLASSES + kk
            cosine, sine = per_row(d_ref[0, k]), per_row(d_ref[1, k])
            real = spectrum[kk * STEP_ROWS : (kk + 1) * STEP_ROWS, :INNER]
            imag = spectrum[kk * STEP_ROWS : (kk + 1) * STEP_ROWS, INNER:]
            pieces.append(
                jnp.concatenate(
                    [real * cosine - imag * sine, imag * cosine + real * sine], axis=1
                )
            )
        high, low = halves(jnp.concatenate(pieces, axis=0))
        x_ref[rows, :] = jnp.dot(
            jnp.concatenate([high, low, high], axis=1), wi_ref[...], preferred_element_type=F32
        )
    for r, h in groups:
        lanes = slice(h * LANES, (h + 1) * LANES)
        values = []
        for k in range(RADIX):
            rows = slice(k * STEP_ROWS + 8 * r, k * STEP_ROWS + 8 * r + 8)
            real = x_ref[rows, lanes]
            imag = x_ref[rows, INNER + h * LANES : INNER + (h + 1) * LANES]
            if k:
                cosine, sine = tw_ref[0, k : k + 1, lanes], tw_ref[1, k : k + 1, lanes]
                real, imag = real * cosine - imag * sine, imag * cosine + real * sine
            values.append((real, imag))
        for b, value in enumerate(dft16(values, True)):
            store(r, b * (INNER // LANES) + h, value)


def per_row(factor):
    if factor.shape[0] == 1:
        return factor
    return jnp.concatenate([factor] * (STEP_ROWS // factor.shape[0]), axis=0)


def forward_x_kernel(f_ref, hol_ref, tw_ref, d_ref, wf_ref, wi_ref, o_ref, x_ref):
    step = pl.program_id(0)

    @pl.when(step == 0)
    def _():
        for j in range(32):
            o_ref[j, 256:272, :] = hol_ref[:, j * LANES : (j + 1) * LANES]

    def load(r, j):
        rows, lanes = slice(8 * r, 8 * r + 8), slice(j * LANES, (j + 1) * LANES)
        return f_ref[0, rows, lanes], f_ref[1, rows, lanes]

    def store(r, j, value):
        for c in range(2):
            start = pl.multiple_of(step * STEP_ROWS + 128 * c + 8 * r, 8)
            o_ref[j, pl.ds(start, 8), :] = value[c]

    filter_rows(load, store, tw_ref, d_ref, wf_ref, wi_ref, x_ref)


def backward_x_kernel(g_ref, held_ref, tw_ref, d_ref, wf_ref, wi_ref, o_ref, x_ref, f_ref):
    step = pl.program_id(0)

    @pl.when(step == 0)
    def _():
        for c in range(2):
            for p in range(PLANES):
                for j in range(N // LANES):
                    f_ref[c, j, pl.ds(p, 16, stride=PLANES), :] = held_ref[
                        p, c, :, j * LANES : (j + 1) * LANES
                    ]

    def load(r, j):
        rows = slice(8 * r, 8 * r + 8)
        return g_ref[j, 0, rows, :], g_ref[j, 1, rows, :]

    def store(r, j, value):
        rows, lanes = slice(8 * r, 8 * r + 8), slice(j * LANES, (j + 1) * LANES)
        held = pl.ds(pl.multiple_of(step * STEP_ROWS + 8 * r, 8), 8)
        for c in range(2):
            o_ref[c, rows, lanes] = f_ref[c, j, held, :] + value[c]

    filter_rows(load, store, tw_ref, d_ref, wf_ref, wi_ref, x_ref)


def whole(shape):
    return pl.BlockSpec(shape, lambda *_: (0,) * len(shape))


def cost_of(microseconds):
    return pl.CostEstimate(flops=0, bytes_accessed=microseconds * 3_000_000, transcendentals=0)


def params():
    return pltpu.CompilerParams(vmem_limit_bytes=56 << 20)


def x_tables():
    forward, inverse = inner_tables()
    return jnp.asarray(twiddles()), jnp.asarray(forward), jnp.asarray(inverse)


def forward_x(field, hologram_rows, transfer):
    tw, wf, wi = x_tables()
    return pl.pallas_call(
        forward_x_kernel,
        grid=(128 // STEP_ROWS,),
        in_specs=[
            pl.BlockSpec((2, STEP_ROWS, N), lambda i: (0, i, 0)),
            whole((16, N)),
            whole((2, RADIX, INNER)),
            whole((2, RADIX, 1, INNER)),
            whole((1536, 512)),
            whole((1536, 512)),
        ],
        out_specs=whole((32, 272, LANES)),
        out_shape=jax.ShapeDtypeStruct((32, 272, LANES), F32),
        scratch_shapes=[pltpu.VMEM((RADIX * STEP_ROWS, 2 * INNER), F32)],
        compiler_params=params(),
        cost_estimate=cost_of(14),
        name="filter_x_forward",
    )(field, hologram_rows, tw, transfer, wf, wi)


def backward_x(gradient, held, transfer):
    tw, wf, wi = x_tables()
    return pl.pallas_call(
        backward_x_kernel,
        grid=(128 // STEP_ROWS,),
        in_specs=[
            pl.BlockSpec((32, 2, STEP_ROWS, LANES), lambda i: (0, 0, i, 0)),
            whole((PLANES, 2, 16, N)),
            whole((2, RADIX, INNER)),
            whole((2, RADIX, PLANES, INNER)),
            whole((1536, 512)),
            whole((1536, 512)),
        ],
        out_specs=pl.BlockSpec((2, STEP_ROWS, N), lambda i: (0, i, 0)),
        out_shape=jax.ShapeDtypeStruct((2, 128, N), F32),
        scratch_shapes=[
            pltpu.VMEM((RADIX * STEP_ROWS, 2 * INNER), F32),
            pltpu.VMEM((2, N // LANES, 128, LANES), F32),
        ],
        compiler_params=params(),
        cost_estimate=cost_of(16),
        name="filter_x_backward",
    )(gradient, held, tw, transfer, wf, wi)


def forward_y_kernel(z_ref, g_ref, t_ref, tt_ref, cs_ref, o_ref, h_ref, u_ref, s_ref):
    step = pl.program_id(0)

    @pl.when(step == 0)
    def _():
        @pl.loop(0, PLANES)
        def _(p):
            for core in range(2):
                for c in range(2):
                    rows = slice(c * 128, (c + 1) * 128)
                    upper = g_ref[p * 4 + core, rows, :].T
                    lower = g_ref[p * 4 + 2 + core, rows, :].T
                    for parity, value in ((0, upper + lower), (1, upper - lower)):
                        high, low = halves(value)
                        for part, piece in ((0, high), (1, low), (2, high)):
                            start = part * INNER + core * 128
                            u_ref[parity, p, c * LANES : (c + 1) * LANES, start : start + 128] = (
                                piece
                            )

        for upper in range(2):
            for core in range(2):
                rows = [g_ref[p * 4 + upper * 2 + core, 256:, :] for p in range(PLANES)]
                block = jnp.concatenate(rows, axis=0).T
                h_ref[0, upper, :, core * 128 : (core + 1) * 128] = block

    parity = lax.rem(step, 2)
    total = None
    for p in range(PLANES):
        result = jnp.dot(u_ref[parity, p], t_ref[0], preferred_element_type=F32)
        piece = (
            cs_ref[0, 2 * p : 2 * p + 1, :] * result[:LANES]
            + cs_ref[0, 2 * p + 1 : 2 * p + 2, :] * result[LANES:]
        )
        total = piece if total is None else total + piece
    turned = jnp.concatenate([-total[:, INNER:], total[:, :INNER]], axis=1)
    high, low = halves(jnp.concatenate([total, turned], axis=0))
    s_ref[step] = jnp.dot(
        jnp.concatenate([high, low, high], axis=1), tt_ref[0], preferred_element_type=F32
    )

    @pl.when(step == CLASSES - 1)
    def _():
        shift = z_ref[0]

        @pl.loop(0, LANES // 8)
        def _(i):
            rows = pl.ds(pl.multiple_of(i * 8, 8), 8)
            other = pl.ds(pl.multiple_of(LANES + i * 8, 8), 8)
            for half in range(2):
                lanes = slice(half * LANES, (half + 1) * LANES)
                values = [(s_ref[k, rows, lanes], s_ref[k, other, lanes]) for k in range(CLASSES)]
                for b, value in enumerate(real_inverse16(values)):
                    block = lax.rem(shift + b, 16)
                    o_ref[lax.rem(block, 8), lax.div(block, 8), rows, lanes] = value


def forward_y(z_index, received, factors):
    forward, backward = class_tables()
    return pl.pallas_call(
        forward_y_kernel,
        grid=(CLASSES,),
        in_specs=[
            pl.BlockSpec(memory_space=pltpu.SMEM),
            whole((32, 272, LANES)),
            pl.BlockSpec((1, 768, 512), lambda k: (k, 0, 0)),
            pl.BlockSpec((1, 1536, 256), lambda k: (k, 0, 0)),
            pl.BlockSpec((1, 16, 512), lambda k: (k, 0, 0)),
        ],
        out_specs=[whole((8, 2, LANES, INNER)), whole((1, 2, LANES, INNER))],
        out_shape=[
            jax.ShapeDtypeStruct((8, 2, LANES, INNER), F32),
            jax.ShapeDtypeStruct((1, 2, LANES, INNER), F32),
        ],
        scratch_shapes=[
            pltpu.VMEM((2, PLANES, 2 * LANES, 768), BF16),
            pltpu.VMEM((CLASSES, 2 * LANES, INNER), F32),
        ],
        compiler_params=params(),
        cost_estimate=cost_of(32),
        name="filter_y_forward",
    )(z_index, received, jnp.asarray(forward), jnp.asarray(backward), factors)


def backward_y_kernel(z_ref, m_ref, t_ref, tt_ref, cs_ref, o_ref, x_ref, a_ref):
    step = pl.program_id(0)

    @pl.when(step == 0)
    def _():
        shift = z_ref[0]

        @pl.loop(0, LANES // 8)
        def _(i):
            rows = pl.ds(pl.multiple_of(i * 8, 8), 8)
            other = pl.ds(pl.multiple_of(LANES + i * 8, 8), 8)
            for half in range(2):
                lanes = slice(half * LANES, (half + 1) * LANES)
                blocks = []
                for b in range(16):
                    block = lax.rem(shift + b, 16)
                    blocks.append(m_ref[lax.rem(block, 8), lax.div(block, 8), rows, lanes])
                for k, (real, imag) in enumerate(real_dft16(blocks)):
                    x_ref[k, rows, lanes] = real
                    x_ref[k, other, lanes] = imag

        @pl.loop(0, PLANES)
        def _(p):
            for parity in range(2):
                a_ref[parity, p] = jnp.zeros((2 * LANES, INNER), F32)

    parity = lax.rem(step, 2)
    high, low = halves(x_ref[step])
    mixed = jnp.dot(
        jnp.concatenate([high, low, high], axis=1), t_ref[0], preferred_element_type=F32
    )
    cosine = mixed[:LANES, :INNER] + mixed[LANES:, INNER:]
    sine = mixed[:LANES, INNER:] - mixed[LANES:, :INNER]
    spectrum = jnp.concatenate([cosine, sine], axis=1)
    for p in range(PLANES):
        product = jnp.concatenate(
            [
                cs_ref[0, 2 * p : 2 * p + 1, :] * spectrum,
                cs_ref[0, 2 * p + 1 : 2 * p + 2, :] * spectrum,
            ],
            axis=0,
        )
        high, low = halves(product)
        a_ref[parity, p] += jnp.dot(
            jnp.concatenate([high, low, high], axis=1), tt_ref[0], preferred_element_type=F32
        )

    @pl.when(step == CLASSES - 1)
    def _():
        @pl.loop(0, PLANES)
        def _(p):
            for core in range(2):
                lanes = slice(core * 128, (core + 1) * 128)
                for c in range(2):
                    rows = slice(c * LANES, (c + 1) * LANES)
                    even, odd = a_ref[0, p, rows, lanes], a_ref[1, p, rows, lanes]
                    upper, lower = (even + odd).T, (even - odd).T
                    for owner in range(PLANES):
                        part = slice(owner * 16, owner * 16 + 16)
                        held = pl.ds(p, 16, stride=PLANES)
                        o_ref[owner * 4 + core, c, held, :] = upper[part]
                        o_ref[owner * 4 + 2 + core, c, held, :] = lower[part]


def backward_y(z_index, misfit, factors):
    forward, backward = class_tables()
    return pl.pallas_call(
        backward_y_kernel,
        grid=(CLASSES,),
        in_specs=[
            pl.BlockSpec(memory_space=pltpu.SMEM),
            whole((8, 2, LANES, INNER)),
            pl.BlockSpec((1, 768, 512), lambda k: (k, 0, 0)),
            pl.BlockSpec((1, 1536, 256), lambda k: (k, 0, 0)),
            pl.BlockSpec((1, 16, 512), lambda k: (k, 0, 0)),
        ],
        out_specs=whole((32, 2, 128, LANES)),
        out_shape=jax.ShapeDtypeStruct((32, 2, 128, LANES), F32),
        scratch_shapes=[
            pltpu.VMEM((CLASSES, 2 * LANES, INNER), F32),
            pltpu.VMEM((2, PLANES, 2 * LANES, INNER), F32),
        ],
        compiler_params=params(),
        cost_estimate=cost_of(30),
        name="filter_y_backward",
    )(z_index, misfit, jnp.asarray(forward), jnp.asarray(backward), factors)


SUBS = 2
LAYERS = 8


def z_exchange_kernel(p_ref, h_ref, o_ref, r_ref, sum_send, sum_recv, all_send, all_recv):
    me = lax.axis_index("z")
    at = lambda distance: lax.rem(me + distance + 2 * LAYERS, LAYERS)
    right, left = at(1), at(-1)
    barrier = pltpu.get_barrier_semaphore()
    for neighbour in (left, right):
        pl.semaphore_signal(
            barrier,
            inc=1,
            device_id={"z": neighbour},
            device_id_type=pl.DeviceIdType.MESH,
        )
    pl.semaphore_wait(barrier, 2)

    size = LANES // SUBS
    rings = [(way, sub) for sub in range(SUBS) for way in range(2)]

    def send(source, target, send_sem, recv_sem, way):
        return pltpu.make_async_remote_copy(
            src_ref=source,
            dst_ref=target,
            send_sem=send_sem,
            recv_sem=recv_sem,
            device_id={"z": (right, left)[way]},
            device_id_type=pl.DeviceIdType.MESH,
        )

    started, arrived = [], {}
    for step in range(LAYERS):
        for way, sub in rings:
            rows = slice(sub * size, (sub + 1) * size)
            block = at((-1 - step) if way == 0 else (1 + step))
            slot = r_ref.at[way, sub]
            if step:
                arrived[way, sub].wait_recv()
                if step < LAYERS - 1:
                    r_ref[way, sub, step - 1] += p_ref[block, way, rows, :]
                else:
                    o_ref[me, way, rows, :] = (
                        r_ref[way, sub, step - 1] + p_ref[me, way, rows, :]
                    ) - h_ref[0, way, rows, :]
            if step < LAYERS - 1:
                source = p_ref.at[block, way, rows, :] if step == 0 else slot.at[step - 1]
                copy = send(
                    source,
                    slot.at[step],
                    sum_send.at[way, sub, step],
                    sum_recv.at[way, sub, step],
                    way,
                )
                copy.start()
                started.append(copy)
                arrived[way, sub] = copy
            else:
                place = o_ref.at[me, way, rows, :]
                copy = send(
                    place, place, all_send.at[way, sub, 0], all_recv.at[way, sub, 0], way
                )
                copy.start()
                started.append(copy)
                arrived[way, sub] = copy
    for step in range(1, LAYERS):
        for way, sub in rings:
            rows = slice(sub * size, (sub + 1) * size)
            arrived[way, sub].wait_recv()
            if step < LAYERS - 1:
                place = o_ref.at[at(-step if way == 0 else step), way, rows, :]
                copy = send(
                    place, place, all_send.at[way, sub, step], all_recv.at[way, sub, step], way
                )
                copy.start()
                started.append(copy)
                arrived[way, sub] = copy
    for copy in started:
        copy.wait_send()


def z_exchange(partial, tile):
    steps = LAYERS - 1
    vmem = pl.BlockSpec(memory_space=pltpu.VMEM)
    return pl.pallas_call(
        z_exchange_kernel,
        in_specs=[vmem, vmem],
        out_specs=vmem,
        out_shape=jax.ShapeDtypeStruct((LAYERS, 2, LANES, INNER), F32),
        scratch_shapes=[
            pltpu.VMEM((2, SUBS, steps, LANES // SUBS, INNER), F32),
            pltpu.SemaphoreType.DMA((2, SUBS, steps)),
            pltpu.SemaphoreType.DMA((2, SUBS, steps)),
            pltpu.SemaphoreType.DMA((2, SUBS, steps)),
            pltpu.SemaphoreType.DMA((2, SUBS, steps)),
        ],
        compiler_params=pltpu.CompilerParams(
            collective_id=0, has_side_effects=True, vmem_limit_bytes=32 << 20
        ),
        cost_estimate=cost_of(50),
        name="z_exchange",
    )(partial, tile)


TV_ROWS = 8


def shrink_kernel(edge_ref, m_ref, next_ref, above_ref, below_ref, o_ref, e_ref, prior_ref):
    step = pl.program_id(0)
    plane = lax.broadcasted_iota(jnp.int32, (PLANES, N), 0)
    column = lax.broadcasted_iota(jnp.int32, (PLANES, N), 1)
    last_plane, first_plane = plane == PLANES - 1, plane == 0
    last_column, first_column = column == N - 1, column == 0

    def flux(here, below):
        squares = None
        diffs = []
        for c in range(2):
            depth = jnp.where(last_plane, 0.0, pltpu.roll(here[c], PLANES - 1, 0) - here[c])
            row = below[c] - here[c]
            col = jnp.where(last_column, 0.0, pltpu.roll(here[c], N - 1, 1) - here[c])
            diffs.append((depth, row, col))
            term = depth * depth + row * row + col * col
            squares = term if squares is None else squares + term
        factor = 1.0 / (1.0 + tv_sharpness * jnp.sqrt(squares))
        return [tuple(d * factor for d in triple) for triple in diffs]

    @pl.when(step == 0)
    def _():
        above = [above_ref[c] for c in range(2)]
        first = [m_ref[c, :PLANES, :] for c in range(2)]
        terms = flux(above, first)
        for c in range(2):
            prior_ref[c] = jnp.where(edge_ref[0] > 0, terms[c][1], 0.0)

    def row_at(t):
        rows = pl.ds(pl.multiple_of(t * PLANES, PLANES), PLANES)
        return [m_ref[c, rows, :] for c in range(2)]

    def emit(t, here, below):
        terms = flux(here, below)
        rows = pl.ds(pl.multiple_of(t * PLANES, PLANES), PLANES)
        for c in range(2):
            depth, row, col = terms[c]
            divergence = (
                (depth - jnp.where(first_plane, 0.0, pltpu.roll(depth, 1, 0)))
                + (row - prior_ref[c])
                + (col - jnp.where(first_column, 0.0, pltpu.roll(col, 1, 1)))
            )
            prior_ref[c] = row
            estimate = here[c] + tv_step_size * divergence
            for j in range(N // LANES):
                e_ref[c, j, rows, :] = estimate[:, j * LANES : (j + 1) * LANES]

    @pl.loop(0, TV_ROWS - 1)
    def _(t):
        emit(t, row_at(t), row_at(t + 1))

    here = row_at(TV_ROWS - 1)
    final = step == 16 // TV_ROWS - 1
    below = []
    for c in range(2):
        beyond = jnp.where(edge_ref[1] > 0, below_ref[c], here[c])
        below.append(jnp.where(final, beyond, next_ref[c]))
    emit(TV_ROWS - 1, here, below)
    for p in range(PLANES):
        for c in range(2):
            for j in range(N // LANES):
                held = pl.ds(p, TV_ROWS, stride=PLANES)
                o_ref[p, c, :, j * LANES : (j + 1) * LANES] = e_ref[c, j, held, :]


def shrink(edges, moved, above, below):
    steps = 16 // TV_ROWS
    return pl.pallas_call(
        shrink_kernel,
        grid=(steps,),
        in_specs=[
            pl.BlockSpec(memory_space=pltpu.SMEM),
            pl.BlockSpec((2, TV_ROWS * PLANES, N), lambda i: (0, i, 0)),
            pl.BlockSpec((2, PLANES, N), lambda i: (0, jnp.minimum((i + 1) * TV_ROWS, 15), 0)),
            whole((2, PLANES, N)),
            whole((2, PLANES, N)),
        ],
        out_specs=pl.BlockSpec((PLANES, 2, TV_ROWS, N), lambda i: (0, 0, i, 0)),
        out_shape=jax.ShapeDtypeStruct((PLANES, 2, 16, N), F32),
        scratch_shapes=[
            pltpu.VMEM((2, N // LANES, TV_ROWS * PLANES, LANES), F32),
            pltpu.VMEM((2, PLANES, N), F32),
        ],
        compiler_params=params(),
        cost_estimate=cost_of(9),
        name="tv_shrink",
    )(edges, moved, moved, above, below)


def along_rows(block, distance):
    place = lambda line: (line % 8) * 32 + line // 8
    route = [
        (place(line - distance), place(line)) for line in range(256) if 0 <= line - distance < 256
    ]
    return lax.ppermute(block, DEPTH + ROW, route)


def phase_of(depth_values, squares):
    return depth_values * (squares * (math.pi / (N * N)))


def per_device(field, hologram, defocus):
    x_lo, y = lax.axis_index("x_lo"), lax.axis_index("y")
    x_hi, z, core = lax.axis_index("x_hi"), lax.axis_index("z"), lax.axis_index("core")
    depth_index = x_lo * 4 + y
    row_index = x_hi * 16 + z * 2 + core
    z_index = z[None].astype(jnp.int32)
    field = field[:, 0]

    x_freq = RADIX * np.arange(INNER)[None, :] + np.arange(RADIX)[:, None]
    x_squares = jnp.asarray(squares_of(x_freq))[:, None, :]
    x_phase = phase_of(defocus[0], x_squares)
    x_forward = jnp.stack([jnp.cos(x_phase) / N, -jnp.sin(x_phase) / N])

    depths = lax.all_gather(defocus, DEPTH, tiled=True)
    x_phase = phase_of(depths[None, :, None], x_squares)
    x_backward = jnp.stack([jnp.cos(x_phase), jnp.sin(x_phase)]) * (-1.0 / (PLANES * N))
    y_squares = jnp.asarray(squares_of(class_frequencies()))[:, None, None, :]
    y_phase = phase_of(depths[None, :, None, None], y_squares)
    weights = np.full((CLASSES, 1, 1, 1), 2.0 / N, np.float32)
    weights[0] = weights[8] = 1.0 / N
    factors = jnp.concatenate([jnp.cos(y_phase), jnp.sin(y_phase)], axis=2) * weights
    factors = factors.reshape(CLASSES, 2 * PLANES, INNER)
    factors = jnp.concatenate([factors, factors], axis=2)

    hologram_rows = lax.dynamic_slice_in_dim(hologram, depth_index * 16, 16, 0)
    sent = forward_x(field, hologram_rows, x_forward)
    received = lax.all_to_all(sent, LAYER, 0, 0, tiled=True)
    partial, tile = forward_y(z_index, received, factors)
    field, partial = lax.optimization_barrier((field, partial))
    held = jnp.transpose(field.reshape(2, PLANES, 16, N), (1, 0, 2, 3))
    held = lax.all_to_all(held, DEPTH, 0, 0, tiled=True)
    misfit = z_exchange(partial, tile)
    sent = backward_y(z_index, misfit, factors)
    received = lax.all_to_all(sent, LAYER, 0, 0, tiled=True)
    moved = backward_x(received, held, x_backward)
    above = along_rows(moved[:, 120:], 1)
    below = along_rows(moved[:, :8], -1)
    line = row_index * 8 + depth_index
    edges = jnp.stack([line > 0, line < 255]).astype(jnp.int32)
    estimate = shrink(edges, moved, above, below)
    estimate = lax.all_to_all(estimate, DEPTH, 0, 0, tiled=True)
    return jnp.transpose(estimate, (1, 0, 2, 3)).reshape(2, 1, 128, N)


def solution(mesh):
    fine = Mesh(mesh.devices.reshape(2, 4, 2, 8, 2), DEPTH + ROW)
    return jax.shard_map(
        per_device,
        mesh=fine,
        in_specs=(P(None, DEPTH, ROW, None), P(ROW, None), P(DEPTH)),
        out_specs=P(None, DEPTH, ROW, None),
        check_vma=False,
    )
```

```python
import functools
import math

import jax
import jax.numpy as jnp
import ml_dtypes
import numpy as np
from jax import lax
from jax.experimental import pallas as pl
from jax.experimental.pallas import tpu as pltpu
from jax.sharding import Mesh
from jax.sharding import PartitionSpec as P

tv_step_size = 1.0 / 12.0
tv_sharpness = 0.25

N = 4096
RADIX = 16
INNER = 256
CLASSES = 9
PLANES = 8
LANES = 128
F32 = jnp.float32
BF16 = jnp.bfloat16

DEPTH = ("x_lo", "y")
ROW = ("x_hi", "z", "core")
LAYER = ("x_lo", "y", "x_hi", "core")


def split_table(table):
    high = table.astype(ml_dtypes.bfloat16)
    low = (table - high.astype(np.float64)).astype(ml_dtypes.bfloat16)
    return high, low


def inner_tables():
    index = np.arange(INNER)
    angle = 2.0 * np.pi * (np.outer(index, index) % INNER) / INNER
    cosine, sine = np.cos(angle), np.sin(angle)
    tables = []
    for sign in (1.0, -1.0):
        whole = np.block([[cosine, -sign * sine], [sign * sine, cosine]])
        high, low = split_table(whole)
        tables.append(np.concatenate([high, high, low], axis=0))
    return tables


def twiddles():
    angle = 2.0 * np.pi * np.outer(np.arange(RADIX), np.arange(INNER)) / N
    return np.stack([np.cos(angle), np.sin(angle)]).astype(np.float32)


def class_frequencies():
    return (RADIX * np.arange(INNER)[None, :] + np.arange(CLASSES)[:, None]) % N


def class_tables():
    freq = class_frequencies()
    angle = 2.0 * np.pi * ((freq[:, None, :] * np.arange(INNER)[None, :, None]) % N) / N
    table = np.concatenate([np.cos(angle), np.sin(angle)], axis=2)
    tables = []
    for each in (table, np.swapaxes(table, 1, 2)):
        high, low = split_table(each)
        tables.append(np.concatenate([high, high, low], axis=1))
    return tables


def squares_of(index):
    centred = np.where(index < N // 2, index, index - N)
    return (centred * centred).astype(np.float32)


def dft4(values, inverse):
    (ar, ai), (br, bi), (cr, ci), (dr, di) = values
    s0r, s0i, s1r, s1i = ar + cr, ai + ci, ar - cr, ai - ci
    s2r, s2i, s3r, s3i = br + dr, bi + di, br - dr, bi - di
    plus = (s1r - s3i, s1i + s3r)
    minus = (s1r + s3i, s1i - s3r)
    first, third = (plus, minus) if inverse else (minus, plus)
    return [(s0r + s2r, s0i + s2i), first, (s0r - s2r, s0i - s2i), third]


def times_constant(value, cosine, sine):
    real, imag = value
    if abs(sine) < 1e-9 and abs(cosine - 1.0) < 1e-9:
        return value
    if abs(cosine) < 1e-9 and abs(sine - 1.0) < 1e-9:
        return (-imag, real)
    if abs(cosine) < 1e-9 and abs(sine + 1.0) < 1e-9:
        return (imag, -real)
    if abs(abs(cosine) - abs(sine)) < 1e-9:
        root = math.sqrt(0.5)
        sc, ss = math.copysign(1.0, cosine), math.copysign(1.0, sine)
        first = (real if sc > 0 else -real) - (imag if ss > 0 else -imag)
        second = (imag if sc > 0 else -imag) + (real if ss > 0 else -real)
        return (first * root, second * root)
    return (real * cosine - imag * sine, imag * cosine + real * sine)


def dft16(values, inverse):
    direction = 1.0 if inverse else -1.0
    stage = [dft4([values[4 * n1 + n2] for n1 in range(4)], inverse) for n2 in range(4)]
    result = [None] * 16
    for k1 in range(4):
        column = []
        for n2 in range(4):
            angle = direction * 2.0 * math.pi * n2 * k1 / 16
            column.append(times_constant(stage[n2][k1], math.cos(angle), math.sin(angle)))
        for k2, value in enumerate(dft4(column, inverse)):
            result[k1 + 4 * k2] = value
    return result


def weighted_sum(terms):
    total = None
    for coefficient, value in terms:
        if abs(coefficient) < 1e-9:
            continue
        if abs(coefficient - 1.0) < 1e-9:
            total = value if total is None else total + value
        elif abs(coefficient + 1.0) < 1e-9:
            total = -value if total is None else total - value
        else:
            piece = value * float(np.float32(coefficient))
            total = piece if total is None else total + piece
    return total


def real_dft16(blocks):
    sums = [blocks[0]] + [blocks[b] + blocks[16 - b] for b in range(1, 8)] + [blocks[8]]
    diffs = [None] + [blocks[b] - blocks[16 - b] for b in range(1, 8)]
    result = []
    for k in range(CLASSES):
        real = weighted_sum([(math.cos(2 * math.pi * k * b / 16), sums[b]) for b in range(9)])
        if k in (0, 8):
            imag = jnp.zeros_like(real)
        else:
            imag = weighted_sum(
                [(-math.sin(2 * math.pi * k * b / 16), diffs[b]) for b in range(1, 8)]
            )
        result.append((real, imag))
    return result


def real_inverse16(values):
    result = [None] * 16
    for b in range(9):
        even = weighted_sum([(math.cos(2 * math.pi * k * b / 16), values[k][0]) for k in range(9)])
        if b in (0, 8):
            result[b] = even
        else:
            odd = weighted_sum(
                [(math.sin(2 * math.pi * k * b / 16), values[k][1]) for k in range(1, 8)]
            )
            result[b] = even - odd
            result[16 - b] = even + odd
    return result


def halves(value):
    high = value.astype(BF16)
    low = (value - high.astype(F32)).astype(BF16)
    return high, low


STEP_ROWS = 32
CHUNK_CLASSES = 16


def filter_rows(load, store, tw_ref, d_ref, wf_ref, wi_ref, x_ref):
    groups = [(r, h) for r in range(STEP_ROWS // 8) for h in range(INNER // LANES)]
    for r, h in groups:
        values = [load(r, b * (INNER // LANES) + h) for b in range(RADIX)]
        lanes = slice(h * LANES, (h + 1) * LANES)
        for k, (real, imag) in enumerate(dft16(values, False)):
            if k:
                cosine, sine = tw_ref[0, k : k + 1, lanes], tw_ref[1, k : k + 1, lanes]
                real, imag = real * cosine + imag * sine, imag * cosine - real * sine
            rows = slice(k * STEP_ROWS + 8 * r, k * STEP_ROWS + 8 * r + 8)
            x_ref[rows, lanes] = real
            x_ref[rows, INNER + h * LANES : INNER + (h + 1) * LANES] = imag
    for chunk in range(RADIX // CHUNK_CLASSES):
        base = chunk * CHUNK_CLASSES * STEP_ROWS
        rows = slice(base, base + CHUNK_CLASSES * STEP_ROWS)
        high, low = halves(x_ref[rows, :])
        spectrum = jnp.dot(
            jnp.concatenate([high, low, high], axis=1), wf_ref[...], preferred_element_type=F32
        )
        pieces = []
        for kk in range(CHUNK_CLASSES):
            k = chunk * CHUNK_CLASSES + kk
            cosine, sine = per_row(d_ref[0, k]), per_row(d_ref[1, k])
            real = spectrum[kk * STEP_ROWS : (kk + 1) * STEP_ROWS, :INNER]
            imag = spectrum[kk * STEP_ROWS : (kk + 1) * STEP_ROWS, INNER:]
            pieces.append(
                jnp.concatenate(
                    [real * cosine - imag * sine, imag * cosine + real * sine], axis=1
                )
            )
        high, low = halves(jnp.concatenate(pieces, axis=0))
        x_ref[rows, :] = jnp.dot(
            jnp.concatenate([high, low, high], axis=1), wi_ref[...], preferred_element_type=F32
        )
    for r, h in groups:
        lanes = slice(h * LANES, (h + 1) * LANES)
        values = []
        for k in range(RADIX):
            rows = slice(k * STEP_ROWS + 8 * r, k * STEP_ROWS + 8 * r + 8)
            real = x_ref[rows, lanes]
            imag = x_ref[rows, INNER + h * LANES : INNER + (h + 1) * LANES]
            if k:
                cosine, sine = tw_ref[0, k : k + 1, lanes], tw_ref[1, k : k + 1, lanes]
                real, imag = real * cosine - imag * sine, imag * cosine + real * sine
            values.append((real, imag))
        for b, value in enumerate(dft16(values, True)):
            store(r, b * (INNER // LANES) + h, value)


def per_row(factor):
    if factor.shape[0] == 1:
        return factor
    return jnp.concatenate([factor] * (STEP_ROWS // factor.shape[0]), axis=0)


def forward_x_kernel(f_ref, hol_ref, tw_ref, d_ref, wf_ref, wi_ref, o_ref, x_ref):
    step = pl.program_id(0)

    @pl.when(step == 0)
    def _():
        for j in range(32):
            o_ref[j, 256:272, :] = hol_ref[:, j * LANES : (j + 1) * LANES]

    def load(r, j):
        rows, lanes = slice(8 * r, 8 * r + 8), slice(j * LANES, (j + 1) * LANES)
        return f_ref[0, rows, lanes], f_ref[1, rows, lanes]

    def store(r, j, value):
        for c in range(2):
            start = pl.multiple_of(step * STEP_ROWS + 128 * c + 8 * r, 8)
            o_ref[j, pl.ds(start, 8), :] = value[c]

    filter_rows(load, store, tw_ref, d_ref, wf_ref, wi_ref, x_ref)


def backward_x_kernel(g_ref, held_ref, tw_ref, d_ref, wf_ref, wi_ref, o_ref, x_ref, f_ref):
    step = pl.program_id(0)

    @pl.when(step == 0)
    def _():
        for c in range(2):
            for p in range(PLANES):
                for j in range(N // LANES):
                    f_ref[c, j, pl.ds(p, 16, stride=PLANES), :] = held_ref[
                        p, c, :, j * LANES : (j + 1) * LANES
                    ]

    def load(r, j):
        rows = slice(8 * r, 8 * r + 8)
        return g_ref[j, 0, rows, :], g_ref[j, 1, rows, :]

    def store(r, j, value):
        rows, lanes = slice(8 * r, 8 * r + 8), slice(j * LANES, (j + 1) * LANES)
        held = pl.ds(pl.multiple_of(step * STEP_ROWS + 8 * r, 8), 8)
        for c in range(2):
            o_ref[c, rows, lanes] = f_ref[c, j, held, :] + value[c]

    filter_rows(load, store, tw_ref, d_ref, wf_ref, wi_ref, x_ref)


def whole(shape):
    return pl.BlockSpec(shape, lambda *_: (0,) * len(shape))


def cost_of(microseconds):
    return pl.CostEstimate(flops=0, bytes_accessed=microseconds * 3_000_000, transcendentals=0)


def params():
    return pltpu.CompilerParams(vmem_limit_bytes=56 << 20)


def x_tables():
    forward, inverse = inner_tables()
    return jnp.asarray(twiddles()), jnp.asarray(forward), jnp.asarray(inverse)


def forward_x(field, hologram_rows, transfer):
    tw, wf, wi = x_tables()
    return pl.pallas_call(
        forward_x_kernel,
        grid=(128 // STEP_ROWS,),
        in_specs=[
            pl.BlockSpec((2, STEP_ROWS, N), lambda i: (0, i, 0)),
            whole((16, N)),
            whole((2, RADIX, INNER)),
            whole((2, RADIX, 1, INNER)),
            whole((1536, 512)),
            whole((1536, 512)),
        ],
        out_specs=whole((32, 272, LANES)),
        out_shape=jax.ShapeDtypeStruct((32, 272, LANES), F32),
        scratch_shapes=[pltpu.VMEM((RADIX * STEP_ROWS, 2 * INNER), F32)],
        compiler_params=params(),
        cost_estimate=cost_of(14),
        name="filter_x_forward",
    )(field, hologram_rows, tw, transfer, wf, wi)


def backward_x(gradient, held, transfer):
    tw, wf, wi = x_tables()
    return pl.pallas_call(
        backward_x_kernel,
        grid=(128 // STEP_ROWS,),
        in_specs=[
            pl.BlockSpec((32, 2, STEP_ROWS, LANES), lambda i: (0, 0, i, 0)),
            whole((PLANES, 2, 16, N)),
            whole((2, RADIX, INNER)),
            whole((2, RADIX, PLANES, INNER)),
            whole((1536, 512)),
            whole((1536, 512)),
        ],
        out_specs=pl.BlockSpec((2, STEP_ROWS, N), lambda i: (0, i, 0)),
        out_shape=jax.ShapeDtypeStruct((2, 128, N), F32),
        scratch_shapes=[
            pltpu.VMEM((RADIX * STEP_ROWS, 2 * INNER), F32),
            pltpu.VMEM((2, N // LANES, 128, LANES), F32),
        ],
        compiler_params=params(),
        cost_estimate=cost_of(16),
        name="filter_x_backward",
    )(gradient, held, tw, transfer, wf, wi)


LAYERS = 8
PART = LANES // LAYERS
REDUCE_HOPS = LAYERS - 1
HOPS = 2 * (LAYERS - 1)


def filter_y_kernel(
    rot_ref, g_ref, t_ref, tt_ref, cs_ref, o_ref, u_ref, s_ref, h_ref, r_ref, a_ref, send_sem, recv_sem
):
    step = pl.program_id(0)
    me = lax.axis_index("z")

    def hop(k, h):
        odd = lax.rem(k, 2)
        sign = 1 - 2 * odd

        def block(distance):
            index = lax.rem(me + sign * distance + 2 * LAYERS, LAYERS)
            return pl.ds(pl.multiple_of(index * PART, PART), PART)

        def copy(source, target, h):
            return pltpu.make_async_remote_copy(
                src_ref=source,
                dst_ref=target,
                send_sem=send_sem.at[k],
                recv_sem=recv_sem.at[k, h],
                device_id={"z": lax.rem(me + sign + LAYERS, LAYERS)},
                device_id_type=pl.DeviceIdType.MESH,
            )

        own = block(0)

        @pl.when(h > 0)
        def _():
            last = copy(s_ref.at[k, own, :], r_ref.at[k, 0], h - 1)
            last.wait_send()
            last.wait_recv()

        @pl.when(h < REDUCE_HOPS)
        def _():
            rows = block(-1 - h)

            @pl.when(h > 0)
            def _():
                s_ref[k, rows, :] += r_ref[k, h - 1]

            copy(s_ref.at[k, rows, :], r_ref.at[k, h], h).start()

        @pl.when(h == REDUCE_HOPS)
        def _():
            h_ref[k, own, :] = s_ref[k, own, :] + r_ref[k, REDUCE_HOPS - 1]

        @pl.when((h >= REDUCE_HOPS) & (h < HOPS))
        def _():
            rows = block(REDUCE_HOPS - h)
            copy(h_ref.at[k, rows, :], h_ref.at[k, rows, :], h).start()

    def progress(slot):
        @pl.loop(0, CLASSES)
        def _(k):
            h = slot - (2 * k + 1)

            @pl.when((h >= 0) & (h <= HOPS))
            def _():
                hop(k, h)

    @pl.when(step == 0)
    def _():
        barrier = pltpu.get_barrier_semaphore()
        for distance in (1, LAYERS - 1):
            pl.semaphore_signal(
                barrier,
                inc=1,
                device_id={"z": lax.rem(me + distance, LAYERS)},
                device_id_type=pl.DeviceIdType.MESH,
            )
        pl.semaphore_wait(barrier, 2)

        def place(p, lanes, core, upper, lower):
            for parity, value in ((0, upper + lower), (1, upper - lower)):
                high, low = halves(value)
                for part, piece in ((0, high), (1, low), (2, high)):
                    start = part * INNER + core * 128
                    u_ref[parity, p, lanes, start : start + 128] = piece

        @pl.loop(0, PLANES)
        def _(p):
            for core in range(2):
                for c in range(2):
                    rows = slice(c * 128, (c + 1) * 128)
                    upper = g_ref[p * 4 + core, rows, :].T
                    lower = g_ref[p * 4 + 2 + core, rows, :].T
                    place(p, slice(c * LANES, (c + 1) * LANES), core, upper, lower)

        for core in range(2):
            tiles = []
            for upper in range(2):
                rows = [g_ref[p * 4 + upper * 2 + core, 256:, :] for p in range(PLANES)]
                tiles.append(jnp.concatenate(rows, axis=0).T)
            place(PLANES, slice(0, LANES), core, tiles[0], tiles[1])

    @pl.when(step < CLASSES)
    def _():
        parity = lax.rem(step, 2)

        def planes(first, total):
            for p in range(first, first + PLANES // 2):
                result = jnp.dot(u_ref[parity, p], t_ref[0], preferred_element_type=F32)
                total = (
                    total
                    + cs_ref[0, 2 * p : 2 * p + 1, :] * result[:LANES]
                    + cs_ref[0, 2 * p + 1 : 2 * p + 2, :] * result[LANES:]
                )
            return total

        minus = jnp.dot(u_ref[parity, PLANES, :LANES, :], t_ref[0], preferred_element_type=F32)
        s_ref[step] = planes(0, -minus)
        progress(2 * step)
        total = planes(PLANES // 2, s_ref[step])
        cosine, sine = rot_ref[step, 0], rot_ref[step, 1]
        real, imag = total[:, :INNER], total[:, INNER:]
        s_ref[step, :, :INNER] = cosine * real - sine * imag
        s_ref[step, :, INNER:] = cosine * imag + sine * real
        progress(2 * step + 1)

    @pl.when(step >= CLASSES)
    def _():
        k = step - CLASSES
        parity = lax.rem(k, 2)
        cosine, sine = rot_ref[k, 2], rot_ref[k, 3]
        real, imag = h_ref[k, :, :INNER], h_ref[k, :, INNER:]
        spectrum = jnp.concatenate(
            [cosine * real + sine * imag, cosine * imag - sine * real], axis=1
        )

        def planes(first):
            for p in range(first, first + PLANES // 2):
                product = jnp.concatenate(
                    [
                        cs_ref[0, 2 * p : 2 * p + 1, :] * spectrum,
                        cs_ref[0, 2 * p + 1 : 2 * p + 2, :] * spectrum,
                    ],
                    axis=0,
                )
                high, low = halves(product)
                value = jnp.dot(
                    jnp.concatenate([high, low, high], axis=1),
                    tt_ref[0],
                    preferred_element_type=F32,
                )
                a_ref[parity, p] = jnp.where(k < 2, value, a_ref[parity, p] + value)

        planes(0)
        progress(2 * step)
        planes(PLANES // 2)
        progress(2 * step + 1)

    @pl.when(step == 2 * CLASSES - 1)
    def _():
        @pl.loop(0, PLANES)
        def _(p):
            for core in range(2):
                lanes = slice(core * 128, (core + 1) * 128)
                for c in range(2):
                    rows = slice(c * LANES, (c + 1) * LANES)
                    even, odd = a_ref[0, p, rows, lanes], a_ref[1, p, rows, lanes]
                    upper, lower = (even + odd).T, (even - odd).T
                    for owner in range(PLANES):
                        part = slice(owner * 16, owner * 16 + 16)
                        held = pl.ds(p, 16, stride=PLANES)
                        o_ref[owner * 4 + core, c, held, :] = upper[part]
                        o_ref[owner * 4 + 2 + core, c, held, :] = lower[part]


def filter_y(rotations, received, factors):
    forward, backward = class_tables()
    last = CLASSES - 1
    return pl.pallas_call(
        filter_y_kernel,
        grid=(2 * CLASSES,),
        in_specs=[
            pl.BlockSpec(memory_space=pltpu.SMEM),
            whole((32, 272, LANES)),
            pl.BlockSpec((1, 768, 512), lambda i: (jnp.minimum(i, last), 0, 0)),
            pl.BlockSpec((1, 1536, 256), lambda i: (jnp.maximum(i - CLASSES, 0), 0, 0)),
            pl.BlockSpec((1, 16, 512), lambda i: (lax.rem(i, CLASSES), 0, 0)),
        ],
        out_specs=whole((32, 2, 128, LANES)),
        out_shape=jax.ShapeDtypeStruct((32, 2, 128, LANES), F32),
        scratch_shapes=[
            pltpu.VMEM((2, PLANES + 1, 2 * LANES, 768), BF16),
            pltpu.VMEM((CLASSES, LANES, 2 * INNER), F32),
            pltpu.VMEM((CLASSES, LANES, 2 * INNER), F32),
            pltpu.VMEM((CLASSES, REDUCE_HOPS, PART, 2 * INNER), F32),
            pltpu.VMEM((2, PLANES, 2 * LANES, INNER), F32),
            pltpu.SemaphoreType.DMA((CLASSES,)),
            pltpu.SemaphoreType.DMA((CLASSES, HOPS)),
        ],
        compiler_params=pltpu.CompilerParams(
            collective_id=0, has_side_effects=True, vmem_limit_bytes=56 << 20
        ),
        cost_estimate=cost_of(90),
        name="filter_y",
    )(rotations, received, jnp.asarray(forward), jnp.asarray(backward), factors)


TV_ROWS = 8


def shrink_kernel(edge_ref, m_ref, next_ref, above_ref, below_ref, o_ref, e_ref, prior_ref):
    step = pl.program_id(0)
    plane = lax.broadcasted_iota(jnp.int32, (PLANES, N), 0)
    column = lax.broadcasted_iota(jnp.int32, (PLANES, N), 1)
    last_plane, first_plane = plane == PLANES - 1, plane == 0
    last_column, first_column = column == N - 1, column == 0

    def flux(here, below):
        squares = None
        diffs = []
        for c in range(2):
            depth = jnp.where(last_plane, 0.0, pltpu.roll(here[c], PLANES - 1, 0) - here[c])
            row = below[c] - here[c]
            col = jnp.where(last_column, 0.0, pltpu.roll(here[c], N - 1, 1) - here[c])
            diffs.append((depth, row, col))
            term = depth * depth + row * row + col * col
            squares = term if squares is None else squares + term
        factor = 1.0 / (1.0 + tv_sharpness * jnp.sqrt(squares))
        return [tuple(d * factor for d in triple) for triple in diffs]

    @pl.when(step == 0)
    def _():
        above = [above_ref[c] for c in range(2)]
        first = [m_ref[c, :PLANES, :] for c in range(2)]
        terms = flux(above, first)
        for c in range(2):
            prior_ref[c] = jnp.where(edge_ref[0] > 0, terms[c][1], 0.0)

    def row_at(t):
        rows = pl.ds(pl.multiple_of(t * PLANES, PLANES), PLANES)
        return [m_ref[c, rows, :] for c in range(2)]

    def emit(t, here, below):
        terms = flux(here, below)
        rows = pl.ds(pl.multiple_of(t * PLANES, PLANES), PLANES)
        for c in range(2):
            depth, row, col = terms[c]
            divergence = (
                (depth - jnp.where(first_plane, 0.0, pltpu.roll(depth, 1, 0)))
                + (row - prior_ref[c])
                + (col - jnp.where(first_column, 0.0, pltpu.roll(col, 1, 1)))
            )
            prior_ref[c] = row
            estimate = here[c] + tv_step_size * divergence
            for j in range(N // LANES):
                e_ref[c, j, rows, :] = estimate[:, j * LANES : (j + 1) * LANES]

    @pl.loop(0, TV_ROWS - 1)
    def _(t):
        emit(t, row_at(t), row_at(t + 1))

    here = row_at(TV_ROWS - 1)
    final = step == 16 // TV_ROWS - 1
    below = []
    for c in range(2):
        beyond = jnp.where(edge_ref[1] > 0, below_ref[c], here[c])
        below.append(jnp.where(final, beyond, next_ref[c]))
    emit(TV_ROWS - 1, here, below)
    for p in range(PLANES):
        for c in range(2):
            for j in range(N // LANES):
                held = pl.ds(p, TV_ROWS, stride=PLANES)
                o_ref[p, c, :, j * LANES : (j + 1) * LANES] = e_ref[c, j, held, :]


def shrink(edges, moved, above, below):
    steps = 16 // TV_ROWS
    return pl.pallas_call(
        shrink_kernel,
        grid=(steps,),
        in_specs=[
            pl.BlockSpec(memory_space=pltpu.SMEM),
            pl.BlockSpec((2, TV_ROWS * PLANES, N), lambda i: (0, i, 0)),
            pl.BlockSpec((2, PLANES, N), lambda i: (0, jnp.minimum((i + 1) * TV_ROWS, 15), 0)),
            whole((2, PLANES, N)),
            whole((2, PLANES, N)),
        ],
        out_specs=pl.BlockSpec((PLANES, 2, TV_ROWS, N), lambda i: (0, 0, i, 0)),
        out_shape=jax.ShapeDtypeStruct((PLANES, 2, 16, N), F32),
        scratch_shapes=[
            pltpu.VMEM((2, N // LANES, TV_ROWS * PLANES, LANES), F32),
            pltpu.VMEM((2, PLANES, N), F32),
        ],
        compiler_params=params(),
        cost_estimate=cost_of(9),
        name="tv_shrink",
    )(edges, moved, moved, above, below)


def along_rows(block, distance):
    place = lambda line: (line % 8) * 32 + line // 8
    route = [
        (place(line - distance), place(line)) for line in range(256) if 0 <= line - distance < 256
    ]
    return lax.ppermute(block, DEPTH + ROW, route)


def phase_of(depth_values, squares):
    return depth_values * (squares * (math.pi / (N * N)))


def per_device(field, hologram, defocus):
    x_lo, y = lax.axis_index("x_lo"), lax.axis_index("y")
    x_hi, z, core = lax.axis_index("x_hi"), lax.axis_index("z"), lax.axis_index("core")
    depth_index = x_lo * 4 + y
    row_index = x_hi * 16 + z * 2 + core
    field = field[:, 0]

    x_freq = RADIX * np.arange(INNER)[None, :] + np.arange(RADIX)[:, None]
    x_squares = jnp.asarray(squares_of(x_freq))[:, None, :]
    x_phase = phase_of(defocus[0], x_squares)
    x_forward = jnp.stack([jnp.cos(x_phase) / N, -jnp.sin(x_phase) / N])

    depths = lax.all_gather(defocus, DEPTH, tiled=True)
    x_phase = phase_of(depths[None, :, None], x_squares)
    x_backward = jnp.stack([jnp.cos(x_phase), jnp.sin(x_phase)]) * (-1.0 / (PLANES * N))
    y_squares = jnp.asarray(squares_of(class_frequencies()))[:, None, None, :]
    y_phase = phase_of(depths[None, :, None, None], y_squares)
    factors = jnp.concatenate([jnp.cos(y_phase), jnp.sin(y_phase)], axis=2)
    factors = factors.reshape(CLASSES, 2 * PLANES, INNER)
    factors = jnp.concatenate([factors, factors], axis=2)

    weights = np.full((CLASSES,), 2.0 / N, np.float32)
    weights[0] = weights[8] = 1.0 / N
    turns = lax.rem(z * np.arange(CLASSES, dtype=np.int32), RADIX).astype(F32)
    turns = turns * (2.0 * math.pi / RADIX)
    cosine, sine = jnp.cos(turns), jnp.sin(turns)
    rotations = jnp.stack([weights * cosine, weights * sine, cosine, sine], axis=1)

    hologram_rows = lax.dynamic_slice_in_dim(hologram, depth_index * 16, 16, 0)
    sent = forward_x(field, hologram_rows, x_forward)
    received = lax.all_to_all(sent, LAYER, 0, 0, tiled=True)
    field, received = lax.optimization_barrier((field, received))
    held = jnp.transpose(field.reshape(2, PLANES, 16, N), (1, 0, 2, 3))
    held = lax.all_to_all(held, DEPTH, 0, 0, tiled=True)
    sent = filter_y(rotations, received, factors)
    received = lax.all_to_all(sent, LAYER, 0, 0, tiled=True)
    moved = backward_x(received, held, x_backward)
    above = along_rows(moved[:, 120:], 1)
    below = along_rows(moved[:, :8], -1)
    line = row_index * 8 + depth_index
    edges = jnp.stack([line > 0, line < 255]).astype(jnp.int32)
    estimate = shrink(edges, moved, above, below)
    estimate = lax.all_to_all(estimate, DEPTH, 0, 0, tiled=True)
    return jnp.transpose(estimate, (1, 0, 2, 3)).reshape(2, 1, 128, N)


def solution(mesh):
    fine = Mesh(mesh.devices.reshape(2, 4, 2, 8, 2), DEPTH + ROW)
    return jax.shard_map(
        per_device,
        mesh=fine,
        in_specs=(P(None, DEPTH, ROW, None), P(ROW, None), P(DEPTH)),
        out_specs=P(None, DEPTH, ROW, None),
        check_vma=False,
    )
```

```python
import functools
import math

import jax
import jax.numpy as jnp
import ml_dtypes
import numpy as np
from jax import lax
from jax.experimental import pallas as pl
from jax.experimental.pallas import tpu as pltpu
from jax.sharding import Mesh
from jax.sharding import PartitionSpec as P

tv_step_size = 1.0 / 12.0
tv_sharpness = 0.25

N = 4096
RADIX = 16
INNER = 256
CLASSES = 9
PLANES = 8
LANES = 128
F32 = jnp.float32
BF16 = jnp.bfloat16

DEPTH = ("x_lo", "y")
ROW = ("x_hi", "z", "core")
LAYER = ("x_lo", "y", "x_hi", "core")


def split_table(table):
    high = table.astype(ml_dtypes.bfloat16)
    low = (table - high.astype(np.float64)).astype(ml_dtypes.bfloat16)
    return high, low


def inner_tables():
    index = np.arange(INNER)
    angle = 2.0 * np.pi * (np.outer(index, index) % INNER) / INNER
    cosine, sine = np.cos(angle), np.sin(angle)
    tables = []
    for sign in (1.0, -1.0):
        whole = np.block([[cosine, -sign * sine], [sign * sine, cosine]])
        high, low = split_table(whole)
        tables.append(np.concatenate([high, high, low], axis=0))
    return tables


def twiddles():
    angle = 2.0 * np.pi * np.outer(np.arange(RADIX), np.arange(INNER)) / N
    return np.stack([np.cos(angle), np.sin(angle)]).astype(np.float32)


def class_frequencies():
    return (RADIX * np.arange(INNER)[None, :] + np.arange(CLASSES)[:, None]) % N


def class_tables():
    freq = class_frequencies()
    angle = 2.0 * np.pi * ((freq[:, None, :] * np.arange(INNER)[None, :, None]) % N) / N
    table = np.concatenate([np.cos(angle), np.sin(angle)], axis=2)
    tables = []
    for each in (table, np.swapaxes(table, 1, 2)):
        high, low = split_table(each)
        tables.append(np.concatenate([high, high, low], axis=1))
    return tables


def squares_of(index):
    centred = np.where(index < N // 2, index, index - N)
    return (centred * centred).astype(np.float32)


def dft4(values, inverse):
    (ar, ai), (br, bi), (cr, ci), (dr, di) = values
    s0r, s0i, s1r, s1i = ar + cr, ai + ci, ar - cr, ai - ci
    s2r, s2i, s3r, s3i = br + dr, bi + di, br - dr, bi - di
    plus = (s1r - s3i, s1i + s3r)
    minus = (s1r + s3i, s1i - s3r)
    first, third = (plus, minus) if inverse else (minus, plus)
    return [(s0r + s2r, s0i + s2i), first, (s0r - s2r, s0i - s2i), third]


def times_constant(value, cosine, sine):
    real, imag = value
    if abs(sine) < 1e-9 and abs(cosine - 1.0) < 1e-9:
        return value
    if abs(cosine) < 1e-9 and abs(sine - 1.0) < 1e-9:
        return (-imag, real)
    if abs(cosine) < 1e-9 and abs(sine + 1.0) < 1e-9:
        return (imag, -real)
    if abs(abs(cosine) - abs(sine)) < 1e-9:
        root = math.sqrt(0.5)
        sc, ss = math.copysign(1.0, cosine), math.copysign(1.0, sine)
        first = (real if sc > 0 else -real) - (imag if ss > 0 else -imag)
        second = (imag if sc > 0 else -imag) + (real if ss > 0 else -real)
        return (first * root, second * root)
    return (real * cosine - imag * sine, imag * cosine + real * sine)


def dft16(values, inverse):
    direction = 1.0 if inverse else -1.0
    stage = [dft4([values[4 * n1 + n2] for n1 in range(4)], inverse) for n2 in range(4)]
    result = [None] * 16
    for k1 in range(4):
        column = []
        for n2 in range(4):
            angle = direction * 2.0 * math.pi * n2 * k1 / 16
            column.append(times_constant(stage[n2][k1], math.cos(angle), math.sin(angle)))
        for k2, value in enumerate(dft4(column, inverse)):
            result[k1 + 4 * k2] = value
    return result


def weighted_sum(terms):
    total = None
    for coefficient, value in terms:
        if abs(coefficient) < 1e-9:
            continue
        if abs(coefficient - 1.0) < 1e-9:
            total = value if total is None else total + value
        elif abs(coefficient + 1.0) < 1e-9:
            total = -value if total is None else total - value
        else:
            piece = value * float(np.float32(coefficient))
            total = piece if total is None else total + piece
    return total


def real_dft16(blocks):
    sums = [blocks[0]] + [blocks[b] + blocks[16 - b] for b in range(1, 8)] + [blocks[8]]
    diffs = [None] + [blocks[b] - blocks[16 - b] for b in range(1, 8)]
    result = []
    for k in range(CLASSES):
        real = weighted_sum([(math.cos(2 * math.pi * k * b / 16), sums[b]) for b in range(9)])
        if k in (0, 8):
            imag = jnp.zeros_like(real)
        else:
            imag = weighted_sum(
                [(-math.sin(2 * math.pi * k * b / 16), diffs[b]) for b in range(1, 8)]
            )
        result.append((real, imag))
    return result


def real_inverse16(values):
    result = [None] * 16
    for b in range(9):
        even = weighted_sum([(math.cos(2 * math.pi * k * b / 16), values[k][0]) for k in range(9)])
        if b in (0, 8):
            result[b] = even
        else:
            odd = weighted_sum(
                [(math.sin(2 * math.pi * k * b / 16), values[k][1]) for k in range(1, 8)]
            )
            result[b] = even - odd
            result[16 - b] = even + odd
    return result


def halves(value):
    high = value.astype(BF16)
    low = (value - high.astype(F32)).astype(BF16)
    return high, low


STEP_ROWS = 32
CHUNK_CLASSES = 16


def filter_rows(load, store, tw_ref, d_ref, wf_ref, wi_ref, x_ref):
    groups = [(r, h) for r in range(STEP_ROWS // 8) for h in range(INNER // LANES)]
    for r, h in groups:
        values = [load(r, b * (INNER // LANES) + h) for b in range(RADIX)]
        lanes = slice(h * LANES, (h + 1) * LANES)
        for k, (real, imag) in enumerate(dft16(values, False)):
            if k:
                cosine, sine = tw_ref[0, k : k + 1, lanes], tw_ref[1, k : k + 1, lanes]
                real, imag = real * cosine + imag * sine, imag * cosine - real * sine
            rows = slice(k * STEP_ROWS + 8 * r, k * STEP_ROWS + 8 * r + 8)
            x_ref[rows, lanes] = real
            x_ref[rows, INNER + h * LANES : INNER + (h + 1) * LANES] = imag
    for chunk in range(RADIX // CHUNK_CLASSES):
        base = chunk * CHUNK_CLASSES * STEP_ROWS
        rows = slice(base, base + CHUNK_CLASSES * STEP_ROWS)
        high, low = halves(x_ref[rows, :])
        spectrum = jnp.dot(
            jnp.concatenate([high, low, high], axis=1), wf_ref[...], preferred_element_type=F32
        )
        pieces = []
        for kk in range(CHUNK_CLASSES):
            k = chunk * CHUNK_CLASSES + kk
            cosine, sine = per_row(d_ref[0, k]), per_row(d_ref[1, k])
            real = spectrum[kk * STEP_ROWS : (kk + 1) * STEP_ROWS, :INNER]
            imag = spectrum[kk * STEP_ROWS : (kk + 1) * STEP_ROWS, INNER:]
            pieces.append(
                jnp.concatenate(
                    [real * cosine - imag * sine, imag * cosine + real * sine], axis=1
                )
            )
        high, low = halves(jnp.concatenate(pieces, axis=0))
        x_ref[rows, :] = jnp.dot(
            jnp.concatenate([high, low, high], axis=1), wi_ref[...], preferred_element_type=F32
        )
    for r, h in groups:
        lanes = slice(h * LANES, (h + 1) * LANES)
        values = []
        for k in range(RADIX):
            rows = slice(k * STEP_ROWS + 8 * r, k * STEP_ROWS + 8 * r + 8)
            real = x_ref[rows, lanes]
            imag = x_ref[rows, INNER + h * LANES : INNER + (h + 1) * LANES]
            if k:
                cosine, sine = tw_ref[0, k : k + 1, lanes], tw_ref[1, k : k + 1, lanes]
                real, imag = real * cosine - imag * sine, imag * cosine + real * sine
            values.append((real, imag))
        for b, value in enumerate(dft16(values, True)):
            store(r, b * (INNER // LANES) + h, value)


def per_row(factor):
    if factor.shape[0] == 1:
        return factor
    return jnp.concatenate([factor] * (STEP_ROWS // factor.shape[0]), axis=0)


def forward_x_kernel(f_ref, hol_ref, tw_ref, d_ref, wf_ref, wi_ref, o_ref, x_ref):
    step = pl.program_id(0)

    @pl.when(step == 0)
    def _():
        for j in range(32):
            o_ref[j, 256:272, :] = hol_ref[:, j * LANES : (j + 1) * LANES]

    def load(r, j):
        rows, lanes = slice(8 * r, 8 * r + 8), slice(j * LANES, (j + 1) * LANES)
        return f_ref[0, rows, lanes], f_ref[1, rows, lanes]

    def store(r, j, value):
        for c in range(2):
            start = pl.multiple_of(step * STEP_ROWS + 128 * c + 8 * r, 8)
            o_ref[j, pl.ds(start, 8), :] = value[c]

    filter_rows(load, store, tw_ref, d_ref, wf_ref, wi_ref, x_ref)


def backward_x_kernel(g_ref, held_ref, tw_ref, d_ref, wf_ref, wi_ref, o_ref, x_ref, f_ref):
    step = pl.program_id(0)

    @pl.when(step == 0)
    def _():
        for c in range(2):
            for p in range(PLANES):
                for j in range(N // LANES):
                    f_ref[c, j, pl.ds(p, 16, stride=PLANES), :] = held_ref[
                        p, c, :, j * LANES : (j + 1) * LANES
                    ]

    def load(r, j):
        rows = slice(8 * r, 8 * r + 8)
        return g_ref[j, 0, rows, :], g_ref[j, 1, rows, :]

    def store(r, j, value):
        rows, lanes = slice(8 * r, 8 * r + 8), slice(j * LANES, (j + 1) * LANES)
        held = pl.ds(pl.multiple_of(step * STEP_ROWS + 8 * r, 8), 8)
        for c in range(2):
            o_ref[c, rows, lanes] = f_ref[c, j, held, :] + value[c]

    filter_rows(load, store, tw_ref, d_ref, wf_ref, wi_ref, x_ref)


def whole(shape):
    return pl.BlockSpec(shape, lambda *_: (0,) * len(shape))


def cost_of(microseconds):
    return pl.CostEstimate(flops=0, bytes_accessed=microseconds * 3_000_000, transcendentals=0)


def params():
    return pltpu.CompilerParams(vmem_limit_bytes=56 << 20)


def x_tables():
    forward, inverse = inner_tables()
    return jnp.asarray(twiddles()), jnp.asarray(forward), jnp.asarray(inverse)


def forward_x(field, hologram_rows, transfer):
    tw, wf, wi = x_tables()
    return pl.pallas_call(
        forward_x_kernel,
        grid=(128 // STEP_ROWS,),
        in_specs=[
            pl.BlockSpec((2, STEP_ROWS, N), lambda i: (0, i, 0)),
            whole((16, N)),
            whole((2, RADIX, INNER)),
            whole((2, RADIX, 1, INNER)),
            whole((1536, 512)),
            whole((1536, 512)),
        ],
        out_specs=whole((32, 272, LANES)),
        out_shape=jax.ShapeDtypeStruct((32, 272, LANES), F32),
        scratch_shapes=[pltpu.VMEM((RADIX * STEP_ROWS, 2 * INNER), F32)],
        compiler_params=params(),
        cost_estimate=cost_of(14),
        name="filter_x_forward",
    )(field, hologram_rows, tw, transfer, wf, wi)


def backward_x(gradient, held, transfer):
    tw, wf, wi = x_tables()
    return pl.pallas_call(
        backward_x_kernel,
        grid=(128 // STEP_ROWS,),
        in_specs=[
            pl.BlockSpec((32, 2, STEP_ROWS, LANES), lambda i: (0, 0, i, 0)),
            whole((PLANES, 2, 16, N)),
            whole((2, RADIX, INNER)),
            whole((2, RADIX, PLANES, INNER)),
            whole((1536, 512)),
            whole((1536, 512)),
        ],
        out_specs=pl.BlockSpec((2, STEP_ROWS, N), lambda i: (0, i, 0)),
        out_shape=jax.ShapeDtypeStruct((2, 128, N), F32),
        scratch_shapes=[
            pltpu.VMEM((RADIX * STEP_ROWS, 2 * INNER), F32),
            pltpu.VMEM((2, N // LANES, 128, LANES), F32),
        ],
        compiler_params=params(),
        cost_estimate=cost_of(16),
        name="filter_x_backward",
    )(gradient, held, tw, transfer, wf, wi)


LAYERS = 8
PART = LANES // LAYERS
LONG = LAYERS // 2
SHORT = LAYERS - 1 - LONG
HOPS = 2 * LONG


def filter_y_kernel(
    rot_ref, g_ref, t_ref, tt_ref, cs_ref, o_ref, u_ref, s_ref, h_ref, r_ref, a_ref, send_sem, recv_sem
):
    step = pl.program_id(0)
    me = lax.axis_index("z")

    def hop(k, h):
        sign = 1 - 2 * lax.rem(k, 2)

        def block(distance):
            index = lax.rem(me + sign * distance + LAYERS, LAYERS)
            return pl.ds(pl.multiple_of(index * PART, PART), PART)

        def copy(source, target, way, h):
            onward = sign if way == 0 else -sign
            return pltpu.make_async_remote_copy(
                src_ref=source,
                dst_ref=target,
                send_sem=send_sem.at[k, way],
                recv_sem=recv_sem.at[k, way, h],
                device_id={"z": lax.rem(me + onward + LAYERS, LAYERS)},
                device_id_type=pl.DeviceIdType.MESH,
            )

        own = block(0)

        def finish(way):
            last = copy(s_ref.at[k, own, :], r_ref.at[k, 0], way, h - 1)
            last.wait_send()
            last.wait_recv()

        @pl.when(h > 0)
        def _():
            finish(0)

        @pl.when((h > 0) & (h != LONG) & (h != 2 * LONG))
        def _():
            finish(1)

        def reduce(way, length, first_slot, rows):
            @pl.when(h < length)
            def _():
                @pl.when(h > 0)
                def _():
                    s_ref[k, rows, :] += r_ref[k, first_slot + h - 1]

                copy(s_ref.at[k, rows, :], r_ref.at[k, first_slot + h], way, h).start()

        reduce(0, LONG, 0, block(LONG - h))
        reduce(1, SHORT, LONG, block(h - SHORT))

        @pl.when(h == LONG)
        def _():
            h_ref[k, own, :] = (
                s_ref[k, own, :] + r_ref[k, LONG - 1] + r_ref[k, LONG + SHORT - 1]
            )

        def gather(way, length, rows):
            @pl.when((h >= LONG) & (h < LONG + length))
            def _():
                copy(h_ref.at[k, rows, :], h_ref.at[k, rows, :], way, h).start()

        gather(0, LONG, block(LONG - h))
        gather(1, SHORT, block(h - LONG))

    def progress(slot):
        @pl.loop(0, CLASSES)
        def _(k):
            h = slot - k

            @pl.when((h >= 0) & (h <= HOPS))
            def _():
                hop(k, h)

    @pl.when(step == 0)
    def _():
        barrier = pltpu.get_barrier_semaphore()
        for distance in (1, LAYERS - 1):
            pl.semaphore_signal(
                barrier,
                inc=1,
                device_id={"z": lax.rem(me + distance, LAYERS)},
                device_id_type=pl.DeviceIdType.MESH,
            )
        pl.semaphore_wait(barrier, 2)

        def place(p, lanes, core, upper, lower):
            for parity, value in ((0, upper + lower), (1, upper - lower)):
                high, low = halves(value)
                for part, piece in ((0, high), (1, low), (2, high)):
                    start = part * INNER + core * 128
                    u_ref[parity, p, lanes, start : start + 128] = piece

        @pl.loop(0, PLANES)
        def _(p):
            for core in range(2):
                for c in range(2):
                    rows = slice(c * 128, (c + 1) * 128)
                    upper = g_ref[p * 4 + core, rows, :].T
                    lower = g_ref[p * 4 + 2 + core, rows, :].T
                    place(p, slice(c * LANES, (c + 1) * LANES), core, upper, lower)

        for core in range(2):
            tiles = []
            for upper in range(2):
                rows = [g_ref[p * 4 + upper * 2 + core, 256:, :] for p in range(PLANES)]
                tiles.append(jnp.concatenate(rows, axis=0).T)
            place(PLANES, slice(0, LANES), core, tiles[0], tiles[1])

    @pl.when(step < CLASSES)
    def _():
        parity = lax.rem(step, 2)

        def planes(first, total):
            for p in range(first, first + PLANES // 2):
                result = jnp.dot(u_ref[parity, p], t_ref[0], preferred_element_type=F32)
                total = (
                    total
                    + cs_ref[0, 2 * p : 2 * p + 1, :] * result[:LANES]
                    + cs_ref[0, 2 * p + 1 : 2 * p + 2, :] * result[LANES:]
                )
            return total

        minus = jnp.dot(u_ref[parity, PLANES, :LANES, :], t_ref[0], preferred_element_type=F32)
        total = planes(PLANES // 2, planes(0, -minus))
        cosine, sine = rot_ref[step, 0], rot_ref[step, 1]
        real, imag = total[:, :INNER], total[:, INNER:]
        s_ref[step, :, :INNER] = cosine * real - sine * imag
        s_ref[step, :, INNER:] = cosine * imag + sine * real

    @pl.when(step >= CLASSES)
    def _():
        k = step - CLASSES
        parity = lax.rem(k, 2)
        cosine, sine = rot_ref[k, 2], rot_ref[k, 3]
        real, imag = h_ref[k, :, :INNER], h_ref[k, :, INNER:]
        spectrum = jnp.concatenate(
            [cosine * real + sine * imag, cosine * imag - sine * real], axis=1
        )

        def planes(first):
            for p in range(first, first + PLANES // 2):
                product = jnp.concatenate(
                    [
                        cs_ref[0, 2 * p : 2 * p + 1, :] * spectrum,
                        cs_ref[0, 2 * p + 1 : 2 * p + 2, :] * spectrum,
                    ],
                    axis=0,
                )
                high, low = halves(product)
                value = jnp.dot(
                    jnp.concatenate([high, low, high], axis=1),
                    tt_ref[0],
                    preferred_element_type=F32,
                )
                a_ref[parity, p] = jnp.where(k < 2, value, a_ref[parity, p] + value)

        planes(0)
        planes(PLANES // 2)

    progress(step)

    @pl.when(step == 2 * CLASSES - 1)
    def _():
        @pl.loop(0, PLANES)
        def _(p):
            for core in range(2):
                lanes = slice(core * 128, (core + 1) * 128)
                for c in range(2):
                    rows = slice(c * LANES, (c + 1) * LANES)
                    even, odd = a_ref[0, p, rows, lanes], a_ref[1, p, rows, lanes]
                    upper, lower = (even + odd).T, (even - odd).T
                    for owner in range(PLANES):
                        part = slice(owner * 16, owner * 16 + 16)
                        held = pl.ds(p, 16, stride=PLANES)
                        o_ref[owner * 4 + core, c, held, :] = upper[part]
                        o_ref[owner * 4 + 2 + core, c, held, :] = lower[part]


def filter_y(rotations, received, factors):
    forward, backward = class_tables()
    last = CLASSES - 1
    return pl.pallas_call(
        filter_y_kernel,
        grid=(2 * CLASSES,),
        in_specs=[
            pl.BlockSpec(memory_space=pltpu.SMEM),
            whole((32, 272, LANES)),
            pl.BlockSpec((1, 768, 512), lambda i: (jnp.minimum(i, last), 0, 0)),
            pl.BlockSpec((1, 1536, 256), lambda i: (jnp.maximum(i - CLASSES, 0), 0, 0)),
            pl.BlockSpec((1, 16, 512), lambda i: (lax.rem(i, CLASSES), 0, 0)),
        ],
        out_specs=whole((32, 2, 128, LANES)),
        out_shape=jax.ShapeDtypeStruct((32, 2, 128, LANES), F32),
        scratch_shapes=[
            pltpu.VMEM((2, PLANES + 1, 2 * LANES, 768), BF16),
            pltpu.VMEM((CLASSES, LANES, 2 * INNER), F32),
            pltpu.VMEM((CLASSES, LANES, 2 * INNER), F32),
            pltpu.VMEM((CLASSES, LONG + SHORT, PART, 2 * INNER), F32),
            pltpu.VMEM((2, PLANES, 2 * LANES, INNER), F32),
            pltpu.SemaphoreType.DMA((CLASSES, 2)),
            pltpu.SemaphoreType.DMA((CLASSES, 2, HOPS)),
        ],
        compiler_params=pltpu.CompilerParams(
            collective_id=0, has_side_effects=True, vmem_limit_bytes=56 << 20
        ),
        cost_estimate=cost_of(90),
        name="filter_y",
    )(rotations, received, jnp.asarray(forward), jnp.asarray(backward), factors)


TV_ROWS = 8


def shrink_kernel(edge_ref, m_ref, next_ref, above_ref, below_ref, o_ref, e_ref, prior_ref):
    step = pl.program_id(0)
    plane = lax.broadcasted_iota(jnp.int32, (PLANES, N), 0)
    column = lax.broadcasted_iota(jnp.int32, (PLANES, N), 1)
    last_plane, first_plane = plane == PLANES - 1, plane == 0
    last_column, first_column = column == N - 1, column == 0

    def flux(here, below):
        squares = None
        diffs = []
        for c in range(2):
            depth = jnp.where(last_plane, 0.0, pltpu.roll(here[c], PLANES - 1, 0) - here[c])
            row = below[c] - here[c]
            col = jnp.where(last_column, 0.0, pltpu.roll(here[c], N - 1, 1) - here[c])
            diffs.append((depth, row, col))
            term = depth * depth + row * row + col * col
            squares = term if squares is None else squares + term
        factor = 1.0 / (1.0 + tv_sharpness * jnp.sqrt(squares))
        return [tuple(d * factor for d in triple) for triple in diffs]

    @pl.when(step == 0)
    def _():
        above = [above_ref[c] for c in range(2)]
        first = [m_ref[c, :PLANES, :] for c in range(2)]
        terms = flux(above, first)
        for c in range(2):
            prior_ref[c] = jnp.where(edge_ref[0] > 0, terms[c][1], 0.0)

    def row_at(t):
        rows = pl.ds(pl.multiple_of(t * PLANES, PLANES), PLANES)
        return [m_ref[c, rows, :] for c in range(2)]

    def emit(t, here, below):
        terms = flux(here, below)
        rows = pl.ds(pl.multiple_of(t * PLANES, PLANES), PLANES)
        for c in range(2):
            depth, row, col = terms[c]
            divergence = (
                (depth - jnp.where(first_plane, 0.0, pltpu.roll(depth, 1, 0)))
                + (row - prior_ref[c])
                + (col - jnp.where(first_column, 0.0, pltpu.roll(col, 1, 1)))
            )
            prior_ref[c] = row
            estimate = here[c] + tv_step_size * divergence
            for j in range(N // LANES):
                e_ref[c, j, rows, :] = estimate[:, j * LANES : (j + 1) * LANES]

    @pl.loop(0, TV_ROWS - 1)
    def _(t):
        emit(t, row_at(t), row_at(t + 1))

    here = row_at(TV_ROWS - 1)
    final = step == 16 // TV_ROWS - 1
    below = []
    for c in range(2):
        beyond = jnp.where(edge_ref[1] > 0, below_ref[c], here[c])
        below.append(jnp.where(final, beyond, next_ref[c]))
    emit(TV_ROWS - 1, here, below)
    for p in range(PLANES):
        for c in range(2):
            for j in range(N // LANES):
                held = pl.ds(p, TV_ROWS, stride=PLANES)
                o_ref[p, c, :, j * LANES : (j + 1) * LANES] = e_ref[c, j, held, :]


def shrink(edges, moved, above, below):
    steps = 16 // TV_ROWS
    return pl.pallas_call(
        shrink_kernel,
        grid=(steps,),
        in_specs=[
            pl.BlockSpec(memory_space=pltpu.SMEM),
            pl.BlockSpec((2, TV_ROWS * PLANES, N), lambda i: (0, i, 0)),
            pl.BlockSpec((2, PLANES, N), lambda i: (0, jnp.minimum((i + 1) * TV_ROWS, 15), 0)),
            whole((2, PLANES, N)),
            whole((2, PLANES, N)),
        ],
        out_specs=pl.BlockSpec((PLANES, 2, TV_ROWS, N), lambda i: (0, 0, i, 0)),
        out_shape=jax.ShapeDtypeStruct((PLANES, 2, 16, N), F32),
        scratch_shapes=[
            pltpu.VMEM((2, N // LANES, TV_ROWS * PLANES, LANES), F32),
            pltpu.VMEM((2, PLANES, N), F32),
        ],
        compiler_params=params(),
        cost_estimate=cost_of(9),
        name="tv_shrink",
    )(edges, moved, moved, above, below)


def along_rows(block, distance):
    place = lambda line: (line % 8) * 32 + line // 8
    route = [
        (place(line - distance), place(line)) for line in range(256) if 0 <= line - distance < 256
    ]
    return lax.ppermute(block, DEPTH + ROW, route)


def phase_of(depth_values, squares):
    return depth_values * (squares * (math.pi / (N * N)))


def per_device(field, hologram, defocus):
    x_lo, y = lax.axis_index("x_lo"), lax.axis_index("y")
    x_hi, z, core = lax.axis_index("x_hi"), lax.axis_index("z"), lax.axis_index("core")
    depth_index = x_lo * 4 + y
    row_index = x_hi * 16 + z * 2 + core
    field = field[:, 0]

    x_freq = RADIX * np.arange(INNER)[None, :] + np.arange(RADIX)[:, None]
    x_squares = jnp.asarray(squares_of(x_freq))[:, None, :]
    x_phase = phase_of(defocus[0], x_squares)
    x_forward = jnp.stack([jnp.cos(x_phase) / N, -jnp.sin(x_phase) / N])

    weights = np.full((CLASSES,), 2.0 / N, np.float32)
    weights[0] = weights[8] = 1.0 / N
    turns = lax.rem(z * np.arange(CLASSES, dtype=np.int32), RADIX).astype(F32)
    turns = turns * (2.0 * math.pi / RADIX)
    cosine, sine = jnp.cos(turns), jnp.sin(turns)
    rotations = jnp.stack([weights * cosine, weights * sine, cosine, sine], axis=1)

    hologram_rows = lax.dynamic_slice_in_dim(hologram, depth_index * 16, 16, 0)
    sent = forward_x(field, hologram_rows, x_forward)
    defocus, sent = lax.optimization_barrier((defocus, sent))
    depths = lax.all_gather(defocus, DEPTH, tiled=True)
    x_phase = phase_of(depths[None, :, None], x_squares)
    x_backward = jnp.stack([jnp.cos(x_phase), jnp.sin(x_phase)]) * (-1.0 / (PLANES * N))
    y_squares = jnp.asarray(squares_of(class_frequencies()))[:, None, None, :]
    y_phase = phase_of(depths[None, :, None, None], y_squares)
    factors = jnp.concatenate([jnp.cos(y_phase), jnp.sin(y_phase)], axis=2)
    factors = factors.reshape(CLASSES, 2 * PLANES, INNER)
    factors = jnp.concatenate([factors, factors], axis=2)
    received = lax.all_to_all(sent, LAYER, 0, 0, tiled=True)
    field, received, factors = lax.optimization_barrier((field, received, factors))
    held = jnp.transpose(field.reshape(2, PLANES, 16, N), (1, 0, 2, 3))
    held = lax.all_to_all(held, DEPTH, 0, 0, tiled=True)
    sent = filter_y(rotations, received, factors)
    received = lax.all_to_all(sent, LAYER, 0, 0, tiled=True)
    moved = backward_x(received, held, x_backward)
    above = along_rows(moved[:, 120:], 1)
    below = along_rows(moved[:, :8], -1)
    line = row_index * 8 + depth_index
    edges = jnp.stack([line > 0, line < 255]).astype(jnp.int32)
    estimate = shrink(edges, moved, above, below)
    estimate = lax.all_to_all(estimate, DEPTH, 0, 0, tiled=True)
    return jnp.transpose(estimate, (1, 0, 2, 3)).reshape(2, 1, 128, N)


def solution(mesh):
    fine = Mesh(mesh.devices.reshape(2, 4, 2, 8, 2), DEPTH + ROW)
    return jax.shard_map(
        per_device,
        mesh=fine,
        in_specs=(P(None, DEPTH, ROW, None), P(ROW, None), P(DEPTH)),
        out_specs=P(None, DEPTH, ROW, None),
        check_vma=False,
    )
```

```python
import functools
import math

import jax
import jax.numpy as jnp
import ml_dtypes
import numpy as np
from jax import lax
from jax.experimental import pallas as pl
from jax.experimental.pallas import tpu as pltpu
from jax.sharding import Mesh
from jax.sharding import PartitionSpec as P

tv_step_size = 1.0 / 12.0
tv_sharpness = 0.25

N = 4096
RADIX = 16
INNER = 256
CLASSES = 9
PLANES = 8
LANES = 128
F32 = jnp.float32
BF16 = jnp.bfloat16

DEPTH = ("x_lo", "y")
ROW = ("x_hi", "z", "core")
LAYER = ("x_lo", "y", "x_hi", "core")


def split_table(table):
    high = table.astype(ml_dtypes.bfloat16)
    low = (table - high.astype(np.float64)).astype(ml_dtypes.bfloat16)
    return high, low


def inner_tables():
    index = np.arange(INNER)
    angle = 2.0 * np.pi * (np.outer(index, index) % INNER) / INNER
    cosine, sine = np.cos(angle), np.sin(angle)
    tables = []
    for sign in (1.0, -1.0):
        whole = np.block([[cosine, -sign * sine], [sign * sine, cosine]])
        high, low = split_table(whole)
        tables.append(np.concatenate([high, high, low], axis=0))
    return tables


def twiddles():
    angle = 2.0 * np.pi * np.outer(np.arange(RADIX), np.arange(INNER)) / N
    return np.stack([np.cos(angle), np.sin(angle)]).astype(np.float32)


def class_frequencies():
    return (RADIX * np.arange(INNER)[None, :] + np.arange(CLASSES)[:, None]) % N


def class_tables():
    freq = class_frequencies()
    angle = 2.0 * np.pi * ((freq[:, None, :] * np.arange(INNER)[None, :, None]) % N) / N
    table = np.concatenate([np.cos(angle), np.sin(angle)], axis=2)
    tables = []
    for each in (table, np.swapaxes(table, 1, 2)):
        high, low = split_table(each)
        tables.append(np.concatenate([high, high, low], axis=1))
    return tables


def squares_of(index):
    centred = np.where(index < N // 2, index, index - N)
    return (centred * centred).astype(np.float32)


def dft4(values, inverse):
    (ar, ai), (br, bi), (cr, ci), (dr, di) = values
    s0r, s0i, s1r, s1i = ar + cr, ai + ci, ar - cr, ai - ci
    s2r, s2i, s3r, s3i = br + dr, bi + di, br - dr, bi - di
    plus = (s1r - s3i, s1i + s3r)
    minus = (s1r + s3i, s1i - s3r)
    first, third = (plus, minus) if inverse else (minus, plus)
    return [(s0r + s2r, s0i + s2i), first, (s0r - s2r, s0i - s2i), third]


def times_constant(value, cosine, sine):
    real, imag = value
    if abs(sine) < 1e-9 and abs(cosine - 1.0) < 1e-9:
        return value
    if abs(cosine) < 1e-9 and abs(sine - 1.0) < 1e-9:
        return (-imag, real)
    if abs(cosine) < 1e-9 and abs(sine + 1.0) < 1e-9:
        return (imag, -real)
    if abs(abs(cosine) - abs(sine)) < 1e-9:
        root = math.sqrt(0.5)
        sc, ss = math.copysign(1.0, cosine), math.copysign(1.0, sine)
        first = (real if sc > 0 else -real) - (imag if ss > 0 else -imag)
        second = (imag if sc > 0 else -imag) + (real if ss > 0 else -real)
        return (first * root, second * root)
    return (real * cosine - imag * sine, imag * cosine + real * sine)


def dft16(values, inverse):
    direction = 1.0 if inverse else -1.0
    stage = [dft4([values[4 * n1 + n2] for n1 in range(4)], inverse) for n2 in range(4)]
    result = [None] * 16
    for k1 in range(4):
        column = []
        for n2 in range(4):
            angle = direction * 2.0 * math.pi * n2 * k1 / 16
            column.append(times_constant(stage[n2][k1], math.cos(angle), math.sin(angle)))
        for k2, value in enumerate(dft4(column, inverse)):
            result[k1 + 4 * k2] = value
    return result


def weighted_sum(terms):
    total = None
    for coefficient, value in terms:
        if abs(coefficient) < 1e-9:
            continue
        if abs(coefficient - 1.0) < 1e-9:
            total = value if total is None else total + value
        elif abs(coefficient + 1.0) < 1e-9:
            total = -value if total is None else total - value
        else:
            piece = value * float(np.float32(coefficient))
            total = piece if total is None else total + piece
    return total


def real_dft16(blocks):
    sums = [blocks[0]] + [blocks[b] + blocks[16 - b] for b in range(1, 8)] + [blocks[8]]
    diffs = [None] + [blocks[b] - blocks[16 - b] for b in range(1, 8)]
    result = []
    for k in range(CLASSES):
        real = weighted_sum([(math.cos(2 * math.pi * k * b / 16), sums[b]) for b in range(9)])
        if k in (0, 8):
            imag = jnp.zeros_like(real)
        else:
            imag = weighted_sum(
                [(-math.sin(2 * math.pi * k * b / 16), diffs[b]) for b in range(1, 8)]
            )
        result.append((real, imag))
    return result


def real_inverse16(values):
    result = [None] * 16
    for b in range(9):
        even = weighted_sum([(math.cos(2 * math.pi * k * b / 16), values[k][0]) for k in range(9)])
        if b in (0, 8):
            result[b] = even
        else:
            odd = weighted_sum(
                [(math.sin(2 * math.pi * k * b / 16), values[k][1]) for k in range(1, 8)]
            )
            result[b] = even - odd
            result[16 - b] = even + odd
    return result


def halves(value):
    high = value.astype(BF16)
    low = (value - high.astype(F32)).astype(BF16)
    return high, low


STEP_ROWS = 32
CHUNK_CLASSES = 16


def filter_rows(load, store, tw_ref, d_ref, wf_ref, wi_ref, x_ref):
    groups = [(r, h) for r in range(STEP_ROWS // 8) for h in range(INNER // LANES)]
    for r, h in groups:
        values = [load(r, b * (INNER // LANES) + h) for b in range(RADIX)]
        lanes = slice(h * LANES, (h + 1) * LANES)
        for k, (real, imag) in enumerate(dft16(values, False)):
            if k:
                cosine, sine = tw_ref[0, k : k + 1, lanes], tw_ref[1, k : k + 1, lanes]
                real, imag = real * cosine + imag * sine, imag * cosine - real * sine
            rows = slice(k * STEP_ROWS + 8 * r, k * STEP_ROWS + 8 * r + 8)
            x_ref[rows, lanes] = real
            x_ref[rows, INNER + h * LANES : INNER + (h + 1) * LANES] = imag
    for chunk in range(RADIX // CHUNK_CLASSES):
        base = chunk * CHUNK_CLASSES * STEP_ROWS
        rows = slice(base, base + CHUNK_CLASSES * STEP_ROWS)
        high, low = halves(x_ref[rows, :])
        spectrum = jnp.dot(
            jnp.concatenate([high, low, high], axis=1), wf_ref[...], preferred_element_type=F32
        )
        pieces = []
        for kk in range(CHUNK_CLASSES):
            k = chunk * CHUNK_CLASSES + kk
            cosine, sine = per_row(d_ref[0, k]), per_row(d_ref[1, k])
            real = spectrum[kk * STEP_ROWS : (kk + 1) * STEP_ROWS, :INNER]
            imag = spectrum[kk * STEP_ROWS : (kk + 1) * STEP_ROWS, INNER:]
            pieces.append(
                jnp.concatenate(
                    [real * cosine - imag * sine, imag * cosine + real * sine], axis=1
                )
            )
        high, low = halves(jnp.concatenate(pieces, axis=0))
        x_ref[rows, :] = jnp.dot(
            jnp.concatenate([high, low, high], axis=1), wi_ref[...], preferred_element_type=F32
        )
    for r, h in groups:
        lanes = slice(h * LANES, (h + 1) * LANES)
        values = []
        for k in range(RADIX):
            rows = slice(k * STEP_ROWS + 8 * r, k * STEP_ROWS + 8 * r + 8)
            real = x_ref[rows, lanes]
            imag = x_ref[rows, INNER + h * LANES : INNER + (h + 1) * LANES]
            if k:
                cosine, sine = tw_ref[0, k : k + 1, lanes], tw_ref[1, k : k + 1, lanes]
                real, imag = real * cosine - imag * sine, imag * cosine + real * sine
            values.append((real, imag))
        for b, value in enumerate(dft16(values, True)):
            store(r, b * (INNER // LANES) + h, value)


def per_row(factor):
    if factor.shape[0] == 1:
        return factor
    return jnp.concatenate([factor] * (STEP_ROWS // factor.shape[0]), axis=0)


def forward_x_kernel(f_ref, hol_ref, depth_ref, tw_ref, d_ref, wf_ref, wi_ref, o_ref, x_ref):
    step = pl.program_id(0)

    @pl.when(step == 0)
    def _():
        for j in range(32):
            o_ref[j, 256:272, :] = hol_ref[:, j * LANES : (j + 1) * LANES]
            o_ref[j, 272:280, :] = depth_ref[...]

    def load(r, j):
        rows, lanes = slice(8 * r, 8 * r + 8), slice(j * LANES, (j + 1) * LANES)
        return f_ref[0, rows, lanes], f_ref[1, rows, lanes]

    def store(r, j, value):
        for c in range(2):
            start = pl.multiple_of(step * STEP_ROWS + 128 * c + 8 * r, 8)
            o_ref[j, pl.ds(start, 8), :] = value[c]

    filter_rows(load, store, tw_ref, d_ref, wf_ref, wi_ref, x_ref)


def backward_x_kernel(g_ref, held_ref, tw_ref, d_ref, wf_ref, wi_ref, o_ref, x_ref, f_ref):
    step = pl.program_id(0)

    @pl.when(step == 0)
    def _():
        for c in range(2):
            for p in range(PLANES):
                for j in range(N // LANES):
                    f_ref[c, j, pl.ds(p, 16, stride=PLANES), :] = held_ref[
                        p, c, :, j * LANES : (j + 1) * LANES
                    ]

    def load(r, j):
        rows = slice(8 * r, 8 * r + 8)
        return g_ref[j, 0, rows, :], g_ref[j, 1, rows, :]

    def store(r, j, value):
        rows, lanes = slice(8 * r, 8 * r + 8), slice(j * LANES, (j + 1) * LANES)
        held = pl.ds(pl.multiple_of(step * STEP_ROWS + 8 * r, 8), 8)
        for c in range(2):
            o_ref[c, rows, lanes] = f_ref[c, j, held, :] + value[c]

    filter_rows(load, store, tw_ref, d_ref, wf_ref, wi_ref, x_ref)


def whole(shape):
    return pl.BlockSpec(shape, lambda *_: (0,) * len(shape))


def cost_of(microseconds):
    return pl.CostEstimate(flops=0, bytes_accessed=microseconds * 3_000_000, transcendentals=0)


def params():
    return pltpu.CompilerParams(vmem_limit_bytes=56 << 20)


def x_tables():
    forward, inverse = inner_tables()
    return jnp.asarray(twiddles()), jnp.asarray(forward), jnp.asarray(inverse)


def forward_x(field, hologram_rows, depth_rows, transfer):
    tw, wf, wi = x_tables()
    return pl.pallas_call(
        forward_x_kernel,
        grid=(128 // STEP_ROWS,),
        in_specs=[
            pl.BlockSpec((2, STEP_ROWS, N), lambda i: (0, i, 0)),
            whole((16, N)),
            whole((8, LANES)),
            whole((2, RADIX, INNER)),
            whole((2, RADIX, 1, INNER)),
            whole((1536, 512)),
            whole((1536, 512)),
        ],
        out_specs=whole((32, 280, LANES)),
        out_shape=jax.ShapeDtypeStruct((32, 280, LANES), F32),
        scratch_shapes=[pltpu.VMEM((RADIX * STEP_ROWS, 2 * INNER), F32)],
        compiler_params=params(),
        cost_estimate=cost_of(14),
        name="filter_x_forward",
    )(field, hologram_rows, depth_rows, tw, transfer, wf, wi)


def backward_x(gradient, held, transfer):
    tw, wf, wi = x_tables()
    return pl.pallas_call(
        backward_x_kernel,
        grid=(128 // STEP_ROWS,),
        in_specs=[
            pl.BlockSpec((32, 2, STEP_ROWS, LANES), lambda i: (0, 0, i, 0)),
            whole((PLANES, 2, 16, N)),
            whole((2, RADIX, INNER)),
            whole((2, RADIX, PLANES, INNER)),
            whole((1536, 512)),
            whole((1536, 512)),
        ],
        out_specs=pl.BlockSpec((2, STEP_ROWS, N), lambda i: (0, i, 0)),
        out_shape=jax.ShapeDtypeStruct((2, 128, N), F32),
        scratch_shapes=[
            pltpu.VMEM((RADIX * STEP_ROWS, 2 * INNER), F32),
            pltpu.VMEM((2, N // LANES, 128, LANES), F32),
        ],
        compiler_params=params(),
        cost_estimate=cost_of(16),
        name="filter_x_backward",
    )(gradient, held, tw, transfer, wf, wi)


LAYERS = 8
PART = LANES // LAYERS
LONG = LAYERS // 2
SHORT = LAYERS - 1 - LONG
HOPS = 2 * LONG
TURN_HIGH = 6.28125
TURN_LOW = 2.0 * math.pi - TURN_HIGH


def filter_y_kernel(
    rot_ref,
    g_ref,
    t_ref,
    tt_ref,
    sq_ref,
    o_ref,
    u_ref,
    s_ref,
    h_ref,
    r_ref,
    a_ref,
    cs_ref,
    send_sem,
    recv_sem,
):
    step = pl.program_id(0)
    me = lax.axis_index("z")

    def hop(k, h):
        sign = 1 - 2 * lax.rem(k, 2)

        def block(distance):
            index = lax.rem(me + sign * distance + LAYERS, LAYERS)
            return pl.ds(pl.multiple_of(index * PART, PART), PART)

        def copy(source, target, way, h):
            onward = sign if way == 0 else -sign
            return pltpu.make_async_remote_copy(
                src_ref=source,
                dst_ref=target,
                send_sem=send_sem.at[k, way],
                recv_sem=recv_sem.at[k, way, h],
                device_id={"z": lax.rem(me + onward + LAYERS, LAYERS)},
                device_id_type=pl.DeviceIdType.MESH,
            )

        own = block(0)

        def finish(way):
            last = copy(s_ref.at[k, own, :], r_ref.at[k, 0], way, h - 1)
            last.wait_send()
            last.wait_recv()

        @pl.when(h > 0)
        def _():
            finish(0)

        @pl.when((h > 0) & (h != LONG) & (h != 2 * LONG))
        def _():
            finish(1)

        def reduce(way, length, first_slot, rows):
            @pl.when(h < length)
            def _():
                @pl.when(h > 0)
                def _():
                    s_ref[k, rows, :] += r_ref[k, first_slot + h - 1]

                copy(s_ref.at[k, rows, :], r_ref.at[k, first_slot + h], way, h).start()

        reduce(0, LONG, 0, block(LONG - h))
        reduce(1, SHORT, LONG, block(h - SHORT))

        @pl.when(h == LONG)
        def _():
            h_ref[k, own, :] = (
                s_ref[k, own, :] + r_ref[k, LONG - 1] + r_ref[k, LONG + SHORT - 1]
            )

        def gather(way, length, rows):
            @pl.when((h >= LONG) & (h < LONG + length))
            def _():
                copy(h_ref.at[k, rows, :], h_ref.at[k, rows, :], way, h).start()

        gather(0, LONG, block(LONG - h))
        gather(1, SHORT, block(h - LONG))

    def factor(k, c, p):
        row = cs_ref[k, c, p : p + 1, :]
        return jnp.concatenate([row, row], axis=1)

    def progress(slot):
        @pl.loop(0, CLASSES)
        def _(k):
            h = slot - k

            @pl.when((h >= 0) & (h <= HOPS))
            def _():
                hop(k, h)

    @pl.when(step == 0)
    def _():
        barrier = pltpu.get_barrier_semaphore()
        for distance in (1, LAYERS - 1):
            pl.semaphore_signal(
                barrier,
                inc=1,
                device_id={"z": lax.rem(me + distance, LAYERS)},
                device_id_type=pl.DeviceIdType.MESH,
            )
        pl.semaphore_wait(barrier, 2)

        depths = jnp.concatenate([g_ref[p * 4, 272:273, :] for p in range(PLANES)], axis=0)
        depths = jnp.concatenate([depths, depths], axis=1)

        @pl.loop(0, CLASSES)
        def _(k):
            phase = depths * sq_ref[k]
            whole_turns = jnp.floor(phase * (0.5 / math.pi) + 0.5)
            phase = (phase - whole_turns * TURN_HIGH) - whole_turns * TURN_LOW
            cs_ref[k, 0] = jnp.cos(phase)
            cs_ref[k, 1] = jnp.sin(phase)

        def place(p, lanes, core, upper, lower):
            for parity, value in ((0, upper + lower), (1, upper - lower)):
                high, low = halves(value)
                for part, piece in ((0, high), (1, low), (2, high)):
                    start = part * INNER + core * 128
                    u_ref[parity, p, lanes, start : start + 128] = piece

        @pl.loop(0, PLANES)
        def _(p):
            for core in range(2):
                for c in range(2):
                    rows = slice(c * 128, (c + 1) * 128)
                    upper = g_ref[p * 4 + core, rows, :].T
                    lower = g_ref[p * 4 + 2 + core, rows, :].T
                    place(p, slice(c * LANES, (c + 1) * LANES), core, upper, lower)

        for core in range(2):
            tiles = []
            for upper in range(2):
                rows = [g_ref[p * 4 + upper * 2 + core, 256:272, :] for p in range(PLANES)]
                tiles.append(jnp.concatenate(rows, axis=0).T)
            place(PLANES, slice(0, LANES), core, tiles[0], tiles[1])

    @pl.when(step < CLASSES)
    def _():
        parity = lax.rem(step, 2)

        def planes(first, total):
            for p in range(first, first + PLANES // 2):
                result = jnp.dot(u_ref[parity, p], t_ref[0], preferred_element_type=F32)
                total = (
                    total
                    + factor(step, 0, p) * result[:LANES]
                    + factor(step, 1, p) * result[LANES:]
                )
            return total

        minus = jnp.dot(u_ref[parity, PLANES, :LANES, :], t_ref[0], preferred_element_type=F32)
        total = planes(PLANES // 2, planes(0, -minus))
        cosine, sine = rot_ref[step, 0], rot_ref[step, 1]
        real, imag = total[:, :INNER], total[:, INNER:]
        s_ref[step, :, :INNER] = cosine * real - sine * imag
        s_ref[step, :, INNER:] = cosine * imag + sine * real

    @pl.when(step >= CLASSES)
    def _():
        k = step - CLASSES
        parity = lax.rem(k, 2)
        cosine, sine = rot_ref[k, 2], rot_ref[k, 3]
        real, imag = h_ref[k, :, :INNER], h_ref[k, :, INNER:]
        spectrum = jnp.concatenate(
            [cosine * real + sine * imag, cosine * imag - sine * real], axis=1
        )

        def planes(first):
            for p in range(first, first + PLANES // 2):
                product = jnp.concatenate(
                    [
                        factor(k, 0, p) * spectrum,
                        factor(k, 1, p) * spectrum,
                    ],
                    axis=0,
                )
                high, low = halves(product)
                value = jnp.dot(
                    jnp.concatenate([high, low, high], axis=1),
                    tt_ref[0],
                    preferred_element_type=F32,
                )
                a_ref[parity, p] = jnp.where(k < 2, value, a_ref[parity, p] + value)

        planes(0)
        planes(PLANES // 2)

    progress(step)

    @pl.when(step == 2 * CLASSES - 1)
    def _():
        @pl.loop(0, PLANES)
        def _(p):
            for core in range(2):
                lanes = slice(core * 128, (core + 1) * 128)
                for c in range(2):
                    rows = slice(c * LANES, (c + 1) * LANES)
                    even, odd = a_ref[0, p, rows, lanes], a_ref[1, p, rows, lanes]
                    upper, lower = (even + odd).T, (even - odd).T
                    for owner in range(PLANES):
                        part = slice(owner * 16, owner * 16 + 16)
                        held = pl.ds(p, 16, stride=PLANES)
                        o_ref[owner * 4 + core, c, held, :] = upper[part]
                        o_ref[owner * 4 + 2 + core, c, held, :] = lower[part]


def filter_y(rotations, received):
    forward, backward = class_tables()
    last = CLASSES - 1
    squares = squares_of(class_frequencies())[:, None, :] * np.float32(math.pi / (N * N))
    squares = jnp.asarray(np.repeat(squares, PLANES, axis=1))
    return pl.pallas_call(
        filter_y_kernel,
        grid=(2 * CLASSES,),
        in_specs=[
            pl.BlockSpec(memory_space=pltpu.SMEM),
            whole((32, 280, LANES)),
            pl.BlockSpec((1, 768, 512), lambda i: (jnp.minimum(i, last), 0, 0)),
            pl.BlockSpec((1, 1536, 256), lambda i: (jnp.maximum(i - CLASSES, 0), 0, 0)),
            whole((CLASSES, PLANES, INNER)),
        ],
        out_specs=whole((32, 2, 128, LANES)),
        out_shape=jax.ShapeDtypeStruct((32, 2, 128, LANES), F32),
        scratch_shapes=[
            pltpu.VMEM((2, PLANES + 1, 2 * LANES, 768), BF16),
            pltpu.VMEM((CLASSES, LANES, 2 * INNER), F32),
            pltpu.VMEM((CLASSES, LANES, 2 * INNER), F32),
            pltpu.VMEM((CLASSES, LONG + SHORT, PART, 2 * INNER), F32),
            pltpu.VMEM((2, PLANES, 2 * LANES, INNER), F32),
            pltpu.VMEM((CLASSES, 2, PLANES, INNER), F32),
            pltpu.SemaphoreType.DMA((CLASSES, 2)),
            pltpu.SemaphoreType.DMA((CLASSES, 2, HOPS)),
        ],
        compiler_params=pltpu.CompilerParams(
            collective_id=0, has_side_effects=True, vmem_limit_bytes=56 << 20
        ),
        cost_estimate=cost_of(90),
        name="filter_y",
    )(rotations, received, jnp.asarray(forward), jnp.asarray(backward), squares)


TV_ROWS = 8


def shrink_kernel(edge_ref, m_ref, next_ref, above_ref, below_ref, o_ref, e_ref, prior_ref):
    step = pl.program_id(0)
    plane = lax.broadcasted_iota(jnp.int32, (PLANES, N), 0)
    column = lax.broadcasted_iota(jnp.int32, (PLANES, N), 1)
    last_plane, first_plane = plane == PLANES - 1, plane == 0
    last_column, first_column = column == N - 1, column == 0

    def flux(here, below):
        squares = None
        diffs = []
        for c in range(2):
            depth = jnp.where(last_plane, 0.0, pltpu.roll(here[c], PLANES - 1, 0) - here[c])
            row = below[c] - here[c]
            col = jnp.where(last_column, 0.0, pltpu.roll(here[c], N - 1, 1) - here[c])
            diffs.append((depth, row, col))
            term = depth * depth + row * row + col * col
            squares = term if squares is None else squares + term
        factor = 1.0 / (1.0 + tv_sharpness * jnp.sqrt(squares))
        return [tuple(d * factor for d in triple) for triple in diffs]

    @pl.when(step == 0)
    def _():
        above = [above_ref[c] for c in range(2)]
        first = [m_ref[c, :PLANES, :] for c in range(2)]
        terms = flux(above, first)
        for c in range(2):
            prior_ref[c] = jnp.where(edge_ref[0] > 0, terms[c][1], 0.0)

    def row_at(t):
        rows = pl.ds(pl.multiple_of(t * PLANES, PLANES), PLANES)
        return [m_ref[c, rows, :] for c in range(2)]

    def emit(t, here, below):
        terms = flux(here, below)
        rows = pl.ds(pl.multiple_of(t * PLANES, PLANES), PLANES)
        for c in range(2):
            depth, row, col = terms[c]
            divergence = (
                (depth - jnp.where(first_plane, 0.0, pltpu.roll(depth, 1, 0)))
                + (row - prior_ref[c])
                + (col - jnp.where(first_column, 0.0, pltpu.roll(col, 1, 1)))
            )
            prior_ref[c] = row
            estimate = here[c] + tv_step_size * divergence
            for j in range(N // LANES):
                e_ref[c, j, rows, :] = estimate[:, j * LANES : (j + 1) * LANES]

    @pl.loop(0, TV_ROWS - 1)
    def _(t):
        emit(t, row_at(t), row_at(t + 1))

    here = row_at(TV_ROWS - 1)
    final = step == 16 // TV_ROWS - 1
    below = []
    for c in range(2):
        beyond = jnp.where(edge_ref[1] > 0, below_ref[c], here[c])
        below.append(jnp.where(final, beyond, next_ref[c]))
    emit(TV_ROWS - 1, here, below)
    for p in range(PLANES):
        for c in range(2):
            for j in range(N // LANES):
                held = pl.ds(p, TV_ROWS, stride=PLANES)
                o_ref[p, c, :, j * LANES : (j + 1) * LANES] = e_ref[c, j, held, :]


def shrink(edges, moved, above, below):
    steps = 16 // TV_ROWS
    return pl.pallas_call(
        shrink_kernel,
        grid=(steps,),
        in_specs=[
            pl.BlockSpec(memory_space=pltpu.SMEM),
            pl.BlockSpec((2, TV_ROWS * PLANES, N), lambda i: (0, i, 0)),
            pl.BlockSpec((2, PLANES, N), lambda i: (0, jnp.minimum((i + 1) * TV_ROWS, 15), 0)),
            whole((2, PLANES, N)),
            whole((2, PLANES, N)),
        ],
        out_specs=pl.BlockSpec((PLANES, 2, TV_ROWS, N), lambda i: (0, 0, i, 0)),
        out_shape=jax.ShapeDtypeStruct((PLANES, 2, 16, N), F32),
        scratch_shapes=[
            pltpu.VMEM((2, N // LANES, TV_ROWS * PLANES, LANES), F32),
            pltpu.VMEM((2, PLANES, N), F32),
        ],
        compiler_params=params(),
        cost_estimate=cost_of(9),
        name="tv_shrink",
    )(edges, moved, moved, above, below)


def along_rows(block, distance):
    place = lambda line: (line % 8) * 32 + line // 8
    route = [
        (place(line - distance), place(line)) for line in range(256) if 0 <= line - distance < 256
    ]
    return lax.ppermute(block, DEPTH + ROW, route)


def phase_of(depth_values, squares):
    return depth_values * (squares * (math.pi / (N * N)))


def per_device(field, hologram, defocus):
    x_lo, y = lax.axis_index("x_lo"), lax.axis_index("y")
    x_hi, z, core = lax.axis_index("x_hi"), lax.axis_index("z"), lax.axis_index("core")
    depth_index = x_lo * 4 + y
    row_index = x_hi * 16 + z * 2 + core
    field = field[:, 0]

    x_freq = RADIX * np.arange(INNER)[None, :] + np.arange(RADIX)[:, None]
    x_squares = jnp.asarray(squares_of(x_freq))[:, None, :]
    x_phase = phase_of(defocus[0], x_squares)
    x_forward = jnp.stack([jnp.cos(x_phase) / N, -jnp.sin(x_phase) / N])

    weights = np.full((CLASSES,), 2.0 / N, np.float32)
    weights[0] = weights[8] = 1.0 / N
    turns = lax.rem(z * np.arange(CLASSES, dtype=np.int32), RADIX).astype(F32)
    turns = turns * (2.0 * math.pi / RADIX)
    cosine, sine = jnp.cos(turns), jnp.sin(turns)
    rotations = jnp.stack([weights * cosine, weights * sine, cosine, sine], axis=1)

    hologram_rows = lax.dynamic_slice_in_dim(hologram, depth_index * 16, 16, 0)
    depth_rows = jnp.full((8, LANES), defocus[0])
    sent = forward_x(field, hologram_rows, depth_rows, x_forward)
    held = jnp.transpose(field.reshape(2, PLANES, 16, N), (1, 0, 2, 3))
    received = lax.all_to_all(sent, LAYER, 0, 0, tiled=True)
    held, received, rotations = lax.optimization_barrier((held, received, rotations))
    held = lax.all_to_all(held, DEPTH, 0, 0, tiled=True)
    depths = received[::4, 272, 0]
    sent = filter_y(rotations, received)
    x_phase = phase_of(depths[None, :, None], x_squares)
    x_backward = jnp.stack([jnp.cos(x_phase), jnp.sin(x_phase)]) * (-1.0 / (PLANES * N))
    received = lax.all_to_all(sent, LAYER, 0, 0, tiled=True)
    moved = backward_x(received, held, x_backward)
    above = along_rows(moved[:, 120:], 1)
    below = along_rows(moved[:, :8], -1)
    line = row_index * 8 + depth_index
    edges = jnp.stack([line > 0, line < 255]).astype(jnp.int32)
    estimate = shrink(edges, moved, above, below)
    estimate = lax.all_to_all(estimate, DEPTH, 0, 0, tiled=True)
    return jnp.transpose(estimate, (1, 0, 2, 3)).reshape(2, 1, 128, N)


def solution(mesh):
    fine = Mesh(mesh.devices.reshape(2, 4, 2, 8, 2), DEPTH + ROW)
    return jax.shard_map(
        per_device,
        mesh=fine,
        in_specs=(P(None, DEPTH, ROW, None), P(ROW, None), P(DEPTH)),
        out_specs=P(None, DEPTH, ROW, None),
        check_vma=False,
    )
```

```python
import functools
import math

import jax
import jax.numpy as jnp
import ml_dtypes
import numpy as np
from jax import lax
from jax.experimental import pallas as pl
from jax.experimental.pallas import tpu as pltpu
from jax.sharding import Mesh
from jax.sharding import PartitionSpec as P

tv_step_size = 1.0 / 12.0
tv_sharpness = 0.25

N = 4096
RADIX = 16
INNER = 256
CLASSES = 9
PLANES = 8
LANES = 128
F32 = jnp.float32
BF16 = jnp.bfloat16

DEPTH = ("x_lo", "y")
ROW = ("x_hi", "z", "core")
LAYER = ("x_lo", "y", "x_hi", "core")


def split_table(table):
    high = table.astype(ml_dtypes.bfloat16)
    low = (table - high.astype(np.float64)).astype(ml_dtypes.bfloat16)
    return high, low


def inner_tables():
    index = np.arange(INNER)
    angle = 2.0 * np.pi * (np.outer(index, index) % INNER) / INNER
    cosine, sine = np.cos(angle), np.sin(angle)
    tables = []
    for sign in (1.0, -1.0):
        whole = np.block([[cosine, -sign * sine], [sign * sine, cosine]])
        high, low = split_table(whole)
        tables.append(np.concatenate([high, high, low], axis=0))
    return tables


def twiddles():
    angle = 2.0 * np.pi * np.outer(np.arange(RADIX), np.arange(INNER)) / N
    return np.stack([np.cos(angle), np.sin(angle)]).astype(np.float32)


def class_frequencies():
    return (RADIX * np.arange(INNER)[None, :] + np.arange(CLASSES)[:, None]) % N


def class_tables():
    freq = class_frequencies()
    angle = 2.0 * np.pi * ((freq[:, None, :] * np.arange(INNER)[None, :, None]) % N) / N
    table = np.concatenate([np.cos(angle), np.sin(angle)], axis=2)
    tables = []
    for each in (table, np.swapaxes(table, 1, 2)):
        high, low = split_table(each)
        tables.append(np.concatenate([high, high, low], axis=1))
    return tables


def squares_of(index):
    centred = np.where(index < N // 2, index, index - N)
    return (centred * centred).astype(np.float32)


def dft4(values, inverse):
    (ar, ai), (br, bi), (cr, ci), (dr, di) = values
    s0r, s0i, s1r, s1i = ar + cr, ai + ci, ar - cr, ai - ci
    s2r, s2i, s3r, s3i = br + dr, bi + di, br - dr, bi - di
    plus = (s1r - s3i, s1i + s3r)
    minus = (s1r + s3i, s1i - s3r)
    first, third = (plus, minus) if inverse else (minus, plus)
    return [(s0r + s2r, s0i + s2i), first, (s0r - s2r, s0i - s2i), third]


def times_constant(value, cosine, sine):
    real, imag = value
    if abs(sine) < 1e-9 and abs(cosine - 1.0) < 1e-9:
        return value
    if abs(cosine) < 1e-9 and abs(sine - 1.0) < 1e-9:
        return (-imag, real)
    if abs(cosine) < 1e-9 and abs(sine + 1.0) < 1e-9:
        return (imag, -real)
    if abs(abs(cosine) - abs(sine)) < 1e-9:
        root = math.sqrt(0.5)
        sc, ss = math.copysign(1.0, cosine), math.copysign(1.0, sine)
        first = (real if sc > 0 else -real) - (imag if ss > 0 else -imag)
        second = (imag if sc > 0 else -imag) + (real if ss > 0 else -real)
        return (first * root, second * root)
    return (real * cosine - imag * sine, imag * cosine + real * sine)


def dft16(values, inverse):
    direction = 1.0 if inverse else -1.0
    stage = [dft4([values[4 * n1 + n2] for n1 in range(4)], inverse) for n2 in range(4)]
    result = [None] * 16
    for k1 in range(4):
        column = []
        for n2 in range(4):
            angle = direction * 2.0 * math.pi * n2 * k1 / 16
            column.append(times_constant(stage[n2][k1], math.cos(angle), math.sin(angle)))
        for k2, value in enumerate(dft4(column, inverse)):
            result[k1 + 4 * k2] = value
    return result


def weighted_sum(terms):
    total = None
    for coefficient, value in terms:
        if abs(coefficient) < 1e-9:
            continue
        if abs(coefficient - 1.0) < 1e-9:
            total = value if total is None else total + value
        elif abs(coefficient + 1.0) < 1e-9:
            total = -value if total is None else total - value
        else:
            piece = value * float(np.float32(coefficient))
            total = piece if total is None else total + piece
    return total


def real_dft16(blocks):
    sums = [blocks[0]] + [blocks[b] + blocks[16 - b] for b in range(1, 8)] + [blocks[8]]
    diffs = [None] + [blocks[b] - blocks[16 - b] for b in range(1, 8)]
    result = []
    for k in range(CLASSES):
        real = weighted_sum([(math.cos(2 * math.pi * k * b / 16), sums[b]) for b in range(9)])
        if k in (0, 8):
            imag = jnp.zeros_like(real)
        else:
            imag = weighted_sum(
                [(-math.sin(2 * math.pi * k * b / 16), diffs[b]) for b in range(1, 8)]
            )
        result.append((real, imag))
    return result


def real_inverse16(values):
    result = [None] * 16
    for b in range(9):
        even = weighted_sum([(math.cos(2 * math.pi * k * b / 16), values[k][0]) for k in range(9)])
        if b in (0, 8):
            result[b] = even
        else:
            odd = weighted_sum(
                [(math.sin(2 * math.pi * k * b / 16), values[k][1]) for k in range(1, 8)]
            )
            result[b] = even - odd
            result[16 - b] = even + odd
    return result


def halves(value):
    high = value.astype(BF16)
    low = (value - high.astype(F32)).astype(BF16)
    return high, low


STEP_ROWS = 32
CHUNK_CLASSES = 16


def filter_rows(load, store, tw_ref, d_ref, wf_ref, wi_ref, x_ref):
    groups = [(r, h) for r in range(STEP_ROWS // 8) for h in range(INNER // LANES)]
    for r, h in groups:
        values = [load(r, b * (INNER // LANES) + h) for b in range(RADIX)]
        lanes = slice(h * LANES, (h + 1) * LANES)
        for k, (real, imag) in enumerate(dft16(values, False)):
            if k:
                cosine, sine = tw_ref[0, k : k + 1, lanes], tw_ref[1, k : k + 1, lanes]
                real, imag = real * cosine + imag * sine, imag * cosine - real * sine
            rows = slice(k * STEP_ROWS + 8 * r, k * STEP_ROWS + 8 * r + 8)
            x_ref[rows, lanes] = real
            x_ref[rows, INNER + h * LANES : INNER + (h + 1) * LANES] = imag
    for chunk in range(RADIX // CHUNK_CLASSES):
        base = chunk * CHUNK_CLASSES * STEP_ROWS
        rows = slice(base, base + CHUNK_CLASSES * STEP_ROWS)
        high, low = halves(x_ref[rows, :])
        spectrum = jnp.dot(
            jnp.concatenate([high, low, high], axis=1), wf_ref[...], preferred_element_type=F32
        )
        pieces = []
        for kk in range(CHUNK_CLASSES):
            k = chunk * CHUNK_CLASSES + kk
            cosine, sine = per_row(d_ref[0, k]), per_row(d_ref[1, k])
            real = spectrum[kk * STEP_ROWS : (kk + 1) * STEP_ROWS, :INNER]
            imag = spectrum[kk * STEP_ROWS : (kk + 1) * STEP_ROWS, INNER:]
            pieces.append(
                jnp.concatenate(
                    [real * cosine - imag * sine, imag * cosine + real * sine], axis=1
                )
            )
        high, low = halves(jnp.concatenate(pieces, axis=0))
        x_ref[rows, :] = jnp.dot(
            jnp.concatenate([high, low, high], axis=1), wi_ref[...], preferred_element_type=F32
        )
    for r, h in groups:
        lanes = slice(h * LANES, (h + 1) * LANES)
        values = []
        for k in range(RADIX):
            rows = slice(k * STEP_ROWS + 8 * r, k * STEP_ROWS + 8 * r + 8)
            real = x_ref[rows, lanes]
            imag = x_ref[rows, INNER + h * LANES : INNER + (h + 1) * LANES]
            if k:
                cosine, sine = tw_ref[0, k : k + 1, lanes], tw_ref[1, k : k + 1, lanes]
                real, imag = real * cosine - imag * sine, imag * cosine + real * sine
            values.append((real, imag))
        for b, value in enumerate(dft16(values, True)):
            store(r, b * (INNER // LANES) + h, value)


def per_row(factor):
    if factor.shape[0] == 1:
        return factor
    return jnp.concatenate([factor] * (STEP_ROWS // factor.shape[0]), axis=0)


def forward_x_kernel(f_ref, hol_ref, depth_ref, tw_ref, d_ref, wf_ref, wi_ref, o_ref, x_ref):
    step = pl.program_id(0)

    @pl.when(step == 0)
    def _():
        for j in range(32):
            o_ref[j, 256:272, :] = hol_ref[:, j * LANES : (j + 1) * LANES]
            o_ref[j, 272:280, :] = depth_ref[...]

    def load(r, j):
        rows, lanes = slice(8 * r, 8 * r + 8), slice(j * LANES, (j + 1) * LANES)
        return f_ref[0, rows, lanes], f_ref[1, rows, lanes]

    def store(r, j, value):
        for c in range(2):
            start = pl.multiple_of(step * STEP_ROWS + 128 * c + 8 * r, 8)
            o_ref[j, pl.ds(start, 8), :] = value[c]

    filter_rows(load, store, tw_ref, d_ref, wf_ref, wi_ref, x_ref)


def backward_x_kernel(g_ref, held_ref, tw_ref, d_ref, wf_ref, wi_ref, o_ref, x_ref, f_ref):
    step = pl.program_id(0)

    @pl.when(step == 0)
    def _():
        for c in range(2):
            for p in range(PLANES):
                for j in range(N // LANES):
                    f_ref[c, j, pl.ds(p, 16, stride=PLANES), :] = held_ref[
                        p, c, :, j * LANES : (j + 1) * LANES
                    ]

    def load(r, j):
        rows = slice(8 * r, 8 * r + 8)
        return g_ref[j, 0, rows, :], g_ref[j, 1, rows, :]

    def store(r, j, value):
        rows, lanes = slice(8 * r, 8 * r + 8), slice(j * LANES, (j + 1) * LANES)
        held = pl.ds(pl.multiple_of(step * STEP_ROWS + 8 * r, 8), 8)
        for c in range(2):
            o_ref[c, rows, lanes] = f_ref[c, j, held, :] + value[c]

    filter_rows(load, store, tw_ref, d_ref, wf_ref, wi_ref, x_ref)


def whole(shape):
    return pl.BlockSpec(shape, lambda *_: (0,) * len(shape))


def cost_of(microseconds):
    return pl.CostEstimate(flops=0, bytes_accessed=microseconds * 3_000_000, transcendentals=0)


def params():
    return pltpu.CompilerParams(vmem_limit_bytes=56 << 20)


def x_tables():
    forward, inverse = inner_tables()
    return jnp.asarray(twiddles()), jnp.asarray(forward), jnp.asarray(inverse)


def forward_x(field, hologram_rows, depth_rows, transfer):
    tw, wf, wi = x_tables()
    return pl.pallas_call(
        forward_x_kernel,
        grid=(128 // STEP_ROWS,),
        in_specs=[
            pl.BlockSpec((2, STEP_ROWS, N), lambda i: (0, i, 0)),
            whole((16, N)),
            whole((8, LANES)),
            whole((2, RADIX, INNER)),
            whole((2, RADIX, 1, INNER)),
            whole((1536, 512)),
            whole((1536, 512)),
        ],
        out_specs=whole((32, 280, LANES)),
        out_shape=jax.ShapeDtypeStruct((32, 280, LANES), F32),
        scratch_shapes=[pltpu.VMEM((RADIX * STEP_ROWS, 2 * INNER), F32)],
        compiler_params=params(),
        cost_estimate=cost_of(14),
        name="filter_x_forward",
    )(field, hologram_rows, depth_rows, tw, transfer, wf, wi)


def backward_x(gradient, held, transfer):
    tw, wf, wi = x_tables()
    return pl.pallas_call(
        backward_x_kernel,
        grid=(128 // STEP_ROWS,),
        in_specs=[
            pl.BlockSpec((32, 2, STEP_ROWS, LANES), lambda i: (0, 0, i, 0)),
            whole((PLANES, 2, 16, N)),
            whole((2, RADIX, INNER)),
            whole((2, RADIX, PLANES, INNER)),
            whole((1536, 512)),
            whole((1536, 512)),
        ],
        out_specs=pl.BlockSpec((2, STEP_ROWS, N), lambda i: (0, i, 0)),
        out_shape=jax.ShapeDtypeStruct((2, 128, N), F32),
        scratch_shapes=[
            pltpu.VMEM((RADIX * STEP_ROWS, 2 * INNER), F32),
            pltpu.VMEM((2, N // LANES, 128, LANES), F32),
        ],
        compiler_params=params(),
        cost_estimate=cost_of(16),
        name="filter_x_backward",
    )(gradient, held, tw, transfer, wf, wi)


LAYERS = 8
PART = LANES // LAYERS
LONG = LAYERS // 2
SHORT = LAYERS - 1 - LONG
HOPS = 2 * LONG
TURN_HIGH = 6.28125
TURN_LOW = 2.0 * math.pi - TURN_HIGH


def filter_y_kernel(
    rot_ref,
    g_ref,
    t_ref,
    tt_ref,
    sq_ref,
    o_ref,
    u_ref,
    s_ref,
    h_ref,
    r_ref,
    a_ref,
    cs_ref,
    send_sem,
    recv_sem,
):
    step = pl.program_id(0)
    me = lax.axis_index("z")

    def hop(k, h):
        sign = 1 - 2 * lax.rem(k, 2)

        def block(distance):
            index = lax.rem(me + sign * distance + LAYERS, LAYERS)
            return pl.ds(pl.multiple_of(index * PART, PART), PART)

        def copy(source, target, way, h):
            onward = sign if way == 0 else -sign
            return pltpu.make_async_remote_copy(
                src_ref=source,
                dst_ref=target,
                send_sem=send_sem.at[k, way],
                recv_sem=recv_sem.at[k, way, h],
                device_id={"z": lax.rem(me + onward + LAYERS, LAYERS)},
                device_id_type=pl.DeviceIdType.MESH,
            )

        own = block(0)

        def finish(way):
            last = copy(s_ref.at[k, own, :], r_ref.at[k, 0], way, h - 1)
            last.wait_send()
            last.wait_recv()

        @pl.when(h > 0)
        def _():
            finish(0)

        @pl.when((h > 0) & (h != LONG) & (h != 2 * LONG))
        def _():
            finish(1)

        def reduce(way, length, first_slot, rows):
            @pl.when(h < length)
            def _():
                @pl.when(h > 0)
                def _():
                    s_ref[k, rows, :] += r_ref[k, first_slot + h - 1]

                copy(s_ref.at[k, rows, :], r_ref.at[k, first_slot + h], way, h).start()

        reduce(0, LONG, 0, block(LONG - h))
        reduce(1, SHORT, LONG, block(h - SHORT))

        @pl.when(h == LONG)
        def _():
            h_ref[k, own, :] = (
                s_ref[k, own, :] + r_ref[k, LONG - 1] + r_ref[k, LONG + SHORT - 1]
            )

        def gather(way, length, rows):
            @pl.when((h >= LONG) & (h < LONG + length))
            def _():
                copy(h_ref.at[k, rows, :], h_ref.at[k, rows, :], way, h).start()

        gather(0, LONG, block(LONG - h))
        gather(1, SHORT, block(h - LONG))

    def factor(k, c, p):
        row = cs_ref[k, c, p : p + 1, :]
        return jnp.concatenate([row, row], axis=1)

    def progress(slot):
        @pl.loop(0, CLASSES)
        def _(i):
            k = CLASSES - 1 - i
            h = slot - k

            @pl.when((h >= 0) & (h <= HOPS))
            def _():
                hop(k, h)

    @pl.when(step == 0)
    def _():
        barrier = pltpu.get_barrier_semaphore()
        for distance in (1, LAYERS - 1):
            pl.semaphore_signal(
                barrier,
                inc=1,
                device_id={"z": lax.rem(me + distance, LAYERS)},
                device_id_type=pl.DeviceIdType.MESH,
            )
        pl.semaphore_wait(barrier, 2)

        depths = jnp.concatenate([g_ref[p * 4, 272:273, :] for p in range(PLANES)], axis=0)
        depths = jnp.concatenate([depths, depths], axis=1)

        @pl.loop(0, CLASSES)
        def _(k):
            phase = depths * sq_ref[k]
            whole_turns = jnp.floor(phase * (0.5 / math.pi) + 0.5)
            phase = (phase - whole_turns * TURN_HIGH) - whole_turns * TURN_LOW
            cs_ref[k, 0] = jnp.cos(phase)
            cs_ref[k, 1] = jnp.sin(phase)

        def place(p, lanes, core, upper, lower):
            for parity, value in ((0, upper + lower), (1, upper - lower)):
                high, low = halves(value)
                for part, piece in ((0, high), (1, low), (2, high)):
                    start = part * INNER + core * 128
                    u_ref[parity, p, lanes, start : start + 128] = piece

        @pl.loop(0, PLANES)
        def _(p):
            for core in range(2):
                for c in range(2):
                    rows = slice(c * 128, (c + 1) * 128)
                    upper = g_ref[p * 4 + core, rows, :].T
                    lower = g_ref[p * 4 + 2 + core, rows, :].T
                    place(p, slice(c * LANES, (c + 1) * LANES), core, upper, lower)

        for core in range(2):
            tiles = []
            for upper in range(2):
                rows = [g_ref[p * 4 + upper * 2 + core, 256:272, :] for p in range(PLANES)]
                tiles.append(jnp.concatenate(rows, axis=0).T)
            place(PLANES, slice(0, LANES), core, tiles[0], tiles[1])

    @pl.when(step < CLASSES)
    def _():
        parity = lax.rem(step, 2)

        def planes(first, total):
            for p in range(first, first + PLANES // 2):
                result = jnp.dot(u_ref[parity, p], t_ref[0], preferred_element_type=F32)
                total = (
                    total
                    + factor(step, 0, p) * result[:LANES]
                    + factor(step, 1, p) * result[LANES:]
                )
            return total

        minus = jnp.dot(u_ref[parity, PLANES, :LANES, :], t_ref[0], preferred_element_type=F32)
        total = planes(PLANES // 2, planes(0, -minus))
        cosine, sine = rot_ref[step, 0], rot_ref[step, 1]
        real, imag = total[:, :INNER], total[:, INNER:]
        s_ref[step, :, :INNER] = cosine * real - sine * imag
        s_ref[step, :, INNER:] = cosine * imag + sine * real

    @pl.when(step >= CLASSES)
    def _():
        k = step - CLASSES
        parity = lax.rem(k, 2)
        cosine, sine = rot_ref[k, 2], rot_ref[k, 3]
        real, imag = h_ref[k, :, :INNER], h_ref[k, :, INNER:]
        spectrum = jnp.concatenate(
            [cosine * real + sine * imag, cosine * imag - sine * real], axis=1
        )

        def planes(first):
            for p in range(first, first + PLANES // 2):
                product = jnp.concatenate(
                    [
                        factor(k, 0, p) * spectrum,
                        factor(k, 1, p) * spectrum,
                    ],
                    axis=0,
                )
                high, low = halves(product)
                value = jnp.dot(
                    jnp.concatenate([high, low, high], axis=1),
                    tt_ref[0],
                    preferred_element_type=F32,
                )
                a_ref[parity, p] = jnp.where(k < 2, value, a_ref[parity, p] + value)

        planes(0)
        planes(PLANES // 2)

    progress(step)

    @pl.when(step == 2 * CLASSES - 1)
    def _():
        @pl.loop(0, PLANES)
        def _(p):
            for core in range(2):
                lanes = slice(core * 128, (core + 1) * 128)
                for c in range(2):
                    rows = slice(c * LANES, (c + 1) * LANES)
                    even, odd = a_ref[0, p, rows, lanes], a_ref[1, p, rows, lanes]
                    upper, lower = (even + odd).T, (even - odd).T
                    for owner in range(PLANES):
                        part = slice(owner * 16, owner * 16 + 16)
                        held = pl.ds(p, 16, stride=PLANES)
                        o_ref[owner * 4 + core, c, held, :] = upper[part]
                        o_ref[owner * 4 + 2 + core, c, held, :] = lower[part]


def filter_y(rotations, received):
    forward, backward = class_tables()
    last = CLASSES - 1
    squares = squares_of(class_frequencies())[:, None, :] * np.float32(math.pi / (N * N))
    squares = jnp.asarray(np.repeat(squares, PLANES, axis=1))
    return pl.pallas_call(
        filter_y_kernel,
        grid=(2 * CLASSES,),
        in_specs=[
            pl.BlockSpec(memory_space=pltpu.SMEM),
            whole((32, 280, LANES)),
            pl.BlockSpec((1, 768, 512), lambda i: (jnp.minimum(i, last), 0, 0)),
            pl.BlockSpec((1, 1536, 256), lambda i: (jnp.maximum(i - CLASSES, 0), 0, 0)),
            whole((CLASSES, PLANES, INNER)),
        ],
        out_specs=whole((32, 2, 128, LANES)),
        out_shape=jax.ShapeDtypeStruct((32, 2, 128, LANES), F32),
        scratch_shapes=[
            pltpu.VMEM((2, PLANES + 1, 2 * LANES, 768), BF16),
            pltpu.VMEM((CLASSES, LANES, 2 * INNER), F32),
            pltpu.VMEM((CLASSES, LANES, 2 * INNER), F32),
            pltpu.VMEM((CLASSES, LONG + SHORT, PART, 2 * INNER), F32),
            pltpu.VMEM((2, PLANES, 2 * LANES, INNER), F32),
            pltpu.VMEM((CLASSES, 2, PLANES, INNER), F32),
            pltpu.SemaphoreType.DMA((CLASSES, 2)),
            pltpu.SemaphoreType.DMA((CLASSES, 2, HOPS)),
        ],
        compiler_params=pltpu.CompilerParams(
            collective_id=0, has_side_effects=True, vmem_limit_bytes=56 << 20
        ),
        cost_estimate=cost_of(90),
        name="filter_y",
    )(rotations, received, jnp.asarray(forward), jnp.asarray(backward), squares)


TV_ROWS = 8


def shrink_kernel(edge_ref, m_ref, next_ref, above_ref, below_ref, o_ref, e_ref, prior_ref):
    step = pl.program_id(0)
    plane = lax.broadcasted_iota(jnp.int32, (PLANES, N), 0)
    column = lax.broadcasted_iota(jnp.int32, (PLANES, N), 1)
    last_plane, first_plane = plane == PLANES - 1, plane == 0
    last_column, first_column = column == N - 1, column == 0

    def flux(here, below):
        squares = None
        diffs = []
        for c in range(2):
            depth = jnp.where(last_plane, 0.0, pltpu.roll(here[c], PLANES - 1, 0) - here[c])
            row = below[c] - here[c]
            col = jnp.where(last_column, 0.0, pltpu.roll(here[c], N - 1, 1) - here[c])
            diffs.append((depth, row, col))
            term = depth * depth + row * row + col * col
            squares = term if squares is None else squares + term
        factor = 1.0 / (1.0 + tv_sharpness * jnp.sqrt(squares))
        return [tuple(d * factor for d in triple) for triple in diffs]

    @pl.when(step == 0)
    def _():
        above = [above_ref[c] for c in range(2)]
        first = [m_ref[c, :PLANES, :] for c in range(2)]
        terms = flux(above, first)
        for c in range(2):
            prior_ref[c] = jnp.where(edge_ref[0] > 0, terms[c][1], 0.0)

    def row_at(t):
        rows = pl.ds(pl.multiple_of(t * PLANES, PLANES), PLANES)
        return [m_ref[c, rows, :] for c in range(2)]

    def emit(t, here, below):
        terms = flux(here, below)
        rows = pl.ds(pl.multiple_of(t * PLANES, PLANES), PLANES)
        for c in range(2):
            depth, row, col = terms[c]
            divergence = (
                (depth - jnp.where(first_plane, 0.0, pltpu.roll(depth, 1, 0)))
                + (row - prior_ref[c])
                + (col - jnp.where(first_column, 0.0, pltpu.roll(col, 1, 1)))
            )
            prior_ref[c] = row
            estimate = here[c] + tv_step_size * divergence
            for j in range(N // LANES):
                e_ref[c, j, rows, :] = estimate[:, j * LANES : (j + 1) * LANES]

    @pl.loop(0, TV_ROWS - 1)
    def _(t):
        emit(t, row_at(t), row_at(t + 1))

    here = row_at(TV_ROWS - 1)
    final = step == 16 // TV_ROWS - 1
    below = []
    for c in range(2):
        beyond = jnp.where(edge_ref[1] > 0, below_ref[c], here[c])
        below.append(jnp.where(final, beyond, next_ref[c]))
    emit(TV_ROWS - 1, here, below)
    for p in range(PLANES):
        for c in range(2):
            for j in range(N // LANES):
                held = pl.ds(p, TV_ROWS, stride=PLANES)
                o_ref[p, c, :, j * LANES : (j + 1) * LANES] = e_ref[c, j, held, :]


def shrink(edges, moved, above, below):
    steps = 16 // TV_ROWS
    return pl.pallas_call(
        shrink_kernel,
        grid=(steps,),
        in_specs=[
            pl.BlockSpec(memory_space=pltpu.SMEM),
            pl.BlockSpec((2, TV_ROWS * PLANES, N), lambda i: (0, i, 0)),
            pl.BlockSpec((2, PLANES, N), lambda i: (0, jnp.minimum((i + 1) * TV_ROWS, 15), 0)),
            whole((2, PLANES, N)),
            whole((2, PLANES, N)),
        ],
        out_specs=pl.BlockSpec((PLANES, 2, TV_ROWS, N), lambda i: (0, 0, i, 0)),
        out_shape=jax.ShapeDtypeStruct((PLANES, 2, 16, N), F32),
        scratch_shapes=[
            pltpu.VMEM((2, N // LANES, TV_ROWS * PLANES, LANES), F32),
            pltpu.VMEM((2, PLANES, N), F32),
        ],
        compiler_params=params(),
        cost_estimate=cost_of(9),
        name="tv_shrink",
    )(edges, moved, moved, above, below)


def along_rows(block, distance):
    place = lambda line: (line % 8) * 32 + line // 8
    route = [
        (place(line - distance), place(line)) for line in range(256) if 0 <= line - distance < 256
    ]
    return lax.ppermute(block, DEPTH + ROW, route)


def phase_of(depth_values, squares):
    return depth_values * (squares * (math.pi / (N * N)))


def per_device(field, hologram, defocus):
    x_lo, y = lax.axis_index("x_lo"), lax.axis_index("y")
    x_hi, z, core = lax.axis_index("x_hi"), lax.axis_index("z"), lax.axis_index("core")
    depth_index = x_lo * 4 + y
    row_index = x_hi * 16 + z * 2 + core
    field = field[:, 0]

    x_freq = RADIX * np.arange(INNER)[None, :] + np.arange(RADIX)[:, None]
    x_squares = jnp.asarray(squares_of(x_freq))[:, None, :]
    x_phase = phase_of(defocus[0], x_squares)
    x_forward = jnp.stack([jnp.cos(x_phase) / N, -jnp.sin(x_phase) / N])

    weights = np.full((CLASSES,), 2.0 / N, np.float32)
    weights[0] = weights[8] = 1.0 / N
    turns = lax.rem(z * np.arange(CLASSES, dtype=np.int32), RADIX).astype(F32)
    turns = turns * (2.0 * math.pi / RADIX)
    cosine, sine = jnp.cos(turns), jnp.sin(turns)
    rotations = jnp.stack([weights * cosine, weights * sine, cosine, sine], axis=1)

    hologram_rows = lax.dynamic_slice_in_dim(hologram, depth_index * 16, 16, 0)
    depth_rows = jnp.full((8, LANES), defocus[0])
    sent = forward_x(field, hologram_rows, depth_rows, x_forward)
    held = jnp.transpose(field.reshape(2, PLANES, 16, N), (1, 0, 2, 3))
    received = lax.all_to_all(sent, LAYER, 0, 0, tiled=True)
    held, received, rotations = lax.optimization_barrier((held, received, rotations))
    held = lax.all_to_all(held, DEPTH, 0, 0, tiled=True)
    depths = received[::4, 272, 0]
    sent = filter_y(rotations, received)
    x_phase = phase_of(depths[None, :, None], x_squares)
    x_backward = jnp.stack([jnp.cos(x_phase), jnp.sin(x_phase)]) * (-1.0 / (PLANES * N))
    received = lax.all_to_all(sent, LAYER, 0, 0, tiled=True)
    moved = backward_x(received, held, x_backward)
    above = along_rows(moved[:, 120:], 1)
    below = along_rows(moved[:, :8], -1)
    line = row_index * 8 + depth_index
    edges = jnp.stack([line > 0, line < 255]).astype(jnp.int32)
    estimate = shrink(edges, moved, above, below)
    estimate = lax.all_to_all(estimate, DEPTH, 0, 0, tiled=True)
    return jnp.transpose(estimate, (1, 0, 2, 3)).reshape(2, 1, 128, N)


def solution(mesh):
    fine = Mesh(mesh.devices.reshape(2, 4, 2, 8, 2), DEPTH + ROW)
    return jax.shard_map(
        per_device,
        mesh=fine,
        in_specs=(P(None, DEPTH, ROW, None), P(ROW, None), P(DEPTH)),
        out_specs=P(None, DEPTH, ROW, None),
        check_vma=False,
    )
```
